128 devices in a mesh: batch: 4 (over x_lo, core), tiles: 32 (over x_hi, z, y).
Axes of the slice: x: 4 (x_hi: 2, x_lo: 2; x = x_hi * 2 + x_lo), y: 4, z: 4, core: 2. Of those that a mesh axis runs over, the one named last changes fastest.
Arguments:
- hidden: bfloat16 [4, 16384, 3072], P('batch', 'tiles'), may hold values from -6 to 6
- frozen_queries: bfloat16 [4, 16384, 1536], P('batch', 'tiles'), may hold values from -108 to 108
- frozen_keys: bfloat16 [4, 16384, 1536], P('batch', 'tiles'), may hold values from -6.09 to 6.09
- frozen_values: bfloat16 [4, 16384, 1536], P('batch', 'tiles'), may hold values from -6 to 6
- reward_output_gradient: bfloat16 [4, 16384, 1536], P('batch', 'tiles'), may hold values from -6 to 6
- truncation_step: int32 [4], P('batch'), may hold values from 0 to 49
- modulation: float32 [50, 2, 3072], replicated, may hold values from -3 to 3
- adapter_down_weight: bfloat16 [3, 3072, 32], replicated, may hold values from -0.109375 to 0.109375
- adapter_up_weight: bfloat16 [3, 32, 1536], replicated, may hold values from -1 to 1
- window: int32 [128, 27], P('tiles'), may hold values from 0 to 1, as said below
Outputs:
- attended: bfloat16 [4, 16384, 1536], P('batch', 'tiles')
- grad_down: float32 [3, 3072, 32], replicated
- grad_up: float32 [3, 32, 1536], replicated
The draws below stay inside these ranges and needn't reach their ends.
Inputs may be any that keep to these rules, and one draw needn't show every extreme that they name: `window`: entry 13, the tile itself, is 1 for every tile.
All inputs are finite; a program needn't handle non-finite values.
Results may differ from the reference program's by a relative error of at most 0.012.
The reference program's roundings to bfloat16 on the way count: a program that leaves them out, or rounds other values in their place, can miss the bound.
Values may be sent and summed in bfloat16 or wider, within the bound.
No kernel may reach another device: no remote copies, remote signals or barrier semaphores. Data moves between devices by JAX's collectives and lax.ppermute only.
A program may use at most 192 MiB of HBM per device.

```python
import math
import jax
import jax.numpy as jnp
from jax import lax

MODEL_WIDTH = 3072
HEADS = 12
HEAD = 128
ADAPTER_RANK = 32
TILE = 128
GF = 2
GR = 2
STEPS = 50
HEAD_FEATURES = 1536
SLAB = 512
TOKENS = 16384
TILES_ALL = 128
BATCH = 4
N_TILES = 32


def base_keys(key):
    return jnp.clip(jax.random.normal(jax.random.fold_in(key, 23), (BATCH, TOKENS, HEAD_FEATURES), jnp.float32), -6.0, 6.0)


def draw_hidden(key, part):
    values = jnp.clip(jax.random.normal(jax.random.fold_in(key, 11), (BATCH, TOKENS, MODEL_WIDTH), jnp.float32), -6.0, 6.0)
    return values.astype(jnp.bfloat16)


def draw_frozen_keys(key, part):
    values = base_keys(key)
    return values.astype(jnp.bfloat16)


def draw_frozen_queries(key, part):
    values = jnp.clip(jax.random.normal(jax.random.fold_in(key, 37), (BATCH, TOKENS, HEAD_FEATURES), jnp.float32), -6.0, 6.0)
    return values.astype(jnp.bfloat16)


def draw_window(key, part):
    slab_total = TILES_ALL // (GF * GR)
    levels = jax.random.randint(jax.random.fold_in(key, 5), (slab_total,), 2, 11)
    tile_level = jnp.repeat(levels, GF * GR)
    picks = jax.random.randint(jax.random.fold_in(key, 6), (TILES_ALL, 27), 0, 10)
    chosen = (picks < tile_level[:, None]).astype(jnp.int32)
    centre = (jnp.arange(27) == 13)[None, :]
    return jnp.where(centre, 1, chosen).astype(jnp.int32)


def with_ends(drawn, rng, least, high):
    longest = drawn.shape.index(max(drawn.shape))
    spots = []
    for shift in (0, 1):
        where = [jax.random.randint(jax.random.fold_in(rng, axis), (), 0, length) for axis, length in enumerate(drawn.shape)]
        where[longest] = (where[longest] + shift) % drawn.shape[longest]
        spots.append(tuple(where))
    return drawn.at[spots[0]].set(least).at[spots[1]].set(high)


def block_levels(stream_key, dims, split, least, top_value):
    loudness, own = 1.0, jax.random.fold_in(stream_key, 6)
    for dim, blocks in split:
        draws = jnp.exp(jax.random.uniform(jax.random.fold_in(own, dim), (blocks,), jnp.float32, least / len(split), top_value / len(split)))
        loudness = loudness * jnp.repeat(draws, dims[dim] // blocks).reshape([-1 if axis == dim else 1 for axis in range(len(dims))])
    return loudness


def scatter_about(rng, extent, width, most, cuts=(), held_as=jnp.bfloat16):
    array = jax.random.normal(rng, extent, jnp.float32) * width
    if len(cuts) > 0:
        array = block_levels(rng, extent, cuts, -0.22, 0.18) * array
    return jnp.clip(array, min=-most, max=most).astype(held_as)


def setup_inputs(seed: int = 0) -> dict:
    key_of = jax.random.split(jax.random.key(seed), 11)
    return {
        "hidden": draw_hidden(jax.random.fold_in(key_of[10], 71), 0),
        "frozen_queries": draw_frozen_queries(jax.random.fold_in(key_of[10], 71), 0),
        "frozen_keys": draw_frozen_keys(jax.random.fold_in(key_of[10], 71), 0),
        "frozen_values": scatter_about(key_of[3], (BATCH, TOKENS, HEAD_FEATURES), 1.0, 6.0, ((0, 4), (1, 32))),
        "reward_output_gradient": scatter_about(key_of[4], (BATCH, TOKENS, HEAD_FEATURES), 1.0, 6.0, ((0, 4), (1, 32))),
        "truncation_step": with_ends(jax.random.randint(key_of[5], (BATCH,), 0, STEPS), jax.random.fold_in(key_of[5], 1), 0, STEPS - 1).astype(jnp.int32),
        "modulation": scatter_about(key_of[6], (STEPS, 2, MODEL_WIDTH), 0.5, 3.0, (), jnp.float32),
        "adapter_down_weight": scatter_about(key_of[7], (3, MODEL_WIDTH, ADAPTER_RANK), MODEL_WIDTH ** -0.5, 0.109375),
        "adapter_up_weight": scatter_about(key_of[8], (3, ADAPTER_RANK, HEAD_FEATURES), ADAPTER_RANK ** -0.5, 1.0),
        "window": draw_window(jax.random.fold_in(key_of[10], 71), 0),
    }


precise_variant = lax.Precision.HIGHEST

def allowed_keys(window_rows, slab_index, slab_count):
    per_slab = GF * GR
    query_tile = jnp.arange(per_slab, dtype=jnp.int32)
    key_tile = jnp.arange(3 * per_slab, dtype=jnp.int32)
    key_side = key_tile // per_slab
    key_local = key_tile % per_slab
    frame_step = key_local[None, :] // GR - query_tile[:, None] // GR
    row_step = key_local[None, :] % GR - query_tile[:, None] % GR
    offset_code = (key_side[None, :] * 3 + frame_step + 1) * 3 + row_step + 1
    nearby = (jnp.abs(frame_step) <= 1) & (jnp.abs(row_step) <= 1)
    neighbour = slab_index + key_side - 1
    inside = (neighbour >= 0) & (neighbour < slab_count)
    offsets = jnp.arange(27, dtype=jnp.int32)
    listed = lax.optimization_barrier(jnp.sum(jnp.where(offset_code[:, :, None] == offsets[None, None, :], window_rows[:, None, :], 0), axis=2))
    tile_mask = nearby & inside[None, :] & (listed > 0)
    return jnp.repeat(jnp.repeat(tile_mask, TILE, axis=0), TILE, axis=1)

def modulate(hidden_rows, shift_scale):
    x_full = hidden_rows.astype(jnp.float32)
    row_mean = lax.optimization_barrier(jnp.mean(x_full, axis=1, keepdims=True))
    centred = x_full - row_mean
    variance = lax.optimization_barrier(jnp.mean(centred * centred, axis=1, keepdims=True))
    normed = centred * lax.rsqrt(variance + 1e-06)
    return normed * (1.0 + shift_scale[1][None, :]) + shift_scale[0][None, :]

def attend(queries, key_rows, value_rows, out_grad, allowed):
    scale_root = 1.0 / math.sqrt(HEAD)
    query_heads = queries.reshape(queries.shape[0], HEADS, HEAD).astype(jnp.float32)
    key_heads = key_rows.reshape(key_rows.shape[0], HEADS, HEAD).astype(jnp.float32)
    value_heads = value_rows.reshape(value_rows.shape[0], HEADS, HEAD).astype(jnp.float32)
    grad_heads = out_grad.reshape(out_grad.shape[0], HEADS, HEAD).astype(jnp.float32)
    scores = jnp.einsum('qhe,khe->hqk', query_heads, key_heads, precision=precise_variant) * scale_root
    scores = jnp.where(allowed[None], scores, -1e+30)
    row_max = lax.optimization_barrier(jnp.max(scores, axis=2, keepdims=True))
    weights = jnp.where(allowed[None], jnp.exp(scores - row_max), 0.0)
    totals = lax.optimization_barrier(jnp.sum(weights, axis=2, keepdims=True))
    probs = weights / totals
    probs_low = probs.astype(jnp.bfloat16).astype(jnp.float32)
    attended = jnp.einsum('hqk,khe->qhe', probs_low, value_heads, precision=precise_variant)
    prob_grad = jnp.einsum('qhe,khe->hqk', grad_heads, value_heads, precision=precise_variant)
    centre = lax.optimization_barrier(jnp.sum(probs * prob_grad, axis=2, keepdims=True))
    score_grad = (probs * (prob_grad - centre) * scale_root).astype(jnp.bfloat16).astype(jnp.float32)
    query_grad = jnp.einsum('hqk,khe->qhe', score_grad, key_heads, precision=precise_variant)
    key_grad = jnp.einsum('hqk,qhe->khe', score_grad, query_heads, precision=precise_variant)
    value_grad = jnp.einsum('hqk,qhe->khe', probs_low, grad_heads, precision=precise_variant)
    slab_rows = queries.shape[0]
    return (attended.reshape(slab_rows, HEAD_FEATURES), query_grad.reshape(slab_rows, HEAD_FEATURES), key_grad.reshape(3 * slab_rows, HEAD_FEATURES), value_grad.reshape(3 * slab_rows, HEAD_FEATURES))

def reference(hidden, frozen_queries, frozen_keys, frozen_values, reward_output_gradient, truncation_step, modulation, adapter_down_weight, adapter_up_weight, window):
    per_slab = GF * GR
    expanded_up_weight = adapter_up_weight.astype(jnp.float32)
    down_total = jnp.zeros((3, MODEL_WIDTH, ADAPTER_RANK), jnp.float32)
    up_total = jnp.zeros((3, ADAPTER_RANK, HEAD_FEATURES), jnp.float32)
    outputs = []
    for sample in range(BATCH):
        input_modulated = modulate(hidden[sample], modulation[truncation_step[sample]])
        input_reduced = lax.optimization_barrier(input_modulated.astype(jnp.bfloat16)).astype(jnp.float32)
        reduced_rank_input = jnp.einsum('mx,pxo->pmo', input_reduced, adapter_down_weight.astype(jnp.float32), precision=precise_variant).astype(jnp.bfloat16)
        projected_output = jnp.einsum('bfe,beg->bfg', reduced_rank_input.astype(jnp.float32), expanded_up_weight, precision=precise_variant)
        queries = (frozen_queries[sample] + projected_output[0]).astype(jnp.bfloat16)
        key_rows = (frozen_keys[sample] + projected_output[1]).astype(jnp.bfloat16)
        value_rows = (frozen_values[sample] + projected_output[2]).astype(jnp.bfloat16)
        zero_rows = jnp.zeros((SLAB, HEAD_FEATURES), jnp.bfloat16)
        key_padded = jnp.concatenate([zero_rows, key_rows, zero_rows], axis=0)
        value_padded = jnp.concatenate([zero_rows, value_rows, zero_rows], axis=0)
        out_grad = reward_output_gradient[sample]

        def visit(carry, slab_index):
            key_acc, value_acc = carry
            start = slab_index * SLAB
            query_slab = lax.dynamic_slice_in_dim(queries, start, SLAB, 0)
            key_slab = lax.dynamic_slice_in_dim(key_padded, start, 3 * SLAB, 0)
            value_slab = lax.dynamic_slice_in_dim(value_padded, start, 3 * SLAB, 0)
            grad_slab = lax.dynamic_slice_in_dim(out_grad, start, SLAB, 0)
            window_rows = lax.dynamic_slice_in_dim(window, slab_index * per_slab, per_slab, 0)
            allowed = allowed_keys(window_rows, slab_index, N_TILES)
            attended, query_grad, key_grad, value_grad = attend(query_slab, key_slab, value_slab, grad_slab, allowed)
            key_acc = lax.dynamic_update_slice_in_dim(key_acc, lax.dynamic_slice_in_dim(key_acc, start, 3 * SLAB, 0) + key_grad, start, 0)
            value_acc = lax.dynamic_update_slice_in_dim(value_acc, lax.dynamic_slice_in_dim(value_acc, start, 3 * SLAB, 0) + value_grad, start, 0)
            return ((key_acc, value_acc), (attended.astype(jnp.bfloat16), query_grad))
        zero_acc = jnp.zeros((TOKENS + 2 * SLAB, HEAD_FEATURES), jnp.float32)
        (key_acc, value_acc), (attended_all, query_all) = lax.scan(visit, (zero_acc, zero_acc), jnp.arange(N_TILES, dtype=jnp.int32))
        outputs.append(attended_all.reshape(TOKENS, HEAD_FEATURES))
        grads = jnp.stack([query_all.reshape(TOKENS, HEAD_FEATURES), key_acc[SLAB:SLAB + TOKENS], value_acc[SLAB:SLAB + TOKENS]])
        rank_grads = jnp.einsum('jth,jrh->jtr', grads, expanded_up_weight, precision=precise_variant)
        down_total = down_total + jnp.einsum('td,jtr->jdr', input_modulated, rank_grads, precision=precise_variant)
        up_total = up_total + jnp.einsum('jtr,jth->jrh', reduced_rank_input.astype(jnp.float32), grads, precision=precise_variant)
    norm_factor = 1.0 / math.sqrt(BATCH * TOKENS)
    return (jnp.stack(outputs), down_total * norm_factor, up_total * norm_factor)
```

```python
import functools
import math

import jax
import jax.numpy as jnp
from jax import lax
from jax.experimental import pallas as pl
from jax.experimental.pallas import tpu as pltpu
from jax.sharding import PartitionSpec as P

HEAD = 128
TILE = 128
GF = 2
GR = 2
RANK = 32
LOG2E = 1.4426950408889634
CHUNKS = (4, 4, 4)
QBLOCK = 256
F32 = jnp.float32
BF16 = jnp.bfloat16


def tile_bias(window_rows, slab_index, slab_count):
    per_slab = GF * GR
    query_tile = jnp.arange(per_slab, dtype=jnp.int32)
    key_tile = jnp.arange(3 * per_slab, dtype=jnp.int32)
    key_side = key_tile // per_slab
    key_local = key_tile % per_slab
    frame_step = key_local[None, :] // GR - query_tile[:, None] // GR
    row_step = key_local[None, :] % GR - query_tile[:, None] % GR
    offset_code = (key_side[None, :] * 3 + frame_step + 1) * 3 + row_step + 1
    nearby = (jnp.abs(frame_step) <= 1) & (jnp.abs(row_step) <= 1)
    neighbour = slab_index + key_side - 1
    inside = (neighbour >= 0) & (neighbour < slab_count)
    offsets = jnp.arange(27, dtype=jnp.int32)
    listed = jnp.sum(
        jnp.where(offset_code[:, :, None] == offsets[None, None, :], window_rows[:, None, :], 0),
        axis=2,
    )
    tile_mask = nearby & inside[None, :] & (listed > 0)
    return jnp.repeat(jnp.where(tile_mask, 0.0, -1e30).astype(F32), TILE, axis=1)


def dot(a, b):
    return lax.dot_general(a, b, (((1,), (0,)), ((), ())), preferred_element_type=F32)


def dot_t(a, b):
    return lax.dot_general(a, b, (((1,), (1,)), ((), ())), preferred_element_type=F32)


def split_rows(x):
    hi = x.astype(BF16)
    lo = (x - hi.astype(F32)).astype(BF16)
    return hi, lo


def attend_kernel(first, slab, *refs):
    (bias, low_prev, low_own, low_next, low0_t, fq, fk, fv, out_grad, halo_prev, halo_next,
     up_wide, up) = refs[:13]
    refs = refs[13:]
    if not first:
        rq_in, rkv_in, _ = refs[:3]
        refs = refs[3:]
    attended, grad_up, rq, rkv, q_s, k_s, vl_s, kx_s, xb_s, xd_s, cat_s = refs
    head = pl.program_id(0)
    scale = 1.0 / math.sqrt(HEAD)

    @pl.when(head == 0)
    def _():
        for i, low in enumerate((low_prev, low_own, low_next)):
            vl_s[i * slab:(i + 1) * slab, HEAD:] = low[...]
        if first:
            rq[...] = jnp.zeros_like(rq)
            rkv[...] = jnp.zeros_like(rkv)
        else:
            rq[...] = rq_in[...]
            rkv[...] = rkv_in[...]

    kv_up = jnp.concatenate([up_wide[1], up_wide[2]], axis=1)
    q_s[...] = (fq[0].astype(F32) + dot(low_own[...], up_wide[0])).astype(BF16)
    sides = ((halo_prev[0], halo_prev[1], low_prev), (fk[0], fv[0], low_own),
             (halo_next[0], halo_next[1], low_next))
    lane = lax.broadcasted_iota(jnp.int32, (slab, HEAD), 1)
    up0 = up[0]
    up0_twice = jnp.concatenate([up0, up0, jnp.zeros((2 * RANK, HEAD), BF16)], axis=0)
    for i, (k_in, v_in, low) in enumerate(sides):
        rows = slice(i * slab, (i + 1) * slab)
        added = dot(low[...], kv_up)
        keys = (k_in.astype(F32) + added[:, :HEAD]).astype(BF16)
        k_s[rows, :] = keys
        vl_s[rows, :HEAD] = (v_in.astype(F32) + added[:, HEAD:]).astype(BF16)
        ku = dot_t(keys, up0_twice)
        rest = ku - ku.astype(BF16).astype(F32)
        kx_s[rows, :] = jnp.where(
            lane < RANK, ku, jnp.where(lane < 2 * RANK, rest, low[...].astype(F32))
        ).astype(BF16)
    hi, lo = split_rows(dot_t(up[1], q_s[...]))
    xb_s[...] = jnp.concatenate([hi, lo, low0_t[...]], axis=0)
    hi, lo = split_rows(dot_t(up[2], out_grad[0]))
    xd_s[...] = jnp.concatenate([hi, lo], axis=0)

    b_total = None
    d_total = None
    for start in range(0, slab, QBLOCK):
        rows = slice(start, start + QBLOCK)
        tiles = range(start // TILE, (start + QBLOCK) // TILE)
        tile_rows = jnp.concatenate(
            [jnp.broadcast_to(bias[t:t + 1, :], (TILE, 3 * slab)) for t in tiles], axis=0
        )
        scores = dot_t(q_s[rows, :], k_s[...]) * (scale * LOG2E) + tile_rows
        row_max = jnp.max(scores, axis=1, keepdims=True)
        weights = jnp.exp2(scores - row_max)
        totals = jnp.sum(weights, axis=1, keepdims=True)
        probs = weights * (1.0 / totals)
        probs_low = probs.astype(BF16)
        prob_grad = dot_t(out_grad[0, rows, :], vl_s[:, :HEAD])
        centre = jnp.sum(probs * prob_grad, axis=1, keepdims=True)
        score_grad = (probs * (prob_grad - centre) * scale).astype(BF16)
        out = dot(probs_low, vl_s[...])
        attended[0, rows, :] = out[:, :HEAD].astype(BF16)
        cat_s[rows, :HEAD] = out[:, HEAD:]
        cat_s[rows, HEAD:] = dot(score_grad, kx_s[...])
        d_part = dot(xd_s[:, rows], probs_low)
        b_part = dot(xb_s[:, rows], score_grad)
        d_total = d_part if d_total is None else d_total + d_part
        b_total = b_part if b_total is None else b_total + b_part

    cat_t = cat_s[...].T
    c_t = cat_t[:RANK]
    a_t = cat_t[HEAD:]
    rq[...] += a_t[:RANK] + a_t[RANK:2 * RANK]
    rkv[:RANK] += b_total[:RANK] + b_total[RANK:2 * RANK]
    rkv[RANK:] += d_total[:RANK] + d_total[RANK:]

    def pair(left, right):
        hi, lo = split_rows(left)
        both = dot(jnp.concatenate([hi, lo], axis=0), right)
        return both[:RANK] + both[RANK:]

    grad_up[0] = pair(b_total[2 * RANK:], k_s[...])
    grad_up[1] = pair(a_t[2 * RANK:3 * RANK], q_s[...])
    grad_up[2] = pair(c_t, out_grad[0])


def attend_chunk(h0, heads, shared, own, halos, ups, carried):
    slab = own[0].shape[1]
    across = own[0].shape[2]
    first = carried is None

    def whole(x):
        return pl.BlockSpec(x.shape, lambda h: (0,) * x.ndim)

    own_spec = pl.BlockSpec((1, slab, HEAD), lambda h: (0, 0, h0 + h))
    halo_spec = pl.BlockSpec((2, slab, HEAD), lambda h: (0, 0, h))
    in_specs = [whole(x) for x in shared] + [own_spec] * 4 + [halo_spec] * 2 + [
        pl.BlockSpec((3, x.shape[1], HEAD), lambda h: (0, 0, h0 + h)) for x in ups
    ]
    operands = [*shared, *own, *halos, *ups]
    aliases = {}
    if not first:
        attended, rq, rkv = carried
        aliases = {len(operands) + 2: 0}
        operands += [rq, rkv, attended]
        in_specs += [whole(rq), whole(rkv), pl.BlockSpec(memory_space=pl.ANY)]
    rq_shape = jax.ShapeDtypeStruct((RANK, slab), F32)
    rkv_shape = jax.ShapeDtypeStruct((2 * RANK, 3 * slab), F32)
    attended, grad_up, rq, rkv = pl.pallas_call(
        functools.partial(attend_kernel, first, slab),
        grid=(heads,),
        in_specs=in_specs,
        out_specs=[
            own_spec,
            pl.BlockSpec((3, RANK, HEAD), lambda h: (0, 0, h)),
            whole(rq_shape),
            whole(rkv_shape),
        ],
        out_shape=[
            jax.ShapeDtypeStruct((1, slab, across), BF16),
            jax.ShapeDtypeStruct((3, RANK, heads * HEAD), F32),
            rq_shape,
            rkv_shape,
        ],
        scratch_shapes=[
            pltpu.VMEM((slab, HEAD), BF16),
            pltpu.VMEM((3 * slab, HEAD), BF16),
            pltpu.VMEM((3 * slab, 2 * HEAD), BF16),
            pltpu.VMEM((3 * slab, HEAD), BF16),
            pltpu.VMEM((3 * RANK, slab), BF16),
            pltpu.VMEM((2 * RANK, slab), BF16),
            pltpu.VMEM((slab, 2 * HEAD), F32),
        ],
        input_output_aliases=aliases,
        compiler_params=pltpu.CompilerParams(
            dimension_semantics=("arbitrary",), vmem_limit_bytes=48 << 20
        ),
        name=f"attend_{h0}",
    )(*operands)
    return attended, grad_up, rq, rkv


def neighbours(value, axis):
    count = lax.axis_size(axis)
    up = [(i, i + 1) for i in range(count - 1)]
    down = [(j, i) for i, j in up]
    return lax.ppermute(value, axis, up), lax.ppermute(value, axis, down)


def reduce_everywhere(x, batch, tiles):
    count = lax.axis_size(tiles)
    parts = x.reshape(count, x.shape[0] // count, x.shape[1])
    got = lax.all_to_all(parts, tiles, 0, 0, tiled=True)
    mine = jnp.sum(got.astype(F32), axis=0)
    peers = lax.axis_size(batch)
    spread = jnp.broadcast_to(mine.astype(BF16)[None], (peers,) + mine.shape)
    got = lax.all_to_all(spread, batch, 0, 0, tiled=True)
    total = jnp.sum(got.astype(F32), axis=0).astype(BF16)
    spread = jnp.broadcast_to(total[None], (count,) + total.shape)
    return lax.all_to_all(spread, tiles, 0, 0, tiled=True).reshape(x.shape)


def per_device(
    hidden,
    frozen_queries,
    frozen_keys,
    frozen_values,
    reward_output_gradient,
    truncation_step,
    modulation,
    adapter_down_weight,
    adapter_up_weight,
    window,
):
    slab = hidden.shape[1]
    width = hidden.shape[2]
    across = frozen_queries.shape[2]
    bounds = []
    h0 = 0
    for heads in CHUNKS:
        bounds.append((h0, heads))
        h0 += heads

    def frozen_part(h0, heads):
        columns = slice(h0 * HEAD, (h0 + heads) * HEAD)
        return jnp.concatenate([frozen_keys[:, :, columns], frozen_values[:, :, columns]], axis=0)

    halos = [neighbours(frozen_part(*bounds[0]), "tiles")]

    x_full = hidden[0].astype(F32)
    row_mean = jnp.mean(x_full, axis=1, keepdims=True)
    centred = x_full - row_mean
    variance = jnp.mean(centred * centred, axis=1, keepdims=True)
    normed = centred * lax.rsqrt(variance + 1e-06)
    shift_scale = lax.dynamic_index_in_dim(modulation, truncation_step[0], 0, keepdims=False)
    x_mod = (normed * (1.0 + shift_scale[1][None, :]) + shift_scale[0][None, :]).astype(BF16)
    down = adapter_down_weight
    down_wide = jnp.concatenate([down[2], down[0], down[1], jnp.zeros_like(down[0])], axis=1)
    low = jnp.dot(x_mod, down_wide, preferred_element_type=F32).astype(BF16)
    low_prev, low_next = neighbours(low, "tiles")
    rest = [frozen_part(*b) for b in bounds[1:]]
    *rest, low = lax.optimization_barrier((*rest, low))
    halos += [neighbours(part, "tiles") for part in rest]

    up = adapter_up_weight
    pad = lambda x, before: jnp.pad(x, ((before, 3 * RANK - before), (0, 0)))
    up_wide = jnp.stack([pad(up[0], RANK), pad(up[1], 2 * RANK), pad(up[2], 0)])
    low0_t = low[:, RANK:2 * RANK].T
    bias = tile_bias(window, lax.axis_index("tiles"), lax.axis_size("tiles"))
    shared = (bias, low_prev, low, low_next, low0_t)
    own = (frozen_queries, frozen_keys, frozen_values, reward_output_gradient)
    carried = None
    grad_up_parts = []
    for (h0, heads), halo in zip(bounds, halos):
        attended, grad_up, rq, rkv = attend_chunk(
            h0, heads, shared, own, halo, (up_wide, up), carried
        )
        carried = (attended, rq, rkv)
        grad_up_parts.append(grad_up)

    norm_factor = 1.0 / math.sqrt(
        hidden.shape[0] * lax.axis_size("batch") * slab * lax.axis_size("tiles")
    )
    count = lax.axis_size("tiles")
    from_prev = lax.ppermute(rkv[:, 2 * slab:], "tiles", [(i, i + 1) for i in range(count - 1)])
    from_next = lax.ppermute(rkv[:, :slab], "tiles", [(i + 1, i) for i in range(count - 1)])
    rank_grads = jnp.concatenate([rq, rkv[:, slab:2 * slab] + from_prev + from_next], axis=0)
    hi, lo = split_rows(rank_grads)
    both = jnp.dot(jnp.concatenate([hi, lo], axis=0), x_mod, preferred_element_type=F32)
    grad_down = (both[:3 * RANK] + both[3 * RANK:]) * norm_factor
    grad_up = jnp.concatenate(grad_up_parts, axis=2) * norm_factor
    flat = jnp.concatenate(
        [grad_down.astype(BF16).reshape(-1, 128), grad_up.astype(BF16).reshape(-1, 128)], axis=0
    )
    summed = reduce_everywhere(flat, "batch", "tiles").astype(F32)
    split = 3 * RANK * width // 128
    grad_down = summed[:split].reshape(3, RANK, width).transpose(0, 2, 1)
    grad_up = summed[split:].reshape(3, RANK, across)
    return (attended, grad_down, grad_up)


def solution(mesh):
    placed = (
        P("batch", "tiles", None),
        P("batch", "tiles", None),
        P("batch", "tiles", None),
        P("batch", "tiles", None),
        P("batch", "tiles", None),
        P("batch"),
        P(),
        P(),
        P(),
        P("tiles", None),
    )
    return jax.shard_map(
        per_device,
        mesh=mesh,
        in_specs=placed,
        out_specs=(P("batch", "tiles", None), P(), P()),
        check_vma=False,
    )
```

```python
import functools
import math

import jax
import jax.numpy as jnp
from jax import lax
from jax.experimental import pallas as pl
from jax.experimental.pallas import tpu as pltpu
from jax.sharding import PartitionSpec as P

HEAD = 128
TILE = 128
GF = 2
GR = 2
RANK = 32
LOG2E = 1.4426950408889634
EARLY = 2
CHUNKS = (6, 4, 2)
QBLOCK = 512
PADDING = 8
PER_STEP = 2
F32 = jnp.float32
BF16 = jnp.bfloat16


def tile_bias(window_rows, slab_index, slab_count):
    per_slab = GF * GR
    query_tile = jnp.arange(per_slab, dtype=jnp.int32)
    key_tile = jnp.arange(3 * per_slab, dtype=jnp.int32)
    key_side = key_tile // per_slab
    key_local = key_tile % per_slab
    frame_step = key_local[None, :] // GR - query_tile[:, None] // GR
    row_step = key_local[None, :] % GR - query_tile[:, None] % GR
    offset_code = (key_side[None, :] * 3 + frame_step + 1) * 3 + row_step + 1
    nearby = (jnp.abs(frame_step) <= 1) & (jnp.abs(row_step) <= 1)
    neighbour = slab_index + key_side - 1
    inside = (neighbour >= 0) & (neighbour < slab_count)
    offsets = jnp.arange(27, dtype=jnp.int32)
    listed = jnp.sum(
        jnp.where(offset_code[:, :, None] == offsets[None, None, :], window_rows[:, None, :], 0),
        axis=2,
    )
    tile_mask = nearby & inside[None, :] & (listed > 0)
    return jnp.repeat(jnp.where(tile_mask, 0.0, -1e30).astype(F32), TILE, axis=1)


def dot(a, b):
    return lax.dot_general(a, b, (((1,), (0,)), ((), ())), preferred_element_type=F32)


def dot_t(a, b):
    return lax.dot_general(a, b, (((1,), (1,)), ((), ())), preferred_element_type=F32)


def split_rows(x):
    hi = x.astype(BF16)
    lo = (x - hi.astype(F32)).astype(BF16)
    return hi, lo


def attend_kernel(first, last, slab, *refs):
    (bias, low_own, low0_t, low_prev, low_next, fq, fk, fv, out_grad, up_wide, up) = refs[:11]
    halos = refs[11:15]
    refs = refs[15:]
    if first:
        early, refs = refs[:4], refs[4:]
    if not first:
        rq_in, rkv_in, _ = refs[:3]
        refs = refs[3:]
    attended, grad_up, rq, rkv = refs[:4]
    refs = refs[4:]
    if last:
        to_prev, to_next = refs[:2]
        refs = refs[2:]
    q_s, k_s, vl_s, kx_s, xb_s, xd_s, cat_s = refs
    scale = 1.0 / math.sqrt(HEAD)

    @pl.when(pl.program_id(0) == 0)
    def _():
        half = TILE // 2
        for n in range(PER_STEP):
            vl_s[n, slab:2 * slab, HEAD:] = low_own[...]
            for i, low in ((0, low_prev), (2, low_next)):
                for g in range(slab // half):
                    rows = slice(i * slab + g * half, i * slab + (g + 1) * half)
                    cols = slice(g // 2 * HEAD, (g // 2 + 1) * HEAD)
                    vl_s[n, rows, HEAD:] = low[g % 2, :, cols]
        if first:
            rq[...] = jnp.zeros_like(rq)
            rkv[...] = jnp.zeros_like(rkv)
        else:
            rq[...] = rq_in[...]
            rkv[...] = rkv_in[...]

    lane = lax.broadcasted_iota(jnp.int32, (slab, HEAD), 1)

    def pair(left, right):
        hi, lo = split_rows(left)
        both = dot(jnp.concatenate([hi, lo], axis=0), right)
        return both[:RANK] + both[RANK:]

    def prepare(n):
        cols = slice(n * HEAD, (n + 1) * HEAD)
        kv_up = jnp.concatenate([up_wide[1, :, cols], up_wide[2, :, cols]], axis=1)
        q_s[n] = (fq[0, :, cols].astype(F32) + dot(low_own[...], up_wide[0, :, cols])).astype(BF16)
        arrived = [halo[0, :, cols] for halo in halos]
        if first:
            begin = pl.program_id(0) == 0
            arrived = [jnp.where(begin, e[0, :, cols], a) for e, a in zip(early, arrived)]
        sides = (arrived[:2], (fk[0, :, cols], fv[0, :, cols]), arrived[2:])
        up0 = up[0, :, cols]
        up0_twice = jnp.concatenate([up0, up0, jnp.zeros((2 * RANK, HEAD), BF16)], axis=0)
        for i, (k_in, v_in) in enumerate(sides):
            rows = slice(i * slab, (i + 1) * slab)
            low = vl_s[n, rows, HEAD:]
            added = dot(low, kv_up)
            keys = (k_in.astype(F32) + added[:, :HEAD]).astype(BF16)
            k_s[n, rows, :] = keys
            vl_s[n, rows, :HEAD] = (v_in.astype(F32) + added[:, HEAD:]).astype(BF16)
            ku = dot_t(keys, up0_twice)
            rest = ku - ku.astype(BF16).astype(F32)
            kx_s[n, rows, :] = jnp.where(
                lane < RANK, ku, jnp.where(lane < 2 * RANK, rest, low.astype(F32))
            ).astype(BF16)
        hi, lo = split_rows(dot_t(up[1, :, cols], q_s[n]))
        xb_s[n] = jnp.concatenate([hi, lo, low0_t[...]], axis=0)
        hi, lo = split_rows(dot_t(up[2, :, cols], out_grad[0, :, cols]))
        xd_s[n] = jnp.concatenate([hi, lo], axis=0)

    def products(n, rows):
        cols = slice(n * HEAD, (n + 1) * HEAD)
        scores = dot_t(q_s[n, rows, :], k_s[n])
        prob_grad = dot_t(out_grad[0, rows, cols], vl_s[n, :, :HEAD])
        return scores, prob_grad

    def soften(rows, scores, prob_grad):
        tiles = range(rows.start // TILE, rows.stop // TILE)
        tile_rows = jnp.concatenate(
            [jnp.broadcast_to(bias[t:t + 1, :], (TILE, 3 * slab)) for t in tiles], axis=0
        )
        scores = scores * (scale * LOG2E) + tile_rows
        row_max = jnp.max(scores, axis=1, keepdims=True)
        weights = jnp.exp2(scores - row_max)
        totals = jnp.sum(weights, axis=1, keepdims=True)
        probs = weights * (1.0 / totals)
        centre = jnp.sum(probs * prob_grad, axis=1, keepdims=True)
        score_grad = (probs * (prob_grad - centre) * scale).astype(BF16)
        return probs.astype(BF16), score_grad

    def spread(n, rows, probs_low, score_grad):
        out = dot(probs_low, vl_s[n])
        attended[0, rows, n * HEAD:(n + 1) * HEAD] = out[:, :HEAD].astype(BF16)
        cat_s[n, rows, :HEAD] = out[:, HEAD:]
        cat_s[n, rows, HEAD:] = dot(score_grad, kx_s[n])
        return dot(xd_s[n, :, rows], probs_low), dot(xb_s[n, :, rows], score_grad)

    def finish(n, d_total, b_total):
        cols = slice(n * HEAD, (n + 1) * HEAD)
        cat_t = cat_s[n].T
        c_t = cat_t[:RANK]
        a_t = cat_t[HEAD:]
        grad_up[0, :, cols] = pair(b_total[2 * RANK:], k_s[n])
        grad_up[1, :, cols] = pair(a_t[2 * RANK:3 * RANK], q_s[n])
        grad_up[2, :, cols] = pair(c_t, out_grad[0, :, cols])
        return (a_t[:RANK] + a_t[RANK:2 * RANK], b_total[:RANK] + b_total[RANK:2 * RANK],
                d_total[:RANK] + d_total[RANK:])

    steps = [(n, slice(r, r + QBLOCK)) for n in range(PER_STEP) for r in range(0, slab, QBLOCK)]
    totals = [[None, None] for _ in range(PER_STEP)]
    for n in range(PER_STEP):
        prepare(n)
    made = {}
    soft = {}
    for i in range(len(steps) + 2):
        if i < len(steps):
            made[i] = products(*steps[i])
        if 0 <= i - 1 < len(steps):
            soft[i - 1] = soften(steps[i - 1][1], *made.pop(i - 1))
        if 0 <= i - 2 < len(steps):
            n, rows = steps[i - 2]
            parts = spread(n, rows, *soft.pop(i - 2))
            totals[n] = [p if t is None else t + p for t, p in zip(totals[n], parts)]
    shares = [finish(n, *totals[n]) for n in range(PER_STEP)]
    rq[...] += sum(s[0] for s in shares)
    rkv[:RANK] += sum(s[1] for s in shares)
    rkv[RANK:] += sum(s[2] for s in shares)

    if last:
        @pl.when(pl.program_id(0) == pl.num_programs(0) - 1)
        def _():
            to_prev[...] = rkv[:, :slab].astype(BF16)
            to_next[...] = rkv[:, 2 * slab:].astype(BF16)


def whole(x):
    return pl.BlockSpec(x.shape, lambda *_: (0,) * len(x.shape))


def attend_chunk(h0, heads, last, shared, own, ups, halo, early, carried):
    slab = own[0].shape[1]
    across = own[0].shape[2]
    first = carried is None
    steps = heads // PER_STEP
    wide = PER_STEP * HEAD
    skipped = early[0].shape[2] // wide if first else 0

    own_spec = pl.BlockSpec((1, slab, wide), lambda h: (0, 0, h0 // PER_STEP + h))

    def halo_specs(skipped):
        return [
            pl.BlockSpec((1, slab, wide), lambda h, kind=kind: (kind, 0, jnp.maximum(h - skipped, 0)))
            for kind in (0, 1, 0, 1)
        ]

    low_rows = TILE // 2
    low_spec = pl.BlockSpec((2, low_rows, shared[-1].shape[2]), lambda h: (0, slab // low_rows, 0))
    in_specs = [whole(x) for x in shared[:-2]] + [low_spec] * 2 + [own_spec] * 4 + [
        pl.BlockSpec((3, x.shape[1], wide), lambda h: (0, 0, h0 // PER_STEP + h)) for x in ups
    ] + halo_specs(skipped)
    operands = [*shared, *own, *ups, halo[0], halo[0], halo[1], halo[1]]
    if first:
        in_specs += [
            pl.BlockSpec((1, slab, wide), lambda h, kind=kind: (kind, 0, 0)) for kind in (0, 1, 0, 1)
        ]
        operands += [early[0], early[0], early[1], early[1]]
    aliases = {}
    if not first:
        attended, rq, rkv = carried
        aliases = {len(operands) + 2: 0}
        operands += [rq, rkv, attended]
        in_specs += [whole(rq), whole(rkv), pl.BlockSpec(memory_space=pl.ANY)]
    rq_shape = jax.ShapeDtypeStruct((RANK, slab), F32)
    rkv_shape = jax.ShapeDtypeStruct((2 * RANK, 3 * slab), F32)
    sent_shape = jax.ShapeDtypeStruct((2 * RANK, slab), BF16)
    return pl.pallas_call(
        functools.partial(attend_kernel, first, last, slab),
        grid=(steps,),
        in_specs=in_specs,
        out_specs=[
            own_spec,
            pl.BlockSpec((3, RANK, wide), lambda h: (0, 0, h)),
            whole(rq_shape),
            whole(rkv_shape),
        ] + [whole(sent_shape)] * (2 * last),
        out_shape=[
            jax.ShapeDtypeStruct((1, slab, across), BF16),
            jax.ShapeDtypeStruct((3, RANK, heads * HEAD), F32),
            rq_shape,
            rkv_shape,
        ] + [sent_shape] * (2 * last),
        scratch_shapes=[
            pltpu.VMEM((PER_STEP, slab, HEAD), BF16),
            pltpu.VMEM((PER_STEP, 3 * slab, HEAD), BF16),
            pltpu.VMEM((PER_STEP, 3 * slab, 2 * HEAD), BF16),
            pltpu.VMEM((PER_STEP, 3 * slab, HEAD), BF16),
            pltpu.VMEM((PER_STEP, 3 * RANK, slab), BF16),
            pltpu.VMEM((PER_STEP, 2 * RANK, slab), BF16),
            pltpu.VMEM((PER_STEP, slab, 2 * HEAD), F32),
        ],
        input_output_aliases=aliases,
        compiler_params=pltpu.CompilerParams(
            dimension_semantics=("arbitrary",), vmem_limit_bytes=48 << 20
        ),
        name=f"attend_{h0}",
    )(*operands)


def prologue_kernel(step, x, shift_scale, down, x_mod, low, low_sent, low0_t, down_s):
    del step
    width = x.shape[2]

    @pl.when(pl.program_id(0) == 0)
    def _():
        down_s[...] = jnp.concatenate(
            [down[2], down[0], down[1], jnp.zeros((RANK, width), BF16)], axis=0
        )

    x_full = x[0].astype(F32)
    centred = x_full - jnp.sum(x_full, axis=1, keepdims=True) * (1.0 / width)
    variance = jnp.sum(centred * centred, axis=1, keepdims=True) * (1.0 / width)
    normed = centred * lax.rsqrt(variance + 1e-06)
    modulated = (normed * (1.0 + shift_scale[0, 1:2, :]) + shift_scale[0, 0:1, :]).astype(BF16)
    x_mod[...] = modulated
    reduced = dot_t(modulated, down_s[...])
    low[...] = reduced.astype(BF16)
    low_sent[...] = reduced.reshape(2, TILE // 2, 4 * RANK).astype(BF16)
    low0_t[...] = reduced.T[RANK:2 * RANK].astype(BF16)


def prologue(hidden, truncation_step, modulation, down):
    _, slab, width = hidden.shape
    hidden, modulation, down = [
        pltpu.with_memory_space_constraint(x, pltpu.HBM) for x in (hidden, modulation, down)
    ]
    return pl.pallas_call(
        prologue_kernel,
        grid_spec=pltpu.PrefetchScalarGridSpec(
            num_scalar_prefetch=1,
            grid=(slab // TILE,),
            in_specs=[
                pl.BlockSpec((1, TILE, width), lambda i, step: (0, i, 0)),
                pl.BlockSpec((1, 2, width), lambda i, step: (step[0], 0, 0)),
                whole(down),
            ],
            out_specs=[
                pl.BlockSpec((TILE, width), lambda i, step: (i, 0)),
                pl.BlockSpec((TILE, 4 * RANK), lambda i, step: (i, 0)),
                pl.BlockSpec((2, TILE // 2, 4 * RANK), lambda i, step: (0, 0, i)),
                pl.BlockSpec((RANK, TILE), lambda i, step: (0, i)),
            ],
            scratch_shapes=[pltpu.VMEM((4 * RANK, width), BF16)],
        ),
        out_shape=[
            jax.ShapeDtypeStruct((slab, width), BF16),
            jax.ShapeDtypeStruct((slab, 4 * RANK), BF16),
            jax.ShapeDtypeStruct((2, TILE // 2, slab // TILE * 4 * RANK), BF16),
            jax.ShapeDtypeStruct((RANK, slab), BF16),
        ],
        compiler_params=pltpu.CompilerParams(
            dimension_semantics=("arbitrary",), vmem_limit_bytes=48 << 20
        ),
        name="prologue",
    )(truncation_step, hidden, modulation, down)


def project_kernel(factor, rq, rkv, from_prev, from_next, x_mod, *refs):
    parts, out = refs[:-1], refs[-1]
    rank_kv = rkv[...] + from_prev[...].astype(F32) + from_next[...].astype(F32)
    hi, lo = split_rows(jnp.concatenate([rq[...], rank_kv], axis=0))
    both = dot(jnp.concatenate([hi, lo], axis=0), x_mod[...])
    down = ((both[:3 * RANK] + both[3 * RANK:]) * factor).astype(BF16)
    columns = x_mod.shape[1] // HEAD
    tiles = 3 * RANK // 16
    first = pl.program_id(0) * (columns * tiles)
    for c in range(columns):
        for r in range(tiles):
            out[first + c * tiles + r] = down[16 * r:16 * r + 16, c * HEAD:(c + 1) * HEAD]

    @pl.when(pl.program_id(0) == pl.num_programs(0) - 1)
    def _():
        at = pl.num_programs(0) * (columns * tiles)
        for part in parts:
            for c in range(part.shape[2] // HEAD):
                for r in range(tiles):
                    rows = slice(16 * (r % 2), 16 * (r % 2) + 16)
                    piece = part[r // 2, rows, c * HEAD:(c + 1) * HEAD] * factor
                    out[at + r] = piece.astype(BF16)
                at = at + tiles
        for g in range(PADDING):
            out[at + g] = jnp.zeros((16, HEAD), BF16)


def project(factor, rq, rkv, from_prev, from_next, x_mod, parts):
    slab, width = x_mod.shape
    across = sum(p.shape[2] for p in parts)
    tiles = (width + across) // HEAD * (3 * RANK // 16) + PADDING
    block = width // 4
    shape = jax.ShapeDtypeStruct((tiles, 16, HEAD), BF16)
    return pl.pallas_call(
        functools.partial(project_kernel, factor),
        grid=(width // block,),
        in_specs=[
            whole(rq),
            pl.BlockSpec((2 * RANK, slab), lambda i: (0, 1)),
            whole(from_prev),
            whole(from_next),
            pl.BlockSpec((slab, block), lambda i: (0, i)),
        ] + [whole(p) for p in parts],
        out_specs=whole(shape),
        out_shape=shape,
        compiler_params=pltpu.CompilerParams(
            dimension_semantics=("arbitrary",), vmem_limit_bytes=48 << 20
        ),
        name="project",
    )(rq, rkv, from_prev, from_next, x_mod, *parts)


def unpack_kernel(packed, down, up):
    tiles = 3 * RANK // 16
    g = 0
    for out in (down, up):
        for c in range(out.shape[2] // HEAD):
            for r in range(tiles):
                rows = slice(16 * (r % 2), 16 * (r % 2) + 16)
                out[r // 2, rows, c * HEAD:(c + 1) * HEAD] = packed[g].astype(F32)
                g += 1


def unpack(packed, width, across):
    shapes = [jax.ShapeDtypeStruct((3, RANK, n), F32) for n in (width, across)]
    return pl.pallas_call(unpack_kernel, out_shape=shapes, name="unpack")(packed)


def neighbours(before, after, axis):
    count = lax.axis_size(axis)
    up = [(i, (i + 1) % count) for i in range(count)]
    down = [(j, i) for i, j in up]
    return lax.ppermute(before, axis, up), lax.ppermute(after, axis, down)


def reduce_everywhere(x, batch, tiles):
    count = lax.axis_size(tiles)
    parts = x.reshape(count, x.shape[0] // count * 16, HEAD)
    got = lax.all_to_all(parts, tiles, 0, 0, tiled=True)
    mine = jnp.sum(got.astype(F32), axis=0).astype(BF16)
    peers = lax.axis_size(batch)
    one, two, three = [
        lax.ppermute(mine, batch, [(i, i ^ d) for i in range(peers)]).astype(F32) for d in (1, 2, 3)
    ]
    total = ((mine.astype(F32) + one) + (two + three)).astype(BF16)
    spread = jnp.broadcast_to(total[None], (count,) + total.shape)
    return lax.all_to_all(spread, tiles, 0, 0, tiled=True).reshape(x.shape)


def per_device(
    hidden,
    frozen_queries,
    frozen_keys,
    frozen_values,
    reward_output_gradient,
    truncation_step,
    modulation,
    adapter_down_weight,
    adapter_up_weight,
    window,
):
    slab = hidden.shape[1]
    width = hidden.shape[2]
    across = frozen_queries.shape[2]
    bounds = []
    h0 = 0
    for heads in CHUNKS:
        bounds.append((h0, heads))
        h0 += heads

    def frozen_part(h0, heads):
        columns = slice(h0 * HEAD, (h0 + heads) * HEAD)
        return jnp.concatenate([frozen_keys[:, :, columns], frozen_values[:, :, columns]], axis=0)

    part = frozen_part(0, EARLY)
    early = neighbours(part, part, "tiles")
    x_mod, low, low_sent, low0_t = prologue(
        hidden, truncation_step, modulation, adapter_down_weight.transpose(0, 2, 1)
    )
    bounds[0] = (EARLY, CHUNKS[0] - EARLY)
    parts = [frozen_part(*b) for b in bounds]
    *early, low_sent = lax.optimization_barrier((*early, low_sent))
    parts[0] = jnp.concatenate([parts[0], low_sent], axis=1)
    bounds[0] = (0, CHUNKS[0])
    parts = lax.optimization_barrier(parts)
    halos = [neighbours(part, part, "tiles") for part in parts]

    up = adapter_up_weight
    pad = lambda x, before: jnp.pad(x, ((before, 3 * RANK - before), (0, 0)))
    up_wide = jnp.stack([pad(up[0], RANK), pad(up[1], 2 * RANK), pad(up[2], 0)])
    bias = tile_bias(window, lax.axis_index("tiles"), lax.axis_size("tiles"))
    shared = (bias, low, low0_t, *halos[0])
    own = (frozen_queries, frozen_keys, frozen_values, reward_output_gradient)
    carried = None
    grad_up_parts = []
    for i, ((h0, heads), halo) in enumerate(zip(bounds, halos)):
        attended, grad_up, rq, rkv, *sent = attend_chunk(
            h0, heads, i == len(bounds) - 1, shared, own, (up_wide, up), halo, early, carried
        )
        carried = (attended, rq, rkv)
        grad_up_parts.append(grad_up)

    norm_factor = 1.0 / math.sqrt(
        hidden.shape[0] * lax.axis_size("batch") * slab * lax.axis_size("tiles")
    )
    to_prev, to_next = sent
    from_prev, from_next = neighbours(to_next, to_prev, "tiles")
    packed = project(norm_factor, rq, rkv, from_prev, from_next, x_mod, grad_up_parts)
    packed = reduce_everywhere(packed, "batch", "tiles")
    grad_down, grad_up = unpack(packed, width, across)
    return (attended, grad_down.transpose(0, 2, 1), grad_up)


def solution(mesh):
    placed = (
        P("batch", "tiles", None),
        P("batch", "tiles", None),
        P("batch", "tiles", None),
        P("batch", "tiles", None),
        P("batch", "tiles", None),
        P("batch"),
        P(),
        P(),
        P(),
        P("tiles", None),
    )
    return jax.shard_map(
        per_device,
        mesh=mesh,
        in_specs=placed,
        out_specs=(P("batch", "tiles", None), P(), P()),
        check_vma=False,
    )
```

```python
import functools
import math

import jax
import jax.numpy as jnp
from jax import lax
from jax.experimental import pallas as pl
from jax.experimental.pallas import tpu as pltpu
from jax.sharding import PartitionSpec as P

HEAD = 128
TILE = 128
GF = 2
GR = 2
RANK = 32
LOG2E = 1.4426950408889634
EARLY = 4
ATTEND_FLOPS = 4_600_000_000
CHUNKS = (6, 4, 2)
QBLOCK = 512
PADDING = 8
PER_STEP = 2
F32 = jnp.float32
BF16 = jnp.bfloat16


def tile_bias(window_rows, slab_index, slab_count):
    per_slab = GF * GR
    query_tile = jnp.arange(per_slab, dtype=jnp.int32)
    key_tile = jnp.arange(3 * per_slab, dtype=jnp.int32)
    key_side = key_tile // per_slab
    key_local = key_tile % per_slab
    frame_step = key_local[None, :] // GR - query_tile[:, None] // GR
    row_step = key_local[None, :] % GR - query_tile[:, None] % GR
    offset_code = (key_side[None, :] * 3 + frame_step + 1) * 3 + row_step + 1
    nearby = (jnp.abs(frame_step) <= 1) & (jnp.abs(row_step) <= 1)
    neighbour = slab_index + key_side - 1
    inside = (neighbour >= 0) & (neighbour < slab_count)
    offsets = jnp.arange(27, dtype=jnp.int32)
    listed = jnp.sum(
        jnp.where(offset_code[:, :, None] == offsets[None, None, :], window_rows[:, None, :], 0),
        axis=2,
    )
    tile_mask = nearby & inside[None, :] & (listed > 0)
    return jnp.repeat(jnp.where(tile_mask, 0.0, -1e30).astype(F32), TILE, axis=1)


def dot(a, b):
    return lax.dot_general(a, b, (((1,), (0,)), ((), ())), preferred_element_type=F32)


def dot_t(a, b):
    return lax.dot_general(a, b, (((1,), (1,)), ((), ())), preferred_element_type=F32)


def split_rows(x):
    hi = x.astype(BF16)
    lo = (x - hi.astype(F32)).astype(BF16)
    return hi, lo


def attend_kernel(first, last, slab, *refs):
    (bias, low_own, low0_t, low_prev, low_next, fq, fk, fv, out_grad, up_wide, up) = refs[:11]
    halos = refs[11:15]
    refs = refs[15:]
    if first:
        early, refs = refs[:4], refs[4:]
    if not first:
        rq_in, rkv_in, _ = refs[:3]
        refs = refs[3:]
    attended, grad_up, rq, rkv = refs[:4]
    refs = refs[4:]
    if last:
        to_prev, to_next = refs[:2]
        refs = refs[2:]
    q_s, k_s, vl_s, kx_s, xb_s, xd_s, cat_s = refs
    scale = 1.0 / math.sqrt(HEAD)

    @pl.when(pl.program_id(0) == 0)
    def _():
        for n in range(PER_STEP):
            vl_s[n, slab:2 * slab, HEAD:] = low_own[...]
            for i, low in ((0, low_prev), (2, low_next)):
                for g in range(slab // TILE):
                    rows = slice(i * slab + g * TILE, i * slab + (g + 1) * TILE)
                    cols = slice(g // 2 * HEAD, (g // 2 + 1) * HEAD)
                    vl_s[n, rows, HEAD:] = low[g % 2, :, cols]
        if first:
            rq[...] = jnp.zeros_like(rq)
            rkv[...] = jnp.zeros_like(rkv)
        else:
            rq[...] = rq_in[...]
            rkv[...] = rkv_in[...]

    lane = lax.broadcasted_iota(jnp.int32, (slab, HEAD), 1)

    def pair(left, right):
        hi, lo = split_rows(left)
        both = dot(jnp.concatenate([hi, lo], axis=0), right)
        return both[:RANK] + both[RANK:]

    def prepare(n):
        cols = slice(n * HEAD, (n + 1) * HEAD)
        kv_up = jnp.concatenate([up_wide[1, :, cols], up_wide[2, :, cols]], axis=1)
        q_s[n] = (fq[0, :, cols].astype(F32) + dot(low_own[...], up_wide[0, :, cols])).astype(BF16)
        arrived = [halo[0, :, cols] for halo in halos]
        if first:
            begin = pl.program_id(0) < EARLY // PER_STEP
            arrived = [jnp.where(begin, e[0, :, cols], a) for e, a in zip(early, arrived)]
        sides = (arrived[:2], (fk[0, :, cols], fv[0, :, cols]), arrived[2:])
        up0 = up[0, :, cols]
        up0_twice = jnp.concatenate([up0, up0, jnp.zeros((2 * RANK, HEAD), BF16)], axis=0)
        for i, (k_in, v_in) in enumerate(sides):
            rows = slice(i * slab, (i + 1) * slab)
            low = vl_s[n, rows, HEAD:]
            added = dot(low, kv_up)
            keys = (k_in.astype(F32) + added[:, :HEAD]).astype(BF16)
            k_s[n, rows, :] = keys
            vl_s[n, rows, :HEAD] = (v_in.astype(F32) + added[:, HEAD:]).astype(BF16)
            ku = dot_t(keys, up0_twice)
            rest = ku - ku.astype(BF16).astype(F32)
            kx_s[n, rows, :] = jnp.where(
                lane < RANK, ku, jnp.where(lane < 2 * RANK, rest, low.astype(F32))
            ).astype(BF16)
        hi, lo = split_rows(dot_t(up[1, :, cols], q_s[n]))
        xb_s[n] = jnp.concatenate([hi, lo, low0_t[...]], axis=0)
        hi, lo = split_rows(dot_t(up[2, :, cols], out_grad[0, :, cols]))
        xd_s[n] = jnp.concatenate([hi, lo], axis=0)

    def products(n, rows):
        cols = slice(n * HEAD, (n + 1) * HEAD)
        scores = dot_t(q_s[n, rows, :], k_s[n])
        prob_grad = dot_t(out_grad[0, rows, cols], vl_s[n, :, :HEAD])
        return scores, prob_grad

    def soften(rows, scores, prob_grad):
        tiles = range(rows.start // TILE, rows.stop // TILE)
        tile_rows = jnp.concatenate(
            [jnp.broadcast_to(bias[t:t + 1, :], (TILE, 3 * slab)) for t in tiles], axis=0
        )
        scores = scores * (scale * LOG2E) + tile_rows
        row_max = jnp.max(scores, axis=1, keepdims=True)
        weights = jnp.exp2(scores - row_max)
        totals = jnp.sum(weights, axis=1, keepdims=True)
        probs = weights * (1.0 / totals)
        centre = jnp.sum(probs * prob_grad, axis=1, keepdims=True)
        score_grad = (probs * (prob_grad - centre) * scale).astype(BF16)
        return probs.astype(BF16), score_grad

    def spread(n, rows, probs_low, score_grad):
        out = dot(probs_low, vl_s[n])
        attended[0, rows, n * HEAD:(n + 1) * HEAD] = out[:, :HEAD].astype(BF16)
        cat_s[n, rows, :HEAD] = out[:, HEAD:]
        cat_s[n, rows, HEAD:] = dot(score_grad, kx_s[n])
        return dot(xd_s[n, :, rows], probs_low), dot(xb_s[n, :, rows], score_grad)

    def finish(n, d_total, b_total):
        cols = slice(n * HEAD, (n + 1) * HEAD)
        cat_t = cat_s[n].T
        c_t = cat_t[:RANK]
        a_t = cat_t[HEAD:]
        grad_up[0, :, cols] = pair(b_total[2 * RANK:], k_s[n])
        grad_up[1, :, cols] = pair(a_t[2 * RANK:3 * RANK], q_s[n])
        grad_up[2, :, cols] = pair(c_t, out_grad[0, :, cols])
        return (a_t[:RANK] + a_t[RANK:2 * RANK], b_total[:RANK] + b_total[RANK:2 * RANK],
                d_total[:RANK] + d_total[RANK:])

    steps = [(n, slice(r, r + QBLOCK)) for n in range(PER_STEP) for r in range(0, slab, QBLOCK)]
    totals = [[None, None] for _ in range(PER_STEP)]
    for n in range(PER_STEP):
        prepare(n)
    made = {}
    soft = {}
    for i in range(len(steps) + 2):
        if i < len(steps):
            made[i] = products(*steps[i])
        if 0 <= i - 1 < len(steps):
            soft[i - 1] = soften(steps[i - 1][1], *made.pop(i - 1))
        if 0 <= i - 2 < len(steps):
            n, rows = steps[i - 2]
            parts = spread(n, rows, *soft.pop(i - 2))
            totals[n] = [p if t is None else t + p for t, p in zip(totals[n], parts)]
    shares = [finish(n, *totals[n]) for n in range(PER_STEP)]
    rq[...] += sum(s[0] for s in shares)
    rkv[:RANK] += sum(s[1] for s in shares)
    rkv[RANK:] += sum(s[2] for s in shares)

    if last:
        @pl.when(pl.program_id(0) == pl.num_programs(0) - 1)
        def _():
            to_prev[...] = rkv[:, :slab].astype(BF16)
            to_next[...] = rkv[:, 2 * slab:].astype(BF16)


def whole(x):
    return pl.BlockSpec(x.shape, lambda *_: (0,) * len(x.shape))


def attend_chunk(h0, heads, last, shared, own, ups, halo, early, carried):
    slab = own[0].shape[1]
    across = own[0].shape[2]
    first = carried is None
    steps = heads // PER_STEP
    wide = PER_STEP * HEAD
    skipped = early[0].shape[2] // wide if first else 0

    own_spec = pl.BlockSpec((1, slab, wide), lambda h: (0, 0, h0 // PER_STEP + h))

    def halo_specs(skipped):
        return [
            pl.BlockSpec((1, slab, wide), lambda h, kind=kind: (kind, 0, jnp.maximum(h - skipped, 0)))
            for kind in (0, 1, 0, 1)
        ]

    low_spec = pl.BlockSpec((2, TILE, shared[-1].shape[2]), lambda h: (0, slab // TILE, 0))
    in_specs = [whole(x) for x in shared[:-2]] + [low_spec] * 2 + [own_spec] * 4 + [
        pl.BlockSpec((3, x.shape[1], wide), lambda h: (0, 0, h0 // PER_STEP + h)) for x in ups
    ] + halo_specs(skipped)
    operands = [*shared, *own, *ups, halo[0], halo[0], halo[1], halo[1]]
    if first:
        in_specs += [
            pl.BlockSpec(
                (1, slab, wide), lambda h, kind=kind: (kind, 0, jnp.minimum(h, skipped - 1))
            ) for kind in (0, 1, 0, 1)
        ]
        operands += [early[0], early[0], early[1], early[1]]
    aliases = {}
    if not first:
        attended, rq, rkv = carried
        aliases = {len(operands) + 2: 0}
        operands += [rq, rkv, attended]
        in_specs += [whole(rq), whole(rkv), pl.BlockSpec(memory_space=pl.ANY)]
    rq_shape = jax.ShapeDtypeStruct((RANK, slab), F32)
    rkv_shape = jax.ShapeDtypeStruct((2 * RANK, 3 * slab), F32)
    sent_shape = jax.ShapeDtypeStruct((2 * RANK, slab), BF16)
    return pl.pallas_call(
        functools.partial(attend_kernel, first, last, slab),
        grid=(steps,),
        in_specs=in_specs,
        out_specs=[
            own_spec,
            pl.BlockSpec((3, RANK, wide), lambda h: (0, 0, h)),
            whole(rq_shape),
            whole(rkv_shape),
        ] + [whole(sent_shape)] * (2 * last),
        out_shape=[
            jax.ShapeDtypeStruct((1, slab, across), BF16),
            jax.ShapeDtypeStruct((3, RANK, heads * HEAD), F32),
            rq_shape,
            rkv_shape,
        ] + [sent_shape] * (2 * last),
        scratch_shapes=[
            pltpu.VMEM((PER_STEP, slab, HEAD), BF16),
            pltpu.VMEM((PER_STEP, 3 * slab, HEAD), BF16),
            pltpu.VMEM((PER_STEP, 3 * slab, 2 * HEAD), BF16),
            pltpu.VMEM((PER_STEP, 3 * slab, HEAD), BF16),
            pltpu.VMEM((PER_STEP, 3 * RANK, slab), BF16),
            pltpu.VMEM((PER_STEP, 2 * RANK, slab), BF16),
            pltpu.VMEM((PER_STEP, slab, 2 * HEAD), F32),
        ],
        input_output_aliases=aliases,
        compiler_params=pltpu.CompilerParams(
            dimension_semantics=("arbitrary",), vmem_limit_bytes=48 << 20
        ),
        cost_estimate=pl.CostEstimate(
            flops=heads * ATTEND_FLOPS, transcendentals=heads * 3 * slab * slab,
            bytes_accessed=heads * 10 * slab * HEAD * 2,
        ),
        name=f"attend_{h0}",
    )(*operands)


def prologue_kernel(step, x, shift_scale, down, x_mod, low, low_sent, low0_t, down_s):
    del step
    width = x.shape[2]

    @pl.when(pl.program_id(0) == 0)
    def _():
        down_s[...] = jnp.concatenate(
            [down[2], down[0], down[1], jnp.zeros((RANK, width), BF16)], axis=0
        )

    x_full = x[0].astype(F32)
    centred = x_full - jnp.sum(x_full, axis=1, keepdims=True) * (1.0 / width)
    variance = jnp.sum(centred * centred, axis=1, keepdims=True) * (1.0 / width)
    normed = centred * lax.rsqrt(variance + 1e-06)
    modulated = (normed * (1.0 + shift_scale[0, 1:2, :]) + shift_scale[0, 0:1, :]).astype(BF16)
    x_mod[...] = modulated
    reduced = dot_t(modulated, down_s[...])
    low[...] = reduced.astype(BF16)
    low_sent[0] = reduced.astype(BF16)
    low0_t[...] = reduced.T[RANK:2 * RANK].astype(BF16)


def prologue(hidden, truncation_step, modulation, down):
    _, slab, width = hidden.shape
    hidden, modulation, down = [
        pltpu.with_memory_space_constraint(x, pltpu.HBM) for x in (hidden, modulation, down)
    ]
    return pl.pallas_call(
        prologue_kernel,
        grid_spec=pltpu.PrefetchScalarGridSpec(
            num_scalar_prefetch=1,
            grid=(slab // TILE,),
            in_specs=[
                pl.BlockSpec((1, TILE, width), lambda i, step: (0, i, 0)),
                pl.BlockSpec((1, 2, width), lambda i, step: (step[0], 0, 0)),
                whole(down),
            ],
            out_specs=[
                pl.BlockSpec((TILE, width), lambda i, step: (i, 0)),
                pl.BlockSpec((TILE, 4 * RANK), lambda i, step: (i, 0)),
                pl.BlockSpec((1, TILE, 4 * RANK), lambda i, step: (i % 2, 0, i // 2)),
                pl.BlockSpec((RANK, TILE), lambda i, step: (0, i)),
            ],
            scratch_shapes=[pltpu.VMEM((4 * RANK, width), BF16)],
        ),
        out_shape=[
            jax.ShapeDtypeStruct((slab, width), BF16),
            jax.ShapeDtypeStruct((slab, 4 * RANK), BF16),
            jax.ShapeDtypeStruct((2, TILE, slab // TILE // 2 * 4 * RANK), BF16),
            jax.ShapeDtypeStruct((RANK, slab), BF16),
        ],
        compiler_params=pltpu.CompilerParams(
            dimension_semantics=("arbitrary",), vmem_limit_bytes=48 << 20
        ),
        name="prologue",
    )(truncation_step, hidden, modulation, down)


def project_kernel(factor, rq, rkv, from_prev, from_next, x_mod, *refs):
    parts, out = refs[:-1], refs[-1]
    rank_kv = rkv[...] + from_prev[...].astype(F32) + from_next[...].astype(F32)
    hi, lo = split_rows(jnp.concatenate([rq[...], rank_kv], axis=0))
    both = dot(jnp.concatenate([hi, lo], axis=0), x_mod[...])
    down = ((both[:3 * RANK] + both[3 * RANK:]) * factor).astype(BF16)
    columns = x_mod.shape[1] // HEAD
    tiles = 3 * RANK // 16
    first = pl.program_id(0) * (columns * tiles)
    for c in range(columns):
        for r in range(tiles):
            out[first + c * tiles + r] = down[16 * r:16 * r + 16, c * HEAD:(c + 1) * HEAD]

    @pl.when(pl.program_id(0) == pl.num_programs(0) - 1)
    def _():
        at = pl.num_programs(0) * (columns * tiles)
        for part in parts:
            for c in range(part.shape[2] // HEAD):
                for r in range(tiles):
                    rows = slice(16 * (r % 2), 16 * (r % 2) + 16)
                    piece = part[r // 2, rows, c * HEAD:(c + 1) * HEAD] * factor
                    out[at + r] = piece.astype(BF16)
                at = at + tiles
        for g in range(PADDING):
            out[at + g] = jnp.zeros((16, HEAD), BF16)


def project(factor, rq, rkv, from_prev, from_next, x_mod, parts):
    slab, width = x_mod.shape
    across = sum(p.shape[2] for p in parts)
    tiles = (width + across) // HEAD * (3 * RANK // 16) + PADDING
    block = width // 4
    shape = jax.ShapeDtypeStruct((tiles, 16, HEAD), BF16)
    return pl.pallas_call(
        functools.partial(project_kernel, factor),
        grid=(width // block,),
        in_specs=[
            whole(rq),
            pl.BlockSpec((2 * RANK, slab), lambda i: (0, 1)),
            whole(from_prev),
            whole(from_next),
            pl.BlockSpec((slab, block), lambda i: (0, i)),
        ] + [whole(p) for p in parts],
        out_specs=whole(shape),
        out_shape=shape,
        compiler_params=pltpu.CompilerParams(
            dimension_semantics=("arbitrary",), vmem_limit_bytes=48 << 20
        ),
        name="project",
    )(rq, rkv, from_prev, from_next, x_mod, *parts)


def unpack_kernel(packed, down, up):
    tiles = 3 * RANK // 16
    g = 0
    for out in (down, up):
        for c in range(out.shape[2] // HEAD):
            for r in range(tiles):
                rows = slice(16 * (r % 2), 16 * (r % 2) + 16)
                out[r // 2, rows, c * HEAD:(c + 1) * HEAD] = packed[g].astype(F32)
                g += 1


def unpack(packed, width, across):
    shapes = [jax.ShapeDtypeStruct((3, RANK, n), F32) for n in (width, across)]
    return pl.pallas_call(unpack_kernel, out_shape=shapes, name="unpack")(packed)


def neighbours(before, after, axis):
    count = lax.axis_size(axis)
    up = [(i, (i + 1) % count) for i in range(count)]
    down = [(j, i) for i, j in up]
    return lax.ppermute(before, axis, up), lax.ppermute(after, axis, down)


def reduce_everywhere(x, batch, tiles):
    count = lax.axis_size(tiles)
    parts = x.reshape(count, x.shape[0] // count * 16, HEAD)
    got = lax.all_to_all(parts, tiles, 0, 0, tiled=True)
    mine = jnp.sum(got.astype(F32), axis=0).astype(BF16)
    peers = lax.axis_size(batch)
    one, two, three = [
        lax.ppermute(mine, batch, [(i, i ^ d) for i in range(peers)]).astype(F32) for d in (1, 2, 3)
    ]
    total = ((mine.astype(F32) + one) + (two + three)).astype(BF16)
    spread = jnp.broadcast_to(total[None], (count,) + total.shape)
    return lax.all_to_all(spread, tiles, 0, 0, tiled=True).reshape(x.shape)


def per_device(
    hidden,
    frozen_queries,
    frozen_keys,
    frozen_values,
    reward_output_gradient,
    truncation_step,
    modulation,
    adapter_down_weight,
    adapter_up_weight,
    window,
):
    slab = hidden.shape[1]
    width = hidden.shape[2]
    across = frozen_queries.shape[2]
    bounds = []
    h0 = 0
    for heads in CHUNKS:
        bounds.append((h0, heads))
        h0 += heads

    def frozen_part(h0, heads):
        columns = slice(h0 * HEAD, (h0 + heads) * HEAD)
        return jnp.concatenate([frozen_keys[:, :, columns], frozen_values[:, :, columns]], axis=0)

    part = frozen_part(0, EARLY)
    early = neighbours(part, part, "tiles")
    x_mod, low, low_sent, low0_t = prologue(
        hidden, truncation_step, modulation, adapter_down_weight.transpose(0, 2, 1)
    )
    bounds[0] = (EARLY, CHUNKS[0] - EARLY)
    parts = [frozen_part(*b) for b in bounds]
    *early, low_sent = lax.optimization_barrier((*early, low_sent))
    parts[0] = jnp.concatenate([parts[0], low_sent], axis=1)
    bounds[0] = (0, CHUNKS[0])
    parts = lax.optimization_barrier(parts)
    halos = [neighbours(part, part, "tiles") for part in parts]

    up = adapter_up_weight
    pad = lambda x, before: jnp.pad(x, ((before, 3 * RANK - before), (0, 0)))
    up_wide = jnp.stack([pad(up[0], RANK), pad(up[1], 2 * RANK), pad(up[2], 0)])
    bias = tile_bias(window, lax.axis_index("tiles"), lax.axis_size("tiles"))
    shared = (bias, low, low0_t, *halos[0])
    own = (frozen_queries, frozen_keys, frozen_values, reward_output_gradient)
    carried = None
    grad_up_parts = []
    for i, ((h0, heads), halo) in enumerate(zip(bounds, halos)):
        attended, grad_up, rq, rkv, *sent = attend_chunk(
            h0, heads, i == len(bounds) - 1, shared, own, (up_wide, up), halo, early, carried
        )
        carried = (attended, rq, rkv)
        grad_up_parts.append(grad_up)

    norm_factor = 1.0 / math.sqrt(
        hidden.shape[0] * lax.axis_size("batch") * slab * lax.axis_size("tiles")
    )
    to_prev, to_next = sent
    from_prev, from_next = neighbours(to_next, to_prev, "tiles")
    packed = project(norm_factor, rq, rkv, from_prev, from_next, x_mod, grad_up_parts)
    packed = reduce_everywhere(packed, "batch", "tiles")
    grad_down, grad_up = unpack(packed, width, across)
    return (attended, grad_down.transpose(0, 2, 1), grad_up)


def solution(mesh):
    placed = (
        P("batch", "tiles", None),
        P("batch", "tiles", None),
        P("batch", "tiles", None),
        P("batch", "tiles", None),
        P("batch", "tiles", None),
        P("batch"),
        P(),
        P(),
        P(),
        P("tiles", None),
    )
    return jax.shard_map(
        per_device,
        mesh=mesh,
        in_specs=placed,
        out_specs=(P("batch", "tiles", None), P(), P()),
        check_vma=False,
    )
```

```python
import functools
import math

import jax
import jax.numpy as jnp
from jax import lax
from jax.experimental import pallas as pl
from jax.experimental.pallas import tpu as pltpu
from jax.sharding import PartitionSpec as P

HEAD = 128
TILE = 128
GF = 2
GR = 2
RANK = 32
LOG2E = 1.4426950408889634
ATTEND_FLOPS = 4_600_000_000
CHUNKS = (6, 4, 2)
QBLOCK = 512
PADDING = 8
PER_STEP = 2
F32 = jnp.float32
BF16 = jnp.bfloat16


def tile_bias(window_rows, slab_index, slab_count):
    per_slab = GF * GR
    query_tile = jnp.arange(per_slab, dtype=jnp.int32)
    key_tile = jnp.arange(3 * per_slab, dtype=jnp.int32)
    key_side = key_tile // per_slab
    key_local = key_tile % per_slab
    frame_step = key_local[None, :] // GR - query_tile[:, None] // GR
    row_step = key_local[None, :] % GR - query_tile[:, None] % GR
    offset_code = (key_side[None, :] * 3 + frame_step + 1) * 3 + row_step + 1
    nearby = (jnp.abs(frame_step) <= 1) & (jnp.abs(row_step) <= 1)
    neighbour = slab_index + key_side - 1
    inside = (neighbour >= 0) & (neighbour < slab_count)
    offsets = jnp.arange(27, dtype=jnp.int32)
    listed = jnp.sum(
        jnp.where(offset_code[:, :, None] == offsets[None, None, :], window_rows[:, None, :], 0),
        axis=2,
    )
    tile_mask = nearby & inside[None, :] & (listed > 0)
    return jnp.repeat(jnp.where(tile_mask, 0.0, -1e30).astype(F32), TILE, axis=1)


def dot(a, b):
    return lax.dot_general(a, b, (((1,), (0,)), ((), ())), preferred_element_type=F32)


def dot_t(a, b):
    return lax.dot_general(a, b, (((1,), (1,)), ((), ())), preferred_element_type=F32)


def split_rows(x):
    hi = x.astype(BF16)
    lo = (x - hi.astype(F32)).astype(BF16)
    return hi, lo


def attend_kernel(first, last, slab, *refs):
    (bias, low_own, low0_t, low_prev, low_next, fq, fk, fv, out_grad, up_wide, up) = refs[:11]
    halos = refs[11:15]
    refs = refs[15:]
    if not first:
        rq_in, rkv_in, _ = refs[:3]
        refs = refs[3:]
    attended, grad_up, rq, rkv = refs[:4]
    refs = refs[4:]
    if last:
        to_prev, to_next = refs[:2]
        refs = refs[2:]
    q_s, kl_s, vl_s, xb_s, xd_s, dq_s, cat_s = refs
    scale = 1.0 / math.sqrt(HEAD)

    @pl.when(pl.program_id(0) == 0)
    def _():
        for n in range(PER_STEP):
            vl_s[n, slab:2 * slab, HEAD:] = low_own[...]
            kl_s[n, slab:2 * slab, HEAD:] = low_own[...]
            for i, low in ((0, low_prev), (2, low_next)):
                rows = slice(i * slab, (i + 1) * slab)
                vl_s[n, rows, HEAD:] = low[...]
                kl_s[n, rows, HEAD:] = low[...]
        if first:
            rq[...] = jnp.zeros_like(rq)
            rkv[...] = jnp.zeros_like(rkv)
        else:
            rq[...] = rq_in[...]
            rkv[...] = rkv_in[...]

    def pair(left, right):
        hi, lo = split_rows(left)
        both = dot(jnp.concatenate([hi, lo], axis=0), right)
        return both[:RANK] + both[RANK:]

    def prepare(n):
        cols = slice(n * HEAD, (n + 1) * HEAD)
        kv_up = jnp.concatenate([up_wide[1, :, cols], up_wide[2, :, cols]], axis=1)
        q_s[n] = (fq[0, :, cols].astype(F32) + dot(low_own[...], up_wide[0, :, cols])).astype(BF16)
        arrived = [halo[0, :, cols] for halo in halos]
        sides = (arrived[:2], (fk[0, :, cols], fv[0, :, cols]), arrived[2:])
        for i, (k_in, v_in) in enumerate(sides):
            rows = slice(i * slab, (i + 1) * slab)
            low = vl_s[n, rows, HEAD:]
            added = dot(low, kv_up)
            kl_s[n, rows, :HEAD] = (k_in.astype(F32) + added[:, :HEAD]).astype(BF16)
            vl_s[n, rows, :HEAD] = (v_in.astype(F32) + added[:, HEAD:]).astype(BF16)
        hi, lo = split_rows(dot_t(up[1, :, cols], q_s[n]))
        xb_s[n] = jnp.concatenate([hi, lo], axis=0)
        hi, lo = split_rows(dot_t(up[2, :, cols], out_grad[0, :, cols]))
        xd_s[n] = jnp.concatenate([hi, lo], axis=0)

    def products(n, rows):
        cols = slice(n * HEAD, (n + 1) * HEAD)
        scores = dot_t(q_s[n, rows, :], kl_s[n, :, :HEAD])
        prob_grad = dot_t(out_grad[0, rows, cols], vl_s[n, :, :HEAD])
        return scores, prob_grad

    def soften(rows, scores, prob_grad):
        tiles = range(rows.start // TILE, rows.stop // TILE)
        tile_rows = jnp.concatenate(
            [jnp.broadcast_to(bias[t:t + 1, :], (TILE, 3 * slab)) for t in tiles], axis=0
        )
        scores = scores * (scale * LOG2E) + tile_rows
        row_max = jnp.max(scores, axis=1, keepdims=True)
        weights = jnp.exp2(scores - row_max)
        totals = jnp.sum(weights, axis=1, keepdims=True)
        probs = weights * (1.0 / totals)
        centre = jnp.sum(probs * prob_grad, axis=1, keepdims=True)
        score_grad = (probs * (prob_grad - centre) * scale).astype(BF16)
        return probs.astype(BF16), score_grad

    def spread(n, rows, probs_low, score_grad):
        out = dot(probs_low, vl_s[n])
        attended[0, rows, n * HEAD:(n + 1) * HEAD] = out[:, :HEAD].astype(BF16)
        cat_s[n, rows, :HEAD] = out[:, HEAD:]
        out = dot(score_grad, kl_s[n])
        hi, lo = split_rows(out[:, :HEAD])
        dq_s[n, rows, :HEAD] = hi
        dq_s[n, rows, HEAD:] = lo
        cat_s[n, rows, HEAD:] = out[:, HEAD:]
        return dot(xd_s[n, :, rows], probs_low), dot(xb_s[n, :, rows], score_grad)

    def finish(n, d_total, b_total):
        cols = slice(n * HEAD, (n + 1) * HEAD)
        cat_t = cat_s[n].T
        both = dot(low0_t[...], dq_s[n])
        grad_up[0, :, cols] = both[:, :HEAD] + both[:, HEAD:]
        grad_up[1, :, cols] = pair(cat_t[HEAD + 2 * RANK:HEAD + 3 * RANK], q_s[n])
        grad_up[2, :, cols] = pair(cat_t[:RANK], out_grad[0, :, cols])
        up0 = up[0, :, cols]
        return (dot_t(jnp.concatenate([up0, up0], axis=1), dq_s[n]),
                b_total[:RANK] + b_total[RANK:], d_total[:RANK] + d_total[RANK:])

    steps = [(n, slice(r, r + QBLOCK)) for n in range(PER_STEP) for r in range(0, slab, QBLOCK)]
    totals = [[None, None] for _ in range(PER_STEP)]
    for n in range(PER_STEP):
        prepare(n)
    made = {}
    soft = {}
    for i in range(len(steps) + 2):
        if i < len(steps):
            made[i] = products(*steps[i])
        if 0 <= i - 1 < len(steps):
            soft[i - 1] = soften(steps[i - 1][1], *made.pop(i - 1))
        if 0 <= i - 2 < len(steps):
            n, rows = steps[i - 2]
            parts = spread(n, rows, *soft.pop(i - 2))
            totals[n] = [p if t is None else t + p for t, p in zip(totals[n], parts)]
    shares = [finish(n, *totals[n]) for n in range(PER_STEP)]
    rq[...] += sum(s[0] for s in shares)
    rkv[:RANK] += sum(s[1] for s in shares)
    rkv[RANK:] += sum(s[2] for s in shares)

    if last:
        @pl.when(pl.program_id(0) == pl.num_programs(0) - 1)
        def _():
            to_prev[...] = rkv[:, :slab].astype(BF16)
            to_next[...] = rkv[:, 2 * slab:].astype(BF16)


def whole(x):
    return pl.BlockSpec(x.shape, lambda *_: (0,) * len(x.shape))


def attend_chunk(h0, heads, last, shared, own, ups, halo, carried):
    slab = own[0].shape[1]
    across = own[0].shape[2]
    first = carried is None
    steps = heads // PER_STEP
    wide = PER_STEP * HEAD

    own_spec = pl.BlockSpec((1, slab, wide), lambda h: (0, 0, h0 // PER_STEP + h))
    halo_specs = [pl.BlockSpec((1, slab, wide), lambda h, kind=kind: (kind, 0, h)) for kind in (0, 1)]
    in_specs = [whole(x) for x in shared] + [own_spec] * 4 + [
        pl.BlockSpec((3, x.shape[1], wide), lambda h: (0, 0, h0 // PER_STEP + h)) for x in ups
    ] + halo_specs * 2
    operands = [*shared, *own, *ups, halo[0], halo[0], halo[1], halo[1]]
    aliases = {}
    if not first:
        attended, rq, rkv = carried
        aliases = {len(operands) + 2: 0}
        operands += [rq, rkv, attended]
        in_specs += [whole(rq), whole(rkv), pl.BlockSpec(memory_space=pl.ANY)]
    rq_shape = jax.ShapeDtypeStruct((RANK, slab), F32)
    rkv_shape = jax.ShapeDtypeStruct((2 * RANK, 3 * slab), F32)
    sent_shape = jax.ShapeDtypeStruct((2 * RANK, slab), BF16)
    return pl.pallas_call(
        functools.partial(attend_kernel, first, last, slab),
        grid=(steps,),
        in_specs=in_specs,
        out_specs=[
            own_spec,
            pl.BlockSpec((3, RANK, wide), lambda h: (0, 0, h)),
            whole(rq_shape),
            whole(rkv_shape),
        ] + [whole(sent_shape)] * (2 * last),
        out_shape=[
            jax.ShapeDtypeStruct((1, slab, across), BF16),
            jax.ShapeDtypeStruct((3, RANK, heads * HEAD), F32),
            rq_shape,
            rkv_shape,
        ] + [sent_shape] * (2 * last),
        scratch_shapes=[
            pltpu.VMEM((PER_STEP, slab, HEAD), BF16),
            pltpu.VMEM((PER_STEP, 3 * slab, 2 * HEAD), BF16),
            pltpu.VMEM((PER_STEP, 3 * slab, 2 * HEAD), BF16),
            pltpu.VMEM((PER_STEP, 2 * RANK, slab), BF16),
            pltpu.VMEM((PER_STEP, 2 * RANK, slab), BF16),
            pltpu.VMEM((PER_STEP, slab, 2 * HEAD), BF16),
            pltpu.VMEM((PER_STEP, slab, 2 * HEAD), F32),
        ],
        input_output_aliases=aliases,
        compiler_params=pltpu.CompilerParams(
            dimension_semantics=("arbitrary",), vmem_limit_bytes=48 << 20
        ),
        cost_estimate=pl.CostEstimate(
            flops=heads * ATTEND_FLOPS, transcendentals=heads * 3 * slab * slab,
            bytes_accessed=heads * 10 * slab * HEAD * 2,
        ),
        name=f"attend_{h0}",
    )(*operands)


def pack_kernel(keys, values, out, sems):
    columns = pl.ds(0, out.shape[2])
    copies = [
        pltpu.make_async_copy(ref.at[0, :, columns], out.at[i], sems.at[i])
        for i, ref in enumerate((keys, values))
    ]
    for copy in copies:
        copy.start()
    for copy in copies:
        copy.wait()


def pack(keys, values, heads):
    keys, values = [pltpu.with_memory_space_constraint(x, pltpu.HBM) for x in (keys, values)]
    hbm = pl.BlockSpec(memory_space=pltpu.HBM)
    return pl.pallas_call(
        pack_kernel,
        in_specs=[hbm, hbm],
        out_specs=hbm,
        out_shape=jax.ShapeDtypeStruct((2, keys.shape[1], heads * HEAD), BF16),
        scratch_shapes=[pltpu.SemaphoreType.DMA((2,))],
        name="pack",
    )(keys, values)


def prologue_kernel(step, x, shift_scale, down, x_mod, low, low0_t, down_s):
    del step
    width = x.shape[2]

    @pl.when(pl.program_id(0) == 0)
    def _():
        down_s[...] = jnp.concatenate(
            [down[2], down[0], down[1], jnp.zeros((RANK, width), BF16)], axis=0
        )

    x_full = x[0].astype(F32)
    centred = x_full - jnp.sum(x_full, axis=1, keepdims=True) * (1.0 / width)
    variance = jnp.sum(centred * centred, axis=1, keepdims=True) * (1.0 / width)
    normed = centred * lax.rsqrt(variance + 1e-06)
    modulated = (normed * (1.0 + shift_scale[0, 1:2, :]) + shift_scale[0, 0:1, :]).astype(BF16)
    x_mod[...] = modulated
    reduced = dot_t(modulated, down_s[...])
    low[...] = reduced.astype(BF16)
    low0_t[...] = reduced.T[RANK:2 * RANK].astype(BF16)


def prologue(hidden, truncation_step, modulation, down):
    _, slab, width = hidden.shape
    hidden, modulation, down = [
        pltpu.with_memory_space_constraint(x, pltpu.HBM) for x in (hidden, modulation, down)
    ]
    return pl.pallas_call(
        prologue_kernel,
        grid_spec=pltpu.PrefetchScalarGridSpec(
            num_scalar_prefetch=1,
            grid=(slab // TILE,),
            in_specs=[
                pl.BlockSpec((1, TILE, width), lambda i, step: (0, i, 0)),
                pl.BlockSpec((1, 2, width), lambda i, step: (step[0], 0, 0)),
                whole(down),
            ],
            out_specs=[
                pl.BlockSpec((TILE, width), lambda i, step: (i, 0)),
                pl.BlockSpec((TILE, 4 * RANK), lambda i, step: (i, 0)),
                pl.BlockSpec((RANK, TILE), lambda i, step: (0, i)),
            ],
            scratch_shapes=[pltpu.VMEM((4 * RANK, width), BF16)],
        ),
        out_shape=[
            jax.ShapeDtypeStruct((slab, width), BF16),
            jax.ShapeDtypeStruct((slab, 4 * RANK), BF16),
            jax.ShapeDtypeStruct((RANK, slab), BF16),
        ],
        compiler_params=pltpu.CompilerParams(
            dimension_semantics=("arbitrary",), vmem_limit_bytes=48 << 20
        ),
        name="prologue",
    )(truncation_step, hidden, modulation, down)


def project_kernel(factor, rq, rkv, from_prev, from_next, x_mod, *refs):
    parts, out = refs[:-1], refs[-1]
    rank_kv = rkv[...] + from_prev[...].astype(F32) + from_next[...].astype(F32)
    hi, lo = split_rows(jnp.concatenate([rq[...], rank_kv], axis=0))
    both = dot(jnp.concatenate([hi, lo], axis=0), x_mod[...])
    down = ((both[:3 * RANK] + both[3 * RANK:]) * factor).astype(BF16)
    columns = x_mod.shape[1] // HEAD
    tiles = 3 * RANK // 16
    first = pl.program_id(0) * (columns * tiles)
    for c in range(columns):
        for r in range(tiles):
            out[first + c * tiles + r] = down[16 * r:16 * r + 16, c * HEAD:(c + 1) * HEAD]

    @pl.when(pl.program_id(0) == pl.num_programs(0) - 1)
    def _():
        at = pl.num_programs(0) * (columns * tiles)
        for part in parts:
            for c in range(part.shape[2] // HEAD):
                for r in range(tiles):
                    rows = slice(16 * (r % 2), 16 * (r % 2) + 16)
                    piece = part[r // 2, rows, c * HEAD:(c + 1) * HEAD] * factor
                    out[at + r] = piece.astype(BF16)
                at = at + tiles
        for g in range(PADDING):
            out[at + g] = jnp.zeros((16, HEAD), BF16)


def project(factor, rq, rkv, from_prev, from_next, x_mod, parts):
    slab, width = x_mod.shape
    across = sum(p.shape[2] for p in parts)
    tiles = (width + across) // HEAD * (3 * RANK // 16) + PADDING
    block = width // 4
    shape = jax.ShapeDtypeStruct((tiles, 16, HEAD), BF16)
    return pl.pallas_call(
        functools.partial(project_kernel, factor),
        grid=(width // block,),
        in_specs=[
            whole(rq),
            pl.BlockSpec((2 * RANK, slab), lambda i: (0, 1)),
            whole(from_prev),
            whole(from_next),
            pl.BlockSpec((slab, block), lambda i: (0, i)),
        ] + [whole(p) for p in parts],
        out_specs=whole(shape),
        out_shape=shape,
        compiler_params=pltpu.CompilerParams(
            dimension_semantics=("arbitrary",), vmem_limit_bytes=48 << 20
        ),
        name="project",
    )(rq, rkv, from_prev, from_next, x_mod, *parts)


def unpack_kernel(packed, down, up):
    tiles = 3 * RANK // 16
    g = 0
    for out in (down, up):
        for c in range(out.shape[2] // HEAD):
            for r in range(tiles):
                rows = slice(16 * (r % 2), 16 * (r % 2) + 16)
                out[r // 2, rows, c * HEAD:(c + 1) * HEAD] = packed[g].astype(F32)
                g += 1


def unpack(packed, width, across):
    shapes = [jax.ShapeDtypeStruct((3, RANK, n), F32) for n in (width, across)]
    return pl.pallas_call(unpack_kernel, out_shape=shapes, name="unpack")(packed)


def neighbours(before, after, axis):
    count = lax.axis_size(axis)
    up = [(i, (i + 1) % count) for i in range(count)]
    down = [(j, i) for i, j in up]
    return lax.ppermute(before, axis, up), lax.ppermute(after, axis, down)


def reduce_everywhere(x, batch, tiles):
    count = lax.axis_size(tiles)
    parts = x.reshape(count, x.shape[0] // count * 16, HEAD)
    got = lax.all_to_all(parts, tiles, 0, 0, tiled=True)
    mine = jnp.sum(got.astype(F32), axis=0).astype(BF16)
    peers = lax.axis_size(batch)
    one, two, three = [
        lax.ppermute(mine, batch, [(i, i ^ d) for i in range(peers)]).astype(F32) for d in (1, 2, 3)
    ]
    total = ((mine.astype(F32) + one) + (two + three)).astype(BF16)
    spread = jnp.broadcast_to(total[None], (count,) + total.shape)
    return lax.all_to_all(spread, tiles, 0, 0, tiled=True).reshape(x.shape)


def per_device(
    hidden,
    frozen_queries,
    frozen_keys,
    frozen_values,
    reward_output_gradient,
    truncation_step,
    modulation,
    adapter_down_weight,
    adapter_up_weight,
    window,
):
    slab = hidden.shape[1]
    width = hidden.shape[2]
    across = frozen_queries.shape[2]
    bounds = []
    h0 = 0
    for heads in CHUNKS:
        bounds.append((h0, heads))
        h0 += heads

    def frozen_part(h0, heads):
        columns = slice(h0 * HEAD, (h0 + heads) * HEAD)
        return jnp.concatenate([frozen_keys[:, :, columns], frozen_values[:, :, columns]], axis=0)

    part = pack(frozen_keys, frozen_values, CHUNKS[0])
    early = neighbours(part, part, "tiles")
    x_mod, low, low0_t = prologue(
        hidden, truncation_step, modulation, adapter_down_weight.transpose(0, 2, 1)
    )
    parts = [frozen_part(*b) for b in bounds[1:]]
    early, low, parts = lax.optimization_barrier((early, low, parts))
    lows = neighbours(low, low, "tiles")
    halos = [early] + [neighbours(part, part, "tiles") for part in parts]

    up = adapter_up_weight
    pad = lambda x, before: jnp.pad(x, ((before, 3 * RANK - before), (0, 0)))
    up_wide = jnp.stack([pad(up[0], RANK), pad(up[1], 2 * RANK), pad(up[2], 0)])
    bias = tile_bias(window, lax.axis_index("tiles"), lax.axis_size("tiles"))
    shared = (bias, low, low0_t, *lows)
    own = (frozen_queries, frozen_keys, frozen_values, reward_output_gradient)
    carried = None
    grad_up_parts = []
    for i, ((h0, heads), halo) in enumerate(zip(bounds, halos)):
        attended, grad_up, rq, rkv, *sent = attend_chunk(
            h0, heads, i == len(bounds) - 1, shared, own, (up_wide, up), halo, carried
        )
        carried = (attended, rq, rkv)
        grad_up_parts.append(grad_up)

    norm_factor = 1.0 / math.sqrt(
        hidden.shape[0] * lax.axis_size("batch") * slab * lax.axis_size("tiles")
    )
    to_prev, to_next = sent
    from_prev, from_next = neighbours(to_next, to_prev, "tiles")
    packed = project(norm_factor, rq, rkv, from_prev, from_next, x_mod, grad_up_parts)
    packed = reduce_everywhere(packed, "batch", "tiles")
    grad_down, grad_up = unpack(packed, width, across)
    return (attended, grad_down.transpose(0, 2, 1), grad_up)


def solution(mesh):
    placed = (
        P("batch", "tiles", None),
        P("batch", "tiles", None),
        P("batch", "tiles", None),
        P("batch", "tiles", None),
        P("batch", "tiles", None),
        P("batch"),
        P(),
        P(),
        P(),
        P("tiles", None),
    )
    return jax.shard_map(
        per_device,
        mesh=mesh,
        in_specs=placed,
        out_specs=(P("batch", "tiles", None), P(), P()),
        check_vma=False,
    )
```

```python
import functools
import math

import jax
import jax.numpy as jnp
from jax import lax
from jax.experimental import pallas as pl
from jax.experimental.pallas import tpu as pltpu
from jax.sharding import PartitionSpec as P

HEAD = 128
TILE = 128
GF = 2
GR = 2
RANK = 32
LOG2E = 1.4426950408889634
ATTEND_FLOPS = 4_600_000_000
CHUNKS = (6, 4, 2)
QBLOCK = 512
PADDING = 8
PER_STEP = 2
F32 = jnp.float32
BF16 = jnp.bfloat16


def tile_bias(window_rows, slab_index, slab_count):
    per_slab = GF * GR
    query_tile = jnp.arange(per_slab, dtype=jnp.int32)
    key_tile = jnp.arange(3 * per_slab, dtype=jnp.int32)
    key_side = key_tile // per_slab
    key_local = key_tile % per_slab
    frame_step = key_local[None, :] // GR - query_tile[:, None] // GR
    row_step = key_local[None, :] % GR - query_tile[:, None] % GR
    offset_code = (key_side[None, :] * 3 + frame_step + 1) * 3 + row_step + 1
    nearby = (jnp.abs(frame_step) <= 1) & (jnp.abs(row_step) <= 1)
    neighbour = slab_index + key_side - 1
    inside = (neighbour >= 0) & (neighbour < slab_count)
    offsets = jnp.arange(27, dtype=jnp.int32)
    listed = jnp.sum(
        jnp.where(offset_code[:, :, None] == offsets[None, None, :], window_rows[:, None, :], 0),
        axis=2,
    )
    tile_mask = nearby & inside[None, :] & (listed > 0)
    return jnp.repeat(jnp.where(tile_mask, 0.0, -1e30).astype(F32), TILE, axis=1)


def dot(a, b):
    return lax.dot_general(a, b, (((1,), (0,)), ((), ())), preferred_element_type=F32)


def dot_t(a, b):
    return lax.dot_general(a, b, (((1,), (1,)), ((), ())), preferred_element_type=F32)


def split_rows(x):
    hi = x.astype(BF16)
    lo = (x - hi.astype(F32)).astype(BF16)
    return hi, lo


def attend_kernel(first, last, slab, *refs):
    (bias, low_own, low0_t, low_prev, low_next, fq, fk, fv, out_grad, up_wide, up) = refs[:11]
    halos = refs[11:15]
    refs = refs[15:]
    if not first:
        rq_in, rkv_in, _ = refs[:3]
        refs = refs[3:]
    attended, grad_up, rq, rkv = refs[:4]
    refs = refs[4:]
    if last:
        to_prev, to_next = refs[:2]
        refs = refs[2:]
    q_s, kl_s, vl_s, xb_s, xd_s, dq_s, cat_s = refs
    scale = 1.0 / math.sqrt(HEAD)

    @pl.when(pl.program_id(0) == 0)
    def _():
        for n in range(PER_STEP):
            vl_s[n, slab:2 * slab, HEAD:] = low_own[...]
            kl_s[n, slab:2 * slab, HEAD:] = low_own[...]
            for i, low in ((0, low_prev), (2, low_next)):
                rows = slice(i * slab, (i + 1) * slab)
                vl_s[n, rows, HEAD:] = low[0]
                kl_s[n, rows, HEAD:] = low[0]
        if first:
            rq[...] = jnp.zeros_like(rq)
            rkv[...] = jnp.zeros_like(rkv)
        else:
            rq[...] = rq_in[...]
            rkv[...] = rkv_in[...]

    def pair(left, right):
        hi, lo = split_rows(left)
        both = dot(jnp.concatenate([hi, lo], axis=0), right)
        return both[:RANK] + both[RANK:]

    def prepare(n):
        cols = slice(n * HEAD, (n + 1) * HEAD)
        kv_up = jnp.concatenate([up_wide[1, :, cols], up_wide[2, :, cols]], axis=1)
        q_s[n] = (fq[0, :, cols].astype(F32) + dot(low_own[...], up_wide[0, :, cols])).astype(BF16)
        at = n if first else (0, slice(None), cols)
        arrived = [halo[at] for halo in halos]
        sides = (arrived[:2], (fk[0, :, cols], fv[0, :, cols]), arrived[2:])
        for i, (k_in, v_in) in enumerate(sides):
            rows = slice(i * slab, (i + 1) * slab)
            low = vl_s[n, rows, HEAD:]
            added = dot(low, kv_up)
            kl_s[n, rows, :HEAD] = (k_in.astype(F32) + added[:, :HEAD]).astype(BF16)
            vl_s[n, rows, :HEAD] = (v_in.astype(F32) + added[:, HEAD:]).astype(BF16)
        hi, lo = split_rows(dot_t(up[1, :, cols], q_s[n]))
        xb_s[n] = jnp.concatenate([hi, lo], axis=0)
        hi, lo = split_rows(dot_t(up[2, :, cols], out_grad[0, :, cols]))
        xd_s[n] = jnp.concatenate([hi, lo], axis=0)

    def products(n, rows):
        cols = slice(n * HEAD, (n + 1) * HEAD)
        scores = dot_t(q_s[n, rows, :], kl_s[n, :, :HEAD])
        prob_grad = dot_t(out_grad[0, rows, cols], vl_s[n, :, :HEAD])
        return scores, prob_grad

    def soften(rows, scores, prob_grad):
        tiles = range(rows.start // TILE, rows.stop // TILE)
        tile_rows = jnp.concatenate(
            [jnp.broadcast_to(bias[t:t + 1, :], (TILE, 3 * slab)) for t in tiles], axis=0
        )
        scores = scores * (scale * LOG2E) + tile_rows
        row_max = jnp.max(scores, axis=1, keepdims=True)
        weights = jnp.exp2(scores - row_max)
        totals = jnp.sum(weights, axis=1, keepdims=True)
        probs = weights * (1.0 / totals)
        centre = jnp.sum(probs * prob_grad, axis=1, keepdims=True)
        score_grad = (probs * (prob_grad - centre) * scale).astype(BF16)
        return probs.astype(BF16), score_grad

    def spread(n, rows, probs_low, score_grad):
        out = dot(probs_low, vl_s[n])
        attended[0, rows, n * HEAD:(n + 1) * HEAD] = out[:, :HEAD].astype(BF16)
        cat_s[n, rows, :HEAD] = out[:, HEAD:]
        out = dot(score_grad, kl_s[n])
        hi, lo = split_rows(out[:, :HEAD])
        dq_s[n, rows, :HEAD] = hi
        dq_s[n, rows, HEAD:] = lo
        cat_s[n, rows, HEAD:] = out[:, HEAD:]
        return dot(xd_s[n, :, rows], probs_low), dot(xb_s[n, :, rows], score_grad)

    def finish(n, d_total, b_total):
        cols = slice(n * HEAD, (n + 1) * HEAD)
        cat_t = cat_s[n].T
        both = dot(low0_t[...], dq_s[n])
        grad_up[0, :, cols] = both[:, :HEAD] + both[:, HEAD:]
        grad_up[1, :, cols] = pair(cat_t[HEAD + 2 * RANK:HEAD + 3 * RANK], q_s[n])
        grad_up[2, :, cols] = pair(cat_t[:RANK], out_grad[0, :, cols])
        up0 = up[0, :, cols]
        return (dot_t(jnp.concatenate([up0, up0], axis=1), dq_s[n]),
                b_total[:RANK] + b_total[RANK:], d_total[:RANK] + d_total[RANK:])

    steps = [(n, slice(r, r + QBLOCK)) for n in range(PER_STEP) for r in range(0, slab, QBLOCK)]
    totals = [[None, None] for _ in range(PER_STEP)]
    for n in range(PER_STEP):
        prepare(n)
    made = {}
    soft = {}
    for i in range(len(steps) + 2):
        if i < len(steps):
            made[i] = products(*steps[i])
        if 0 <= i - 1 < len(steps):
            soft[i - 1] = soften(steps[i - 1][1], *made.pop(i - 1))
        if 0 <= i - 2 < len(steps):
            n, rows = steps[i - 2]
            parts = spread(n, rows, *soft.pop(i - 2))
            totals[n] = [p if t is None else t + p for t, p in zip(totals[n], parts)]
    shares = [finish(n, *totals[n]) for n in range(PER_STEP)]
    rq[...] += sum(s[0] for s in shares)
    rkv[:RANK] += sum(s[1] for s in shares)
    rkv[RANK:] += sum(s[2] for s in shares)

    if last:
        @pl.when(pl.program_id(0) == pl.num_programs(0) - 1)
        def _():
            to_prev[...] = rkv[:, :slab].astype(BF16)
            to_next[...] = rkv[:, 2 * slab:].astype(BF16)


def whole(x):
    return pl.BlockSpec(x.shape, lambda *_: (0,) * len(x.shape))


def attend_chunk(h0, heads, last, shared, lows, own, ups, halo, carried):
    slab = own[0].shape[1]
    across = own[0].shape[2]
    first = carried is None
    steps = heads // PER_STEP
    wide = PER_STEP * HEAD

    own_spec = pl.BlockSpec((1, slab, wide), lambda h: (0, 0, h0 // PER_STEP + h))
    low_spec = pl.BlockSpec((1, slab, HEAD), lambda h: (lows[0].shape[0] - 1, 0, 0))
    if first:
        halo_specs = [
            pl.BlockSpec((PER_STEP, slab, HEAD), lambda h, skip=skip: (skip + h, 0, 0))
            for skip in (0, steps)
        ]
    else:
        halo_specs = [
            pl.BlockSpec((1, slab, wide), lambda h, kind=kind: (kind, 0, h)) for kind in (0, 1)
        ]
    in_specs = [whole(x) for x in shared] + [low_spec] * 2 + [own_spec] * 4 + [
        pl.BlockSpec((3, x.shape[1], wide), lambda h: (0, 0, h0 // PER_STEP + h)) for x in ups
    ] + halo_specs * 2
    operands = [*shared, *lows, *own, *ups, halo[0], halo[0], halo[1], halo[1]]
    aliases = {}
    if not first:
        attended, rq, rkv = carried
        aliases = {len(operands) + 2: 0}
        operands += [rq, rkv, attended]
        in_specs += [whole(rq), whole(rkv), pl.BlockSpec(memory_space=pl.ANY)]
    rq_shape = jax.ShapeDtypeStruct((RANK, slab), F32)
    rkv_shape = jax.ShapeDtypeStruct((2 * RANK, 3 * slab), F32)
    sent_shape = jax.ShapeDtypeStruct((2 * RANK, slab), BF16)
    return pl.pallas_call(
        functools.partial(attend_kernel, first, last, slab),
        grid=(steps,),
        in_specs=in_specs,
        out_specs=[
            own_spec,
            pl.BlockSpec((3, RANK, wide), lambda h: (0, 0, h)),
            whole(rq_shape),
            whole(rkv_shape),
        ] + [whole(sent_shape)] * (2 * last),
        out_shape=[
            jax.ShapeDtypeStruct((1, slab, across), BF16),
            jax.ShapeDtypeStruct((3, RANK, heads * HEAD), F32),
            rq_shape,
            rkv_shape,
        ] + [sent_shape] * (2 * last),
        scratch_shapes=[
            pltpu.VMEM((PER_STEP, slab, HEAD), BF16),
            pltpu.VMEM((PER_STEP, 3 * slab, 2 * HEAD), BF16),
            pltpu.VMEM((PER_STEP, 3 * slab, 2 * HEAD), BF16),
            pltpu.VMEM((PER_STEP, 2 * RANK, slab), BF16),
            pltpu.VMEM((PER_STEP, 2 * RANK, slab), BF16),
            pltpu.VMEM((PER_STEP, slab, 2 * HEAD), BF16),
            pltpu.VMEM((PER_STEP, slab, 2 * HEAD), F32),
        ],
        input_output_aliases=aliases,
        compiler_params=pltpu.CompilerParams(
            dimension_semantics=("arbitrary",), vmem_limit_bytes=48 << 20
        ),
        cost_estimate=pl.CostEstimate(
            flops=heads * ATTEND_FLOPS, transcendentals=heads * 3 * slab * slab,
            bytes_accessed=heads * 10 * slab * HEAD * 2,
        ),
        name=f"attend_{h0}",
    )(*operands)


def prologue_kernel(step, x, shift_scale, down, fk, fv, x_mod, first_halo, low0_t, down_s):
    del step
    width = x.shape[2]
    heads = fk.shape[2] // HEAD

    @pl.when(pl.program_id(0) == 0)
    def _():
        down_s[...] = jnp.concatenate(
            [down[2], down[0], down[1], jnp.zeros((RANK, width), BF16)], axis=0
        )

    x_full = x[0].astype(F32)
    centred = x_full - jnp.sum(x_full, axis=1, keepdims=True) * (1.0 / width)
    variance = jnp.sum(centred * centred, axis=1, keepdims=True) * (1.0 / width)
    normed = centred * lax.rsqrt(variance + 1e-06)
    modulated = (normed * (1.0 + shift_scale[0, 1:2, :]) + shift_scale[0, 0:1, :]).astype(BF16)
    x_mod[...] = modulated
    reduced = dot_t(modulated, down_s[...])
    for n in range(heads):
        first_halo[n] = fk[0, :, n * HEAD:(n + 1) * HEAD]
        first_halo[heads + n] = fv[0, :, n * HEAD:(n + 1) * HEAD]
    first_halo[2 * heads] = reduced.astype(BF16)
    low0_t[...] = reduced.T[RANK:2 * RANK].astype(BF16)


def prologue(hidden, truncation_step, modulation, down, frozen_keys, frozen_values, heads):
    _, slab, width = hidden.shape
    hidden, modulation, down, frozen_keys, frozen_values = [
        pltpu.with_memory_space_constraint(x, pltpu.HBM)
        for x in (hidden, modulation, down, frozen_keys, frozen_values)
    ]
    frozen_spec = pl.BlockSpec((1, TILE, heads * HEAD), lambda i, step: (0, i, 0))
    return pl.pallas_call(
        prologue_kernel,
        grid_spec=pltpu.PrefetchScalarGridSpec(
            num_scalar_prefetch=1,
            grid=(slab // TILE,),
            in_specs=[
                pl.BlockSpec((1, TILE, width), lambda i, step: (0, i, 0)),
                pl.BlockSpec((1, 2, width), lambda i, step: (step[0], 0, 0)),
                whole(down),
                frozen_spec,
                frozen_spec,
            ],
            out_specs=[
                pl.BlockSpec((TILE, width), lambda i, step: (i, 0)),
                pl.BlockSpec((2 * heads + 1, TILE, HEAD), lambda i, step: (0, i, 0)),
                pl.BlockSpec((RANK, TILE), lambda i, step: (0, i)),
            ],
            scratch_shapes=[pltpu.VMEM((4 * RANK, width), BF16)],
        ),
        out_shape=[
            jax.ShapeDtypeStruct((slab, width), BF16),
            jax.ShapeDtypeStruct((2 * heads + 1, slab, HEAD), BF16),
            jax.ShapeDtypeStruct((RANK, slab), BF16),
        ],
        compiler_params=pltpu.CompilerParams(
            dimension_semantics=("arbitrary",), vmem_limit_bytes=48 << 20
        ),
        name="prologue",
    )(truncation_step, hidden, modulation, down, frozen_keys, frozen_values)


def project_kernel(factor, rq, rkv, from_prev, from_next, x_mod, *refs):
    parts, out = refs[:-1], refs[-1]
    rank_kv = rkv[...] + from_prev[...].astype(F32) + from_next[...].astype(F32)
    hi, lo = split_rows(jnp.concatenate([rq[...], rank_kv], axis=0))
    both = dot(jnp.concatenate([hi, lo], axis=0), x_mod[...])
    down = ((both[:3 * RANK] + both[3 * RANK:]) * factor).astype(BF16)
    columns = x_mod.shape[1] // HEAD
    tiles = 3 * RANK // 16
    first = pl.program_id(0) * (columns * tiles)
    for c in range(columns):
        for r in range(tiles):
            out[first + c * tiles + r] = down[16 * r:16 * r + 16, c * HEAD:(c + 1) * HEAD]

    @pl.when(pl.program_id(0) == pl.num_programs(0) - 1)
    def _():
        at = pl.num_programs(0) * (columns * tiles)
        for part in parts:
            for c in range(part.shape[2] // HEAD):
                for r in range(tiles):
                    rows = slice(16 * (r % 2), 16 * (r % 2) + 16)
                    piece = part[r // 2, rows, c * HEAD:(c + 1) * HEAD] * factor
                    out[at + r] = piece.astype(BF16)
                at = at + tiles
        for g in range(PADDING):
            out[at + g] = jnp.zeros((16, HEAD), BF16)


def project(factor, rq, rkv, from_prev, from_next, x_mod, parts):
    slab, width = x_mod.shape
    across = sum(p.shape[2] for p in parts)
    tiles = (width + across) // HEAD * (3 * RANK // 16) + PADDING
    block = width // 4
    shape = jax.ShapeDtypeStruct((tiles, 16, HEAD), BF16)
    return pl.pallas_call(
        functools.partial(project_kernel, factor),
        grid=(width // block,),
        in_specs=[
            whole(rq),
            pl.BlockSpec((2 * RANK, slab), lambda i: (0, 1)),
            whole(from_prev),
            whole(from_next),
            pl.BlockSpec((slab, block), lambda i: (0, i)),
        ] + [whole(p) for p in parts],
        out_specs=whole(shape),
        out_shape=shape,
        compiler_params=pltpu.CompilerParams(
            dimension_semantics=("arbitrary",), vmem_limit_bytes=48 << 20
        ),
        name="project",
    )(rq, rkv, from_prev, from_next, x_mod, *parts)


def unpack_kernel(packed, down, up):
    tiles = 3 * RANK // 16
    g = 0
    for out in (down, up):
        for c in range(out.shape[2] // HEAD):
            for r in range(tiles):
                rows = slice(16 * (r % 2), 16 * (r % 2) + 16)
                out[r // 2, rows, c * HEAD:(c + 1) * HEAD] = packed[g].astype(F32)
                g += 1


def unpack(packed, width, across):
    shapes = [jax.ShapeDtypeStruct((3, RANK, n), F32) for n in (width, across)]
    return pl.pallas_call(unpack_kernel, out_shape=shapes, name="unpack")(packed)


def neighbours(before, after, axis):
    count = lax.axis_size(axis)
    up = [(i, (i + 1) % count) for i in range(count)]
    down = [(j, i) for i, j in up]
    return lax.ppermute(before, axis, up), lax.ppermute(after, axis, down)


def reduce_everywhere(x, batch, tiles):
    count = lax.axis_size(tiles)
    parts = x.reshape(count, x.shape[0] // count * 16, HEAD)
    got = lax.all_to_all(parts, tiles, 0, 0, tiled=True)
    mine = jnp.sum(got.astype(F32), axis=0).astype(BF16)
    peers = lax.axis_size(batch)
    one, two, three = [
        lax.ppermute(mine, batch, [(i, i ^ d) for i in range(peers)]).astype(F32) for d in (1, 2, 3)
    ]
    total = ((mine.astype(F32) + one) + (two + three)).astype(BF16)
    spread = jnp.broadcast_to(total[None], (count,) + total.shape)
    return lax.all_to_all(spread, tiles, 0, 0, tiled=True).reshape(x.shape)


def per_device(
    hidden,
    frozen_queries,
    frozen_keys,
    frozen_values,
    reward_output_gradient,
    truncation_step,
    modulation,
    adapter_down_weight,
    adapter_up_weight,
    window,
):
    slab = hidden.shape[1]
    width = hidden.shape[2]
    across = frozen_queries.shape[2]
    bounds = []
    h0 = 0
    for heads in CHUNKS:
        bounds.append((h0, heads))
        h0 += heads

    def frozen_part(keys, values, h0, heads):
        columns = slice(h0 * HEAD, (h0 + heads) * HEAD)
        return jnp.concatenate([keys[:, :, columns], values[:, :, columns]], axis=0)

    x_mod, first_halo, low0_t = prologue(
        hidden, truncation_step, modulation, adapter_down_weight.transpose(0, 2, 1),
        frozen_keys, frozen_values, CHUNKS[0],
    )
    halos = [neighbours(first_halo, first_halo, "tiles")]
    first_halo, keys, values = lax.optimization_barrier((first_halo, frozen_keys, frozen_values))
    parts = [frozen_part(keys, values, *b) for b in bounds[1:]]
    halos += [neighbours(part, part, "tiles") for part in parts]
    low = first_halo[2 * CHUNKS[0]]

    up = adapter_up_weight
    pad = lambda x, before: jnp.pad(x, ((before, 3 * RANK - before), (0, 0)))
    up_wide = jnp.stack([pad(up[0], RANK), pad(up[1], 2 * RANK), pad(up[2], 0)])
    bias = tile_bias(window, lax.axis_index("tiles"), lax.axis_size("tiles"))
    shared = (bias, low, low0_t)
    own = (frozen_queries, frozen_keys, frozen_values, reward_output_gradient)
    carried = None
    grad_up_parts = []
    for i, ((h0, heads), halo) in enumerate(zip(bounds, halos)):
        attended, grad_up, rq, rkv, *sent = attend_chunk(
            h0, heads, i == len(bounds) - 1, shared, halos[0], own, (up_wide, up), halo, carried
        )
        carried = (attended, rq, rkv)
        grad_up_parts.append(grad_up)

    norm_factor = 1.0 / math.sqrt(
        hidden.shape[0] * lax.axis_size("batch") * slab * lax.axis_size("tiles")
    )
    to_prev, to_next = sent
    from_prev, from_next = neighbours(to_next, to_prev, "tiles")
    packed = project(norm_factor, rq, rkv, from_prev, from_next, x_mod, grad_up_parts)
    packed = reduce_everywhere(packed, "batch", "tiles")
    grad_down, grad_up = unpack(packed, width, across)
    return (attended, grad_down.transpose(0, 2, 1), grad_up)


def solution(mesh):
    placed = (
        P("batch", "tiles", None),
        P("batch", "tiles", None),
        P("batch", "tiles", None),
        P("batch", "tiles", None),
        P("batch", "tiles", None),
        P("batch"),
        P(),
        P(),
        P(),
        P("tiles", None),
    )
    return jax.shard_map(
        per_device,
        mesh=mesh,
        in_specs=placed,
        out_specs=(P("batch", "tiles", None), P(), P()),
        check_vma=False,
    )
```

```python
import functools
import math

import jax
import jax.numpy as jnp
from jax import lax
from jax.experimental import pallas as pl
from jax.experimental.pallas import tpu as pltpu
from jax.sharding import PartitionSpec as P

HEAD = 128
TILE = 128
GF = 2
GR = 2
RANK = 32
LOG2E = 1.4426950408889634
ATTEND_FLOPS = 4_600_000_000
CHUNKS = (4, 4, 2, 2)
QBLOCK = 512
PADDING = 8
PER_STEP = 2
F32 = jnp.float32
BF16 = jnp.bfloat16


def tile_bias(window_rows, slab_index, slab_count):
    per_slab = GF * GR
    query_tile = jnp.arange(per_slab, dtype=jnp.int32)
    key_tile = jnp.arange(3 * per_slab, dtype=jnp.int32)
    key_side = key_tile // per_slab
    key_local = key_tile % per_slab
    frame_step = key_local[None, :] // GR - query_tile[:, None] // GR
    row_step = key_local[None, :] % GR - query_tile[:, None] % GR
    offset_code = (key_side[None, :] * 3 + frame_step + 1) * 3 + row_step + 1
    nearby = (jnp.abs(frame_step) <= 1) & (jnp.abs(row_step) <= 1)
    neighbour = slab_index + key_side - 1
    inside = (neighbour >= 0) & (neighbour < slab_count)
    offsets = jnp.arange(27, dtype=jnp.int32)
    listed = jnp.sum(
        jnp.where(offset_code[:, :, None] == offsets[None, None, :], window_rows[:, None, :], 0),
        axis=2,
    )
    tile_mask = nearby & inside[None, :] & (listed > 0)
    return jnp.repeat(jnp.where(tile_mask, 0.0, -1e30).astype(F32), TILE, axis=1)


def dot(a, b):
    return lax.dot_general(a, b, (((1,), (0,)), ((), ())), preferred_element_type=F32)


def dot_t(a, b):
    return lax.dot_general(a, b, (((1,), (1,)), ((), ())), preferred_element_type=F32)


def split_rows(x):
    hi = x.astype(BF16)
    lo = (x - hi.astype(F32)).astype(BF16)
    return hi, lo


def attend_kernel(first, last, slab, *refs):
    (bias, low_own, low0_t, low_prev, low_next, fq, fk, fv, out_grad, up_wide, up) = refs[:11]
    halos = refs[11:15]
    refs = refs[15:]
    if not first:
        rq_in, rkv_in, _ = refs[:3]
        refs = refs[3:]
    attended, grad_up, rq, rkv = refs[:4]
    refs = refs[4:]
    if last:
        to_prev, to_next = refs[:2]
        refs = refs[2:]
    q_s, kl_s, vl_s, xb_s, xd_s, dq_s, cat_s = refs
    scale = 1.0 / math.sqrt(HEAD)

    @pl.when(pl.program_id(0) == 0)
    def _():
        for n in range(PER_STEP):
            vl_s[n, slab:2 * slab, HEAD:] = low_own[...]
            kl_s[n, slab:2 * slab, HEAD:] = low_own[...]
            for i, low in ((0, low_prev), (2, low_next)):
                rows = slice(i * slab, (i + 1) * slab)
                vl_s[n, rows, HEAD:] = low[0]
                kl_s[n, rows, HEAD:] = low[0]
        if first:
            rq[...] = jnp.zeros_like(rq)
            rkv[...] = jnp.zeros_like(rkv)
        else:
            rq[...] = rq_in[...]
            rkv[...] = rkv_in[...]

    def pair(left, right):
        hi, lo = split_rows(left)
        both = dot(jnp.concatenate([hi, lo], axis=0), right)
        return both[:RANK] + both[RANK:]

    def prepare(n):
        cols = slice(n * HEAD, (n + 1) * HEAD)
        kv_up = jnp.concatenate([up_wide[1, :, cols], up_wide[2, :, cols]], axis=1)
        q_s[n] = (fq[0, :, cols].astype(F32) + dot(low_own[...], up_wide[0, :, cols])).astype(BF16)
        at = n if first else (0, slice(None), cols)
        arrived = [halo[at] for halo in halos]
        sides = (arrived[:2], (fk[0, :, cols], fv[0, :, cols]), arrived[2:])
        for i, (k_in, v_in) in enumerate(sides):
            rows = slice(i * slab, (i + 1) * slab)
            low = vl_s[n, rows, HEAD:]
            added = dot(low, kv_up)
            kl_s[n, rows, :HEAD] = (k_in.astype(F32) + added[:, :HEAD]).astype(BF16)
            vl_s[n, rows, :HEAD] = (v_in.astype(F32) + added[:, HEAD:]).astype(BF16)
        hi, lo = split_rows(dot_t(up[1, :, cols], q_s[n]))
        xb_s[n] = jnp.concatenate([hi, lo], axis=0)
        hi, lo = split_rows(dot_t(up[2, :, cols], out_grad[0, :, cols]))
        xd_s[n] = jnp.concatenate([hi, lo], axis=0)

    def products(n, rows):
        cols = slice(n * HEAD, (n + 1) * HEAD)
        scores = dot_t(q_s[n, rows, :], kl_s[n, :, :HEAD])
        prob_grad = dot_t(out_grad[0, rows, cols], vl_s[n, :, :HEAD])
        return scores, prob_grad

    def soften(rows, scores, prob_grad):
        tiles = range(rows.start // TILE, rows.stop // TILE)
        tile_rows = jnp.concatenate(
            [jnp.broadcast_to(bias[t:t + 1, :], (TILE, 3 * slab)) for t in tiles], axis=0
        )
        scores = scores * (scale * LOG2E) + tile_rows
        row_max = jnp.max(scores, axis=1, keepdims=True)
        weights = jnp.exp2(scores - row_max)
        totals = jnp.sum(weights, axis=1, keepdims=True)
        probs = weights * (1.0 / totals)
        centre = jnp.sum(probs * prob_grad, axis=1, keepdims=True)
        score_grad = (probs * (prob_grad - centre) * scale).astype(BF16)
        return probs.astype(BF16), score_grad

    def spread(n, rows, probs_low, score_grad):
        out = dot(probs_low, vl_s[n])
        attended[0, rows, n * HEAD:(n + 1) * HEAD] = out[:, :HEAD].astype(BF16)
        cat_s[n, rows, :HEAD] = out[:, HEAD:]
        out = dot(score_grad, kl_s[n])
        hi, lo = split_rows(out[:, :HEAD])
        dq_s[n, rows, :HEAD] = hi
        dq_s[n, rows, HEAD:] = lo
        cat_s[n, rows, HEAD:] = out[:, HEAD:]
        return dot(xd_s[n, :, rows], probs_low), dot(xb_s[n, :, rows], score_grad)

    def finish(n, d_total, b_total):
        cols = slice(n * HEAD, (n + 1) * HEAD)
        cat_t = cat_s[n].T
        both = dot(low0_t[...], dq_s[n])
        grad_up[0, :, cols] = both[:, :HEAD] + both[:, HEAD:]
        grad_up[1, :, cols] = pair(cat_t[HEAD + 2 * RANK:HEAD + 3 * RANK], q_s[n])
        grad_up[2, :, cols] = pair(cat_t[:RANK], out_grad[0, :, cols])
        up0 = up[0, :, cols]
        return (dot_t(jnp.concatenate([up0, up0], axis=1), dq_s[n]),
                b_total[:RANK] + b_total[RANK:], d_total[:RANK] + d_total[RANK:])

    steps = [(n, slice(r, r + QBLOCK)) for n in range(PER_STEP) for r in range(0, slab, QBLOCK)]
    totals = [[None, None] for _ in range(PER_STEP)]
    for n in range(PER_STEP):
        prepare(n)
    made = {}
    soft = {}
    for i in range(len(steps) + 2):
        if i < len(steps):
            made[i] = products(*steps[i])
        if 0 <= i - 1 < len(steps):
            soft[i - 1] = soften(steps[i - 1][1], *made.pop(i - 1))
        if 0 <= i - 2 < len(steps):
            n, rows = steps[i - 2]
            parts = spread(n, rows, *soft.pop(i - 2))
            totals[n] = [p if t is None else t + p for t, p in zip(totals[n], parts)]
    shares = [finish(n, *totals[n]) for n in range(PER_STEP)]
    rq[...] += sum(s[0] for s in shares)
    rkv[:RANK] += sum(s[1] for s in shares)
    rkv[RANK:] += sum(s[2] for s in shares)

    if last:
        @pl.when(pl.program_id(0) == pl.num_programs(0) - 1)
        def _():
            to_prev[...] = rkv[:, :slab].astype(BF16)
            to_next[...] = rkv[:, 2 * slab:].astype(BF16)


def whole(x):
    return pl.BlockSpec(x.shape, lambda *_: (0,) * len(x.shape))


def attend_chunk(h0, heads, last, shared, lows, own, ups, halo, carried):
    slab = own[0].shape[1]
    across = own[0].shape[2]
    first = carried is None
    steps = heads // PER_STEP
    wide = PER_STEP * HEAD

    own_spec = pl.BlockSpec((1, slab, wide), lambda h: (0, 0, h0 // PER_STEP + h))
    low_spec = pl.BlockSpec((1, slab, HEAD), lambda h: (lows[0].shape[0] - 1, 0, 0))
    if first:
        halo_specs = [
            pl.BlockSpec((PER_STEP, slab, HEAD), lambda h, skip=skip: (skip + h, 0, 0))
            for skip in (0, steps)
        ]
    else:
        halo_specs = [
            pl.BlockSpec((1, slab, wide), lambda h, kind=kind: (kind, 0, h)) for kind in (0, 1)
        ]
    in_specs = [whole(x) for x in shared] + [low_spec] * 2 + [own_spec] * 4 + [
        pl.BlockSpec((3, x.shape[1], wide), lambda h: (0, 0, h0 // PER_STEP + h)) for x in ups
    ] + halo_specs * 2
    operands = [*shared, *lows, *own, *ups, halo[0], halo[0], halo[1], halo[1]]
    aliases = {}
    if not first:
        attended, rq, rkv = carried
        aliases = {len(operands) + 2: 0}
        operands += [rq, rkv, attended]
        in_specs += [whole(rq), whole(rkv), pl.BlockSpec(memory_space=pl.ANY)]
    rq_shape = jax.ShapeDtypeStruct((RANK, slab), F32)
    rkv_shape = jax.ShapeDtypeStruct((2 * RANK, 3 * slab), F32)
    sent_shape = jax.ShapeDtypeStruct((2 * RANK, slab), BF16)
    return pl.pallas_call(
        functools.partial(attend_kernel, first, last, slab),
        grid=(steps,),
        in_specs=in_specs,
        out_specs=[
            own_spec,
            pl.BlockSpec((3, RANK, wide), lambda h: (0, 0, h)),
            whole(rq_shape),
            whole(rkv_shape),
        ] + [whole(sent_shape)] * (2 * last),
        out_shape=[
            jax.ShapeDtypeStruct((1, slab, across), BF16),
            jax.ShapeDtypeStruct((3, RANK, heads * HEAD), F32),
            rq_shape,
            rkv_shape,
        ] + [sent_shape] * (2 * last),
        scratch_shapes=[
            pltpu.VMEM((PER_STEP, slab, HEAD), BF16),
            pltpu.VMEM((PER_STEP, 3 * slab, 2 * HEAD), BF16),
            pltpu.VMEM((PER_STEP, 3 * slab, 2 * HEAD), BF16),
            pltpu.VMEM((PER_STEP, 2 * RANK, slab), BF16),
            pltpu.VMEM((PER_STEP, 2 * RANK, slab), BF16),
            pltpu.VMEM((PER_STEP, slab, 2 * HEAD), BF16),
            pltpu.VMEM((PER_STEP, slab, 2 * HEAD), F32),
        ],
        input_output_aliases=aliases,
        compiler_params=pltpu.CompilerParams(
            dimension_semantics=("arbitrary",), vmem_limit_bytes=48 << 20
        ),
        cost_estimate=pl.CostEstimate(
            flops=heads * ATTEND_FLOPS, transcendentals=heads * 3 * slab * slab,
            bytes_accessed=heads * 10 * slab * HEAD * 2,
        ),
        name=f"attend_{h0}",
    )(*operands)


def prologue_kernel(step, x, shift_scale, down, fk, fv, x_mod, first_halo, low0_t, down_s):
    del step
    width = x.shape[2]
    heads = fk.shape[2] // HEAD

    @pl.when(pl.program_id(0) == 0)
    def _():
        down_s[...] = jnp.concatenate(
            [down[2], down[0], down[1], jnp.zeros((RANK, width), BF16)], axis=0
        )

    x_full = x[0].astype(F32)
    centred = x_full - jnp.sum(x_full, axis=1, keepdims=True) * (1.0 / width)
    variance = jnp.sum(centred * centred, axis=1, keepdims=True) * (1.0 / width)
    normed = centred * lax.rsqrt(variance + 1e-06)
    modulated = (normed * (1.0 + shift_scale[0, 1:2, :]) + shift_scale[0, 0:1, :]).astype(BF16)
    x_mod[...] = modulated
    reduced = dot_t(modulated, down_s[...])
    for n in range(heads):
        first_halo[n] = fk[0, :, n * HEAD:(n + 1) * HEAD]
        first_halo[heads + n] = fv[0, :, n * HEAD:(n + 1) * HEAD]
    first_halo[2 * heads] = reduced.astype(BF16)
    low0_t[...] = reduced.T[RANK:2 * RANK].astype(BF16)


def prologue(hidden, truncation_step, modulation, down, frozen_keys, frozen_values, heads):
    _, slab, width = hidden.shape
    hidden, modulation, down, frozen_keys, frozen_values = [
        pltpu.with_memory_space_constraint(x, pltpu.HBM)
        for x in (hidden, modulation, down, frozen_keys, frozen_values)
    ]
    frozen_spec = pl.BlockSpec((1, TILE, heads * HEAD), lambda i, step: (0, i, 0))
    return pl.pallas_call(
        prologue_kernel,
        grid_spec=pltpu.PrefetchScalarGridSpec(
            num_scalar_prefetch=1,
            grid=(slab // TILE,),
            in_specs=[
                pl.BlockSpec((1, TILE, width), lambda i, step: (0, i, 0)),
                pl.BlockSpec((1, 2, width), lambda i, step: (step[0], 0, 0)),
                whole(down),
                frozen_spec,
                frozen_spec,
            ],
            out_specs=[
                pl.BlockSpec((TILE, width), lambda i, step: (i, 0)),
                pl.BlockSpec((2 * heads + 1, TILE, HEAD), lambda i, step: (0, i, 0)),
                pl.BlockSpec((RANK, TILE), lambda i, step: (0, i)),
            ],
            scratch_shapes=[pltpu.VMEM((4 * RANK, width), BF16)],
        ),
        out_shape=[
            jax.ShapeDtypeStruct((slab, width), BF16),
            jax.ShapeDtypeStruct((2 * heads + 1, slab, HEAD), BF16),
            jax.ShapeDtypeStruct((RANK, slab), BF16),
        ],
        compiler_params=pltpu.CompilerParams(
            dimension_semantics=("arbitrary",), vmem_limit_bytes=48 << 20
        ),
        name="prologue",
    )(truncation_step, hidden, modulation, down, frozen_keys, frozen_values)


def project_kernel(factor, rq, rkv, from_prev, from_next, x_mod, *refs):
    parts, out = refs[:-1], refs[-1]
    rank_kv = rkv[...] + from_prev[...].astype(F32) + from_next[...].astype(F32)
    hi, lo = split_rows(jnp.concatenate([rq[...], rank_kv], axis=0))
    both = dot(jnp.concatenate([hi, lo], axis=0), x_mod[...])
    down = ((both[:3 * RANK] + both[3 * RANK:]) * factor).astype(BF16)
    columns = x_mod.shape[1] // HEAD
    tiles = 3 * RANK // 16
    first = pl.program_id(0) * (columns * tiles)
    for c in range(columns):
        for r in range(tiles):
            out[first + c * tiles + r] = down[16 * r:16 * r + 16, c * HEAD:(c + 1) * HEAD]

    @pl.when(pl.program_id(0) == pl.num_programs(0) - 1)
    def _():
        at = pl.num_programs(0) * (columns * tiles)
        for part in parts:
            for c in range(part.shape[2] // HEAD):
                for r in range(tiles):
                    rows = slice(16 * (r % 2), 16 * (r % 2) + 16)
                    piece = part[r // 2, rows, c * HEAD:(c + 1) * HEAD] * factor
                    out[at + r] = piece.astype(BF16)
                at = at + tiles
        for g in range(PADDING):
            out[at + g] = jnp.zeros((16, HEAD), BF16)


def project(factor, rq, rkv, from_prev, from_next, x_mod, parts):
    slab, width = x_mod.shape
    across = sum(p.shape[2] for p in parts)
    tiles = (width + across) // HEAD * (3 * RANK // 16) + PADDING
    block = width // 4
    shape = jax.ShapeDtypeStruct((tiles, 16, HEAD), BF16)
    return pl.pallas_call(
        functools.partial(project_kernel, factor),
        grid=(width // block,),
        in_specs=[
            whole(rq),
            pl.BlockSpec((2 * RANK, slab), lambda i: (0, 1)),
            whole(from_prev),
            whole(from_next),
            pl.BlockSpec((slab, block), lambda i: (0, i)),
        ] + [whole(p) for p in parts],
        out_specs=whole(shape),
        out_shape=shape,
        compiler_params=pltpu.CompilerParams(
            dimension_semantics=("arbitrary",), vmem_limit_bytes=48 << 20
        ),
        name="project",
    )(rq, rkv, from_prev, from_next, x_mod, *parts)


def unpack_kernel(packed, down, up):
    tiles = 3 * RANK // 16
    first = 2 * pl.program_id(0)
    at = 0
    for out in (down, up):
        for c in range(out.shape[2] // HEAD):
            for half in (0, 1):
                rows = slice(16 * half, 16 * half + 16)
                piece = packed[at + c * tiles + half + first]
                out[0, rows, c * HEAD:(c + 1) * HEAD] = piece.astype(F32)
        at += out.shape[2] // HEAD * tiles


def unpack(packed, width, across):
    return pl.pallas_call(
        unpack_kernel,
        grid=(3,),
        in_specs=[whole(packed)],
        out_specs=[pl.BlockSpec((1, RANK, n), lambda i: (i, 0, 0)) for n in (width, across)],
        out_shape=[jax.ShapeDtypeStruct((3, RANK, n), F32) for n in (width, across)],
        name="unpack",
    )(packed)


def neighbours(before, after, axis):
    count = lax.axis_size(axis)
    up = [(i, (i + 1) % count) for i in range(count)]
    down = [(j, i) for i, j in up]
    return lax.ppermute(before, axis, up), lax.ppermute(after, axis, down)


def reduce_everywhere(x, batch, tiles):
    count = lax.axis_size(tiles)
    parts = x.reshape(count, x.shape[0] // count * 16, HEAD)
    got = lax.all_to_all(parts, tiles, 0, 0, tiled=True)
    mine = jnp.sum(got.astype(F32), axis=0).astype(BF16)
    peers = lax.axis_size(batch)
    one, two, three = [
        lax.ppermute(mine, batch, [(i, i ^ d) for i in range(peers)]).astype(F32) for d in (1, 2, 3)
    ]
    total = ((mine.astype(F32) + one) + (two + three)).astype(BF16)
    spread = jnp.broadcast_to(total[None], (count,) + total.shape)
    return lax.all_to_all(spread, tiles, 0, 0, tiled=True).reshape(x.shape)


def per_device(
    hidden,
    frozen_queries,
    frozen_keys,
    frozen_values,
    reward_output_gradient,
    truncation_step,
    modulation,
    adapter_down_weight,
    adapter_up_weight,
    window,
):
    slab = hidden.shape[1]
    width = hidden.shape[2]
    across = frozen_queries.shape[2]
    bounds = []
    h0 = 0
    for heads in CHUNKS:
        bounds.append((h0, heads))
        h0 += heads

    def frozen_part(keys, values, h0, heads):
        columns = slice(h0 * HEAD, (h0 + heads) * HEAD)
        return jnp.concatenate([keys[:, :, columns], values[:, :, columns]], axis=0)

    x_mod, first_halo, low0_t = prologue(
        hidden, truncation_step, modulation, adapter_down_weight.transpose(0, 2, 1),
        frozen_keys, frozen_values, CHUNKS[0],
    )
    halos = [neighbours(first_halo, first_halo, "tiles")]
    first_halo, keys, values = lax.optimization_barrier((first_halo, frozen_keys, frozen_values))
    parts = [frozen_part(keys, values, *b) for b in bounds[1:]]
    halos += [neighbours(part, part, "tiles") for part in parts]
    low = first_halo[2 * CHUNKS[0]]

    up = adapter_up_weight
    pad = lambda x, before: jnp.pad(x, ((before, 3 * RANK - before), (0, 0)))
    up_wide = jnp.stack([pad(up[0], RANK), pad(up[1], 2 * RANK), pad(up[2], 0)])
    bias = tile_bias(window, lax.axis_index("tiles"), lax.axis_size("tiles"))
    shared = (bias, low, low0_t)
    own = (frozen_queries, frozen_keys, frozen_values, reward_output_gradient)
    carried = None
    grad_up_parts = []
    for i, ((h0, heads), halo) in enumerate(zip(bounds, halos)):
        attended, grad_up, rq, rkv, *sent = attend_chunk(
            h0, heads, i == len(bounds) - 1, shared, halos[0], own, (up_wide, up), halo, carried
        )
        carried = (attended, rq, rkv)
        grad_up_parts.append(grad_up)

    norm_factor = 1.0 / math.sqrt(
        hidden.shape[0] * lax.axis_size("batch") * slab * lax.axis_size("tiles")
    )
    to_prev, to_next = sent
    from_prev, from_next = neighbours(to_next, to_prev, "tiles")
    packed = project(norm_factor, rq, rkv, from_prev, from_next, x_mod, grad_up_parts)
    packed = reduce_everywhere(packed, "batch", "tiles")
    grad_down, grad_up = unpack(packed, width, across)
    return (attended, grad_down.transpose(0, 2, 1), grad_up)


def solution(mesh):
    placed = (
        P("batch", "tiles", None),
        P("batch", "tiles", None),
        P("batch", "tiles", None),
        P("batch", "tiles", None),
        P("batch", "tiles", None),
        P("batch"),
        P(),
        P(),
        P(),
        P("tiles", None),
    )
    return jax.shard_map(
        per_device,
        mesh=mesh,
        in_specs=placed,
        out_specs=(P("batch", "tiles", None), P(), P()),
        check_vma=False,
    )
```

```python
import functools
import math

import jax
import jax.numpy as jnp
from jax import lax
from jax.experimental import pallas as pl
from jax.experimental.pallas import tpu as pltpu
from jax.sharding import PartitionSpec as P

HEAD = 128
TILE = 128
GF = 2
GR = 2
RANK = 32
LOG2E = 1.4426950408889634
ATTEND_FLOPS = 4_600_000_000
CHUNKS = (4, 2, 4, 2)
QBLOCK = 512
PADDING = 8
PER_STEP = 2
F32 = jnp.float32
BF16 = jnp.bfloat16


def tile_bias(window_rows, slab_index, slab_count):
    per_slab = GF * GR
    query_tile = jnp.arange(per_slab, dtype=jnp.int32)
    key_tile = jnp.arange(3 * per_slab, dtype=jnp.int32)
    key_side = key_tile // per_slab
    key_local = key_tile % per_slab
    frame_step = key_local[None, :] // GR - query_tile[:, None] // GR
    row_step = key_local[None, :] % GR - query_tile[:, None] % GR
    offset_code = (key_side[None, :] * 3 + frame_step + 1) * 3 + row_step + 1
    nearby = (jnp.abs(frame_step) <= 1) & (jnp.abs(row_step) <= 1)
    neighbour = slab_index + key_side - 1
    inside = (neighbour >= 0) & (neighbour < slab_count)
    offsets = jnp.arange(27, dtype=jnp.int32)
    listed = jnp.sum(
        jnp.where(offset_code[:, :, None] == offsets[None, None, :], window_rows[:, None, :], 0),
        axis=2,
    )
    tile_mask = nearby & inside[None, :] & (listed > 0)
    return jnp.repeat(jnp.where(tile_mask, 0.0, -1e30).astype(F32), TILE, axis=1)


def dot(a, b):
    return lax.dot_general(a, b, (((1,), (0,)), ((), ())), preferred_element_type=F32)


def dot_t(a, b):
    return lax.dot_general(a, b, (((1,), (1,)), ((), ())), preferred_element_type=F32)


def split_rows(x):
    hi = x.astype(BF16)
    lo = (x - hi.astype(F32)).astype(BF16)
    return hi, lo


def attend_kernel(first, last, slab, *refs):
    (bias, low_own, low0_t, low_prev, low_next, fq, fk, fv, out_grad, up_wide, up) = refs[:11]
    halos = refs[11:15]
    refs = refs[15:]
    if not first:
        rq_in, rkv_in, _ = refs[:3]
        refs = refs[3:]
    attended, grad_up, rq, rkv = refs[:4]
    refs = refs[4:]
    if last:
        to_prev, to_next = refs[:2]
        refs = refs[2:]
    q_s, kl_s, vl_s, xb_s, xd_s, dq_s, cat_s = refs
    scale = 1.0 / math.sqrt(HEAD)

    @pl.when(pl.program_id(0) == 0)
    def _():
        for n in range(PER_STEP):
            vl_s[n, slab:2 * slab, HEAD:] = low_own[...]
            kl_s[n, slab:2 * slab, HEAD:] = low_own[...]
            for i, low in ((0, low_prev), (2, low_next)):
                rows = slice(i * slab, (i + 1) * slab)
                vl_s[n, rows, HEAD:] = low[0]
                kl_s[n, rows, HEAD:] = low[0]
        if first:
            rq[...] = jnp.zeros_like(rq)
            rkv[...] = jnp.zeros_like(rkv)
        else:
            rq[...] = rq_in[...]
            rkv[...] = rkv_in[...]

    def pair(left, right):
        hi, lo = split_rows(left)
        both = dot(jnp.concatenate([hi, lo], axis=0), right)
        return both[:RANK] + both[RANK:]

    def prepare(n):
        cols = slice(n * HEAD, (n + 1) * HEAD)
        kv_up = jnp.concatenate([up_wide[1, :, cols], up_wide[2, :, cols]], axis=1)
        q_s[n] = (fq[0, :, cols].astype(F32) + dot(low_own[...], up_wide[0, :, cols])).astype(BF16)
        at = n if first else (0, slice(None), cols)
        arrived = [halo[at] for halo in halos]
        sides = (arrived[:2], (fk[0, :, cols], fv[0, :, cols]), arrived[2:])
        for i, (k_in, v_in) in enumerate(sides):
            rows = slice(i * slab, (i + 1) * slab)
            low = vl_s[n, rows, HEAD:]
            added = dot(low, kv_up)
            kl_s[n, rows, :HEAD] = (k_in.astype(F32) + added[:, :HEAD]).astype(BF16)
            vl_s[n, rows, :HEAD] = (v_in.astype(F32) + added[:, HEAD:]).astype(BF16)
        hi, lo = split_rows(dot_t(up[1, :, cols], q_s[n]))
        xb_s[n] = jnp.concatenate([hi, lo], axis=0)
        hi, lo = split_rows(dot_t(up[2, :, cols], out_grad[0, :, cols]))
        xd_s[n] = jnp.concatenate([hi, lo], axis=0)

    def products(n, rows):
        cols = slice(n * HEAD, (n + 1) * HEAD)
        scores = dot_t(q_s[n, rows, :], kl_s[n, :, :HEAD])
        prob_grad = dot_t(out_grad[0, rows, cols], vl_s[n, :, :HEAD])
        return scores, prob_grad

    def soften(rows, scores, prob_grad):
        tiles = range(rows.start // TILE, rows.stop // TILE)
        tile_rows = jnp.concatenate(
            [jnp.broadcast_to(bias[t:t + 1, :], (TILE, 3 * slab)) for t in tiles], axis=0
        )
        scores = scores * (scale * LOG2E) + tile_rows
        row_max = jnp.max(scores, axis=1, keepdims=True)
        weights = jnp.exp2(scores - row_max)
        totals = jnp.sum(weights, axis=1, keepdims=True)
        probs = weights * (1.0 / totals)
        centre = jnp.sum(probs * prob_grad, axis=1, keepdims=True)
        score_grad = (probs * (prob_grad - centre) * scale).astype(BF16)
        return probs.astype(BF16), score_grad

    def spread(n, rows, probs_low, score_grad):
        out = dot(probs_low, vl_s[n])
        attended[0, rows, n * HEAD:(n + 1) * HEAD] = out[:, :HEAD].astype(BF16)
        rows_seen = out[:, HEAD:]
        out = dot(score_grad, kl_s[n])
        hi, lo = split_rows(out[:, :HEAD])
        dq_s[n, rows, :HEAD] = hi
        dq_s[n, rows, HEAD:] = lo
        lane = lax.broadcasted_iota(jnp.int32, (QBLOCK, HEAD), 1)
        cat_s[n, rows, :] = jnp.where(lane < RANK, rows_seen, out[:, HEAD:])
        return dot(xd_s[n, :, rows], probs_low), dot(xb_s[n, :, rows], score_grad)

    def finish(n, d_total, b_total):
        cols = slice(n * HEAD, (n + 1) * HEAD)
        cat_t = cat_s[n].T
        both = dot(low0_t[...], dq_s[n])
        grad_up[0, :, cols] = both[:, :HEAD] + both[:, HEAD:]
        grad_up[1, :, cols] = pair(cat_t[2 * RANK:3 * RANK], q_s[n])
        grad_up[2, :, cols] = pair(cat_t[:RANK], out_grad[0, :, cols])
        up0 = up[0, :, cols]
        return (dot_t(jnp.concatenate([up0, up0], axis=1), dq_s[n]),
                b_total[:RANK] + b_total[RANK:], d_total[:RANK] + d_total[RANK:])

    steps = [(n, slice(r, r + QBLOCK)) for n in range(PER_STEP) for r in range(0, slab, QBLOCK)]
    totals = [[None, None] for _ in range(PER_STEP)]
    for n in range(PER_STEP):
        prepare(n)
    made = {}
    soft = {}
    for i in range(len(steps) + 2):
        if i < len(steps):
            made[i] = products(*steps[i])
        if 0 <= i - 1 < len(steps):
            soft[i - 1] = soften(steps[i - 1][1], *made.pop(i - 1))
        if 0 <= i - 2 < len(steps):
            n, rows = steps[i - 2]
            parts = spread(n, rows, *soft.pop(i - 2))
            totals[n] = [p if t is None else t + p for t, p in zip(totals[n], parts)]
    shares = [finish(n, *totals[n]) for n in range(PER_STEP)]
    rq[...] += sum(s[0] for s in shares)
    rkv[:RANK] += sum(s[1] for s in shares)
    rkv[RANK:] += sum(s[2] for s in shares)

    if last:
        @pl.when(pl.program_id(0) == pl.num_programs(0) - 1)
        def _():
            to_prev[...] = rkv[:, :slab].astype(BF16)
            to_next[...] = rkv[:, 2 * slab:].astype(BF16)


def whole(x):
    return pl.BlockSpec(x.shape, lambda *_: (0,) * len(x.shape))


def attend_chunk(h0, heads, last, shared, lows, own, ups, halo, carried):
    slab = own[0].shape[1]
    across = own[0].shape[2]
    first = carried is None
    steps = heads // PER_STEP
    wide = PER_STEP * HEAD

    own_spec = pl.BlockSpec((1, slab, wide), lambda h: (0, 0, h0 // PER_STEP + h))
    low_spec = pl.BlockSpec((1, slab, HEAD), lambda h: (lows[0].shape[0] - 1, 0, 0))
    if first:
        halo_specs = [
            pl.BlockSpec((PER_STEP, slab, HEAD), lambda h, skip=skip: (skip + h, 0, 0))
            for skip in (0, steps)
        ]
    else:
        halo_specs = [
            pl.BlockSpec((1, slab, wide), lambda h, kind=kind: (kind, 0, h)) for kind in (0, 1)
        ]
    in_specs = [whole(x) for x in shared] + [low_spec] * 2 + [own_spec] * 4 + [
        pl.BlockSpec((3, x.shape[1], wide), lambda h: (0, 0, h0 // PER_STEP + h)) for x in ups
    ] + halo_specs * 2
    operands = [*shared, *lows, *own, *ups, halo[0], halo[0], halo[1], halo[1]]
    aliases = {}
    if not first:
        attended, rq, rkv = carried
        aliases = {len(operands) + 2: 0}
        operands += [rq, rkv, attended]
        in_specs += [whole(rq), whole(rkv), pl.BlockSpec(memory_space=pl.ANY)]
    rq_shape = jax.ShapeDtypeStruct((RANK, slab), F32)
    rkv_shape = jax.ShapeDtypeStruct((2 * RANK, 3 * slab), F32)
    sent_shape = jax.ShapeDtypeStruct((2 * RANK, slab), BF16)
    return pl.pallas_call(
        functools.partial(attend_kernel, first, last, slab),
        grid=(steps,),
        in_specs=in_specs,
        out_specs=[
            own_spec,
            pl.BlockSpec((3, RANK, wide), lambda h: (0, 0, h)),
            whole(rq_shape),
            whole(rkv_shape),
        ] + [whole(sent_shape)] * (2 * last),
        out_shape=[
            jax.ShapeDtypeStruct((1, slab, across), BF16),
            jax.ShapeDtypeStruct((3, RANK, heads * HEAD), F32),
            rq_shape,
            rkv_shape,
        ] + [sent_shape] * (2 * last),
        scratch_shapes=[
            pltpu.VMEM((PER_STEP, slab, HEAD), BF16),
            pltpu.VMEM((PER_STEP, 3 * slab, 2 * HEAD), BF16),
            pltpu.VMEM((PER_STEP, 3 * slab, 2 * HEAD), BF16),
            pltpu.VMEM((PER_STEP, 2 * RANK, slab), BF16),
            pltpu.VMEM((PER_STEP, 2 * RANK, slab), BF16),
            pltpu.VMEM((PER_STEP, slab, 2 * HEAD), BF16),
            pltpu.VMEM((PER_STEP, slab, HEAD), F32),
        ],
        input_output_aliases=aliases,
        compiler_params=pltpu.CompilerParams(
            dimension_semantics=("arbitrary",), vmem_limit_bytes=48 << 20
        ),
        cost_estimate=pl.CostEstimate(
            flops=heads * ATTEND_FLOPS, transcendentals=heads * 3 * slab * slab,
            bytes_accessed=heads * 10 * slab * HEAD * 2,
        ),
        name=f"attend_{h0}",
    )(*operands)


def prologue_kernel(step, x, shift_scale, down, fk, fv, x_mod, first_halo, low0_t, down_s):
    del step
    width = x.shape[2]
    heads = fk.shape[2] // HEAD

    @pl.when(pl.program_id(0) == 0)
    def _():
        down_s[...] = jnp.concatenate(
            [down[2], down[0], down[1], jnp.zeros((RANK, width), BF16)], axis=0
        )

    x_full = x[0].astype(F32)
    centred = x_full - jnp.sum(x_full, axis=1, keepdims=True) * (1.0 / width)
    variance = jnp.sum(centred * centred, axis=1, keepdims=True) * (1.0 / width)
    normed = centred * lax.rsqrt(variance + 1e-06)
    modulated = (normed * (1.0 + shift_scale[0, 1:2, :]) + shift_scale[0, 0:1, :]).astype(BF16)
    x_mod[...] = modulated
    reduced = dot_t(modulated, down_s[...])
    for n in range(heads):
        first_halo[n] = fk[0, :, n * HEAD:(n + 1) * HEAD]
        first_halo[heads + n] = fv[0, :, n * HEAD:(n + 1) * HEAD]
    first_halo[2 * heads] = reduced.astype(BF16)
    low0_t[...] = reduced.T[RANK:2 * RANK].astype(BF16)


def prologue(hidden, truncation_step, modulation, down, frozen_keys, frozen_values, heads):
    _, slab, width = hidden.shape
    hidden, modulation, down, frozen_keys, frozen_values = [
        pltpu.with_memory_space_constraint(x, pltpu.HBM)
        for x in (hidden, modulation, down, frozen_keys, frozen_values)
    ]
    frozen_spec = pl.BlockSpec((1, TILE, heads * HEAD), lambda i, step: (0, i, 0))
    return pl.pallas_call(
        prologue_kernel,
        grid_spec=pltpu.PrefetchScalarGridSpec(
            num_scalar_prefetch=1,
            grid=(slab // TILE,),
            in_specs=[
                pl.BlockSpec((1, TILE, width), lambda i, step: (0, i, 0)),
                pl.BlockSpec((1, 2, width), lambda i, step: (step[0], 0, 0)),
                whole(down),
                frozen_spec,
                frozen_spec,
            ],
            out_specs=[
                pl.BlockSpec((TILE, width), lambda i, step: (i, 0)),
                pl.BlockSpec((2 * heads + 1, TILE, HEAD), lambda i, step: (0, i, 0)),
                pl.BlockSpec((RANK, TILE), lambda i, step: (0, i)),
            ],
            scratch_shapes=[pltpu.VMEM((4 * RANK, width), BF16)],
        ),
        out_shape=[
            jax.ShapeDtypeStruct((slab, width), BF16),
            jax.ShapeDtypeStruct((2 * heads + 1, slab, HEAD), BF16),
            jax.ShapeDtypeStruct((RANK, slab), BF16),
        ],
        compiler_params=pltpu.CompilerParams(
            dimension_semantics=("arbitrary",), vmem_limit_bytes=48 << 20
        ),
        name="prologue",
    )(truncation_step, hidden, modulation, down, frozen_keys, frozen_values)


def project_kernel(factor, rq, rkv, from_prev, from_next, x_mod, *refs):
    parts, out = refs[:-1], refs[-1]
    rank_kv = rkv[...] + from_prev[...].astype(F32) + from_next[...].astype(F32)
    hi, lo = split_rows(jnp.concatenate([rq[...], rank_kv], axis=0))
    both = dot(jnp.concatenate([hi, lo], axis=0), x_mod[...])
    down = ((both[:3 * RANK] + both[3 * RANK:]) * factor).astype(BF16)
    columns = x_mod.shape[1] // HEAD
    tiles = 3 * RANK // 16
    first = pl.program_id(0) * (columns * tiles)
    for c in range(columns):
        for r in range(tiles):
            out[first + c * tiles + r] = down[16 * r:16 * r + 16, c * HEAD:(c + 1) * HEAD]

    @pl.when(pl.program_id(0) == pl.num_programs(0) - 1)
    def _():
        at = pl.num_programs(0) * (columns * tiles)
        for part in parts:
            for c in range(part.shape[2] // HEAD):
                for r in range(tiles):
                    rows = slice(16 * (r % 2), 16 * (r % 2) + 16)
                    piece = part[r // 2, rows, c * HEAD:(c + 1) * HEAD] * factor
                    out[at + r] = piece.astype(BF16)
                at = at + tiles
        for g in range(PADDING):
            out[at + g] = jnp.zeros((16, HEAD), BF16)


def project(factor, rq, rkv, from_prev, from_next, x_mod, parts):
    slab, width = x_mod.shape
    across = sum(p.shape[2] for p in parts)
    tiles = (width + across) // HEAD * (3 * RANK // 16) + PADDING
    block = width // 4
    shape = jax.ShapeDtypeStruct((tiles, 16, HEAD), BF16)
    return pl.pallas_call(
        functools.partial(project_kernel, factor),
        grid=(width // block,),
        in_specs=[
            whole(rq),
            pl.BlockSpec((2 * RANK, slab), lambda i: (0, 1)),
            whole(from_prev),
            whole(from_next),
            pl.BlockSpec((slab, block), lambda i: (0, i)),
        ] + [whole(p) for p in parts],
        out_specs=whole(shape),
        out_shape=shape,
        compiler_params=pltpu.CompilerParams(
            dimension_semantics=("arbitrary",), vmem_limit_bytes=48 << 20
        ),
        name="project",
    )(rq, rkv, from_prev, from_next, x_mod, *parts)


def unpack_kernel(packed, down, up):
    tiles = 3 * RANK // 16
    g = 0
    for out in (down, up):
        for c in range(out.shape[2] // HEAD):
            for r in range(tiles):
                rows = slice(16 * (r % 2), 16 * (r % 2) + 16)
                out[r // 2, rows, c * HEAD:(c + 1) * HEAD] = packed[g].astype(F32)
                g += 1


def unpack(packed, width, across):
    shapes = [jax.ShapeDtypeStruct((3, RANK, n), F32) for n in (width, across)]
    return pl.pallas_call(unpack_kernel, out_shape=shapes, name="unpack")(packed)


def neighbours(before, after, axis):
    count = lax.axis_size(axis)
    up = [(i, (i + 1) % count) for i in range(count)]
    down = [(j, i) for i, j in up]
    return lax.ppermute(before, axis, up), lax.ppermute(after, axis, down)


def reduce_everywhere(x, batch, tiles):
    count = lax.axis_size(tiles)
    parts = x.reshape(count, x.shape[0] // count * 16, HEAD)
    got = lax.all_to_all(parts, tiles, 0, 0, tiled=True)
    mine = jnp.sum(got.astype(F32), axis=0).astype(BF16)
    peers = lax.axis_size(batch)
    one, two, three = [
        lax.ppermute(mine, batch, [(i, i ^ d) for i in range(peers)]).astype(F32) for d in (1, 2, 3)
    ]
    total = ((mine.astype(F32) + one) + (two + three)).astype(BF16)
    spread = jnp.broadcast_to(total[None], (count,) + total.shape)
    return lax.all_to_all(spread, tiles, 0, 0, tiled=True).reshape(x.shape)


def per_device(
    hidden,
    frozen_queries,
    frozen_keys,
    frozen_values,
    reward_output_gradient,
    truncation_step,
    modulation,
    adapter_down_weight,
    adapter_up_weight,
    window,
):
    slab = hidden.shape[1]
    width = hidden.shape[2]
    across = frozen_queries.shape[2]
    bounds = []
    h0 = 0
    for heads in CHUNKS:
        bounds.append((h0, heads))
        h0 += heads

    def frozen_part(keys, values, h0, heads):
        columns = slice(h0 * HEAD, (h0 + heads) * HEAD)
        return jnp.concatenate([keys[:, :, columns], values[:, :, columns]], axis=0)

    x_mod, first_halo, low0_t = prologue(
        hidden, truncation_step, modulation, adapter_down_weight.transpose(0, 2, 1),
        frozen_keys, frozen_values, CHUNKS[0],
    )
    halos = [neighbours(first_halo, first_halo, "tiles")]
    first_halo, keys, values = lax.optimization_barrier((first_halo, frozen_keys, frozen_values))
    parts = [frozen_part(keys, values, *b) for b in bounds[1:]]
    halos += [neighbours(part, part, "tiles") for part in parts]
    low = first_halo[2 * CHUNKS[0]]

    up = adapter_up_weight
    pad = lambda x, before: jnp.pad(x, ((before, 3 * RANK - before), (0, 0)))
    up_wide = jnp.stack([pad(up[0], RANK), pad(up[1], 2 * RANK), pad(up[2], 0)])
    bias = tile_bias(window, lax.axis_index("tiles"), lax.axis_size("tiles"))
    shared = (bias, low, low0_t)
    own = (frozen_queries, frozen_keys, frozen_values, reward_output_gradient)
    carried = None
    grad_up_parts = []
    for i, ((h0, heads), halo) in enumerate(zip(bounds, halos)):
        attended, grad_up, rq, rkv, *sent = attend_chunk(
            h0, heads, i == len(bounds) - 1, shared, halos[0], own, (up_wide, up), halo, carried
        )
        carried = (attended, rq, rkv)
        grad_up_parts.append(grad_up)

    norm_factor = 1.0 / math.sqrt(
        hidden.shape[0] * lax.axis_size("batch") * slab * lax.axis_size("tiles")
    )
    to_prev, to_next = sent
    from_prev, from_next = neighbours(to_next, to_prev, "tiles")
    packed = project(norm_factor, rq, rkv, from_prev, from_next, x_mod, grad_up_parts)
    packed = reduce_everywhere(packed, "batch", "tiles")
    grad_down, grad_up = unpack(packed, width, across)
    return (attended, grad_down.transpose(0, 2, 1), grad_up)


def solution(mesh):
    placed = (
        P("batch", "tiles", None),
        P("batch", "tiles", None),
        P("batch", "tiles", None),
        P("batch", "tiles", None),
        P("batch", "tiles", None),
        P("batch"),
        P(),
        P(),
        P(),
        P("tiles", None),
    )
    return jax.shard_map(
        per_device,
        mesh=mesh,
        in_specs=placed,
        out_specs=(P("batch", "tiles", None), P(), P()),
        check_vma=False,
    )
```

```python
import functools
import math

import jax
import jax.numpy as jnp
from jax import lax
from jax.experimental import pallas as pl
from jax.experimental.pallas import tpu as pltpu
from jax.sharding import PartitionSpec as P

HEAD = 128
TILE = 128
GF = 2
GR = 2
RANK = 32
LOG2E = 1.4426950408889634
ATTEND_FLOPS = 4_600_000_000
CHUNKS = (6, 4, 2)
QBLOCK = 512
PADDING = 8
PER_STEP = 2
F32 = jnp.float32
BF16 = jnp.bfloat16


def tile_bias(window_rows, slab_index, slab_count):
    per_slab = GF * GR
    query_tile = jnp.arange(per_slab, dtype=jnp.int32)
    key_tile = jnp.arange(3 * per_slab, dtype=jnp.int32)
    key_side = key_tile // per_slab
    key_local = key_tile % per_slab
    frame_step = key_local[None, :] // GR - query_tile[:, None] // GR
    row_step = key_local[None, :] % GR - query_tile[:, None] % GR
    offset_code = (key_side[None, :] * 3 + frame_step + 1) * 3 + row_step + 1
    nearby = (jnp.abs(frame_step) <= 1) & (jnp.abs(row_step) <= 1)
    neighbour = slab_index + key_side - 1
    inside = (neighbour >= 0) & (neighbour < slab_count)
    offsets = jnp.arange(27, dtype=jnp.int32)
    listed = jnp.sum(
        jnp.where(offset_code[:, :, None] == offsets[None, None, :], window_rows[:, None, :], 0),
        axis=2,
    )
    tile_mask = nearby & inside[None, :] & (listed > 0)
    return jnp.repeat(jnp.where(tile_mask, 0.0, -1e30).astype(F32), TILE, axis=1)


def dot(a, b):
    return lax.dot_general(a, b, (((1,), (0,)), ((), ())), preferred_element_type=F32)


def dot_t(a, b):
    return lax.dot_general(a, b, (((1,), (1,)), ((), ())), preferred_element_type=F32)


def split_rows(x):
    hi = x.astype(BF16)
    lo = (x - hi.astype(F32)).astype(BF16)
    return hi, lo


def attend_kernel(first, last, slab, *refs):
    (bias, low_own, low0_t, low_prev, low_next, fq, fk, fv, out_grad, up_wide, up) = refs[:11]
    halos = refs[11:15]
    refs = refs[15:]
    if not first:
        rq_in, rkv_in, _ = refs[:3]
        refs = refs[3:]
    attended, grad_up, rq, rkv = refs[:4]
    refs = refs[4:]
    if last:
        to_prev, to_next = refs[:2]
        refs = refs[2:]
    q_s, kl_s, vl_s, xb_s, xd_s, dq_s, cat_s = refs
    scale = 1.0 / math.sqrt(HEAD)

    @pl.when(pl.program_id(0) == 0)
    def _():
        for n in range(PER_STEP):
            vl_s[n, slab:2 * slab, HEAD:] = low_own[...]
            kl_s[n, slab:2 * slab, HEAD:] = low_own[...]
            for i, low in ((0, low_prev), (2, low_next)):
                rows = slice(i * slab, (i + 1) * slab)
                vl_s[n, rows, HEAD:] = low[0]
                kl_s[n, rows, HEAD:] = low[0]
        if first:
            rq[...] = jnp.zeros_like(rq)
            rkv[...] = jnp.zeros_like(rkv)
        else:
            rq[...] = rq_in[...]
            rkv[...] = rkv_in[...]

    def pair(left, right):
        hi, lo = split_rows(left)
        both = dot(jnp.concatenate([hi, lo], axis=0), right)
        return both[:RANK] + both[RANK:]

    def prepare(n):
        cols = slice(n * HEAD, (n + 1) * HEAD)
        kv_up = jnp.concatenate([up_wide[1, :, cols], up_wide[2, :, cols]], axis=1)
        q_s[n] = (fq[0, :, cols].astype(F32) + dot(low_own[...], up_wide[0, :, cols])).astype(BF16)
        at = n if first else (0, slice(None), cols)
        arrived = [halo[at] for halo in halos]
        sides = (arrived[:2], (fk[0, :, cols], fv[0, :, cols]), arrived[2:])
        for i, (k_in, v_in) in enumerate(sides):
            rows = slice(i * slab, (i + 1) * slab)
            low = vl_s[n, rows, HEAD:]
            added = dot(low, kv_up)
            kl_s[n, rows, :HEAD] = (k_in.astype(F32) + added[:, :HEAD]).astype(BF16)
            vl_s[n, rows, :HEAD] = (v_in.astype(F32) + added[:, HEAD:]).astype(BF16)
        hi, lo = split_rows(dot_t(up[1, :, cols], q_s[n]))
        xb_s[n] = jnp.concatenate([hi, lo], axis=0)
        hi, lo = split_rows(dot_t(up[2, :, cols], out_grad[0, :, cols]))
        xd_s[n] = jnp.concatenate([hi, lo], axis=0)

    def products(n, rows):
        cols = slice(n * HEAD, (n + 1) * HEAD)
        scores = dot_t(q_s[n, rows, :], kl_s[n, :, :HEAD])
        prob_grad = dot_t(out_grad[0, rows, cols], vl_s[n, :, :HEAD])
        return scores, prob_grad

    def soften(rows, scores, prob_grad):
        tiles = range(rows.start // TILE, rows.stop // TILE)
        tile_rows = jnp.concatenate(
            [jnp.broadcast_to(bias[t:t + 1, :], (TILE, 3 * slab)) for t in tiles], axis=0
        )
        scores = scores * (scale * LOG2E) + tile_rows
        row_max = jnp.max(scores, axis=1, keepdims=True)
        weights = jnp.exp2(scores - row_max)
        totals = jnp.sum(weights, axis=1, keepdims=True)
        probs = weights * (1.0 / totals)
        centre = jnp.sum(probs * prob_grad, axis=1, keepdims=True)
        score_grad = (probs * (prob_grad - centre) * scale).astype(BF16)
        return probs.astype(BF16), score_grad

    def spread(n, rows, probs_low, score_grad):
        out = dot(probs_low, vl_s[n])
        attended[0, rows, n * HEAD:(n + 1) * HEAD] = out[:, :HEAD].astype(BF16)
        rows_seen = out[:, HEAD:]
        out = dot(score_grad, kl_s[n])
        hi, lo = split_rows(out[:, :HEAD])
        dq_s[n, rows, :HEAD] = hi
        dq_s[n, rows, HEAD:] = lo
        lane = lax.broadcasted_iota(jnp.int32, (QBLOCK, HEAD), 1)
        cat_s[n, rows, :] = jnp.where(lane < RANK, rows_seen, out[:, HEAD:])
        return dot(xd_s[n, :, rows], probs_low), dot(xb_s[n, :, rows], score_grad)

    def finish(n, d_total, b_total):
        cols = slice(n * HEAD, (n + 1) * HEAD)
        cat_t = cat_s[n].T
        both = dot(low0_t[...], dq_s[n])
        grad_up[0, :, cols] = both[:, :HEAD] + both[:, HEAD:]
        grad_up[1, :, cols] = pair(cat_t[2 * RANK:3 * RANK], q_s[n])
        grad_up[2, :, cols] = pair(cat_t[:RANK], out_grad[0, :, cols])
        up0 = up[0, :, cols]
        return (dot_t(jnp.concatenate([up0, up0], axis=1), dq_s[n]),
                b_total[:RANK] + b_total[RANK:], d_total[:RANK] + d_total[RANK:])

    steps = [(n, slice(r, r + QBLOCK)) for n in range(PER_STEP) for r in range(0, slab, QBLOCK)]
    totals = [[None, None] for _ in range(PER_STEP)]
    for n in range(PER_STEP):
        prepare(n)
    made = {}
    soft = {}
    for i in range(len(steps) + 2):
        if i < len(steps):
            made[i] = products(*steps[i])
        if 0 <= i - 1 < len(steps):
            soft[i - 1] = soften(steps[i - 1][1], *made.pop(i - 1))
        if 0 <= i - 2 < len(steps):
            n, rows = steps[i - 2]
            parts = spread(n, rows, *soft.pop(i - 2))
            totals[n] = [p if t is None else t + p for t, p in zip(totals[n], parts)]
    shares = [finish(n, *totals[n]) for n in range(PER_STEP)]
    rq[...] += sum(s[0] for s in shares)
    rkv[:RANK] += sum(s[1] for s in shares)
    rkv[RANK:] += sum(s[2] for s in shares)

    if last:
        @pl.when(pl.program_id(0) == pl.num_programs(0) - 1)
        def _():
            to_prev[...] = rkv[:, :slab].astype(BF16)
            to_next[...] = rkv[:, 2 * slab:].astype(BF16)


def whole(x):
    return pl.BlockSpec(x.shape, lambda *_: (0,) * len(x.shape))


def attend_chunk(h0, heads, last, shared, lows, own, ups, halo, carried):
    slab = own[0].shape[1]
    across = own[0].shape[2]
    first = carried is None
    steps = heads // PER_STEP
    wide = PER_STEP * HEAD

    own_spec = pl.BlockSpec((1, slab, wide), lambda h: (0, 0, h0 // PER_STEP + h))
    low_spec = pl.BlockSpec((1, slab, HEAD), lambda h: (lows[0].shape[0] - 1, 0, 0))
    if first:
        halo_specs = [
            pl.BlockSpec((PER_STEP, slab, HEAD), lambda h, skip=skip: (skip + h, 0, 0))
            for skip in (0, steps)
        ]
    else:
        halo_specs = [
            pl.BlockSpec((1, slab, wide), lambda h, kind=kind: (kind, 0, h)) for kind in (0, 1)
        ]
    in_specs = [whole(x) for x in shared] + [low_spec] * 2 + [own_spec] * 4 + [
        pl.BlockSpec((3, x.shape[1], wide), lambda h: (0, 0, h0 // PER_STEP + h)) for x in ups
    ] + halo_specs * 2
    operands = [*shared, *lows, *own, *ups, halo[0], halo[0], halo[1], halo[1]]
    aliases = {}
    if not first:
        attended, rq, rkv = carried
        aliases = {len(operands) + 2: 0}
        operands += [rq, rkv, attended]
        in_specs += [whole(rq), whole(rkv), pl.BlockSpec(memory_space=pl.ANY)]
    rq_shape = jax.ShapeDtypeStruct((RANK, slab), F32)
    rkv_shape = jax.ShapeDtypeStruct((2 * RANK, 3 * slab), F32)
    sent_shape = jax.ShapeDtypeStruct((2 * RANK, slab), BF16)
    return pl.pallas_call(
        functools.partial(attend_kernel, first, last, slab),
        grid=(steps,),
        in_specs=in_specs,
        out_specs=[
            own_spec,
            pl.BlockSpec((3, RANK, wide), lambda h: (0, 0, h)),
            whole(rq_shape),
            whole(rkv_shape),
        ] + [whole(sent_shape)] * (2 * last),
        out_shape=[
            jax.ShapeDtypeStruct((1, slab, across), BF16),
            jax.ShapeDtypeStruct((3, RANK, heads * HEAD), F32),
            rq_shape,
            rkv_shape,
        ] + [sent_shape] * (2 * last),
        scratch_shapes=[
            pltpu.VMEM((PER_STEP, slab, HEAD), BF16),
            pltpu.VMEM((PER_STEP, 3 * slab, 2 * HEAD), BF16),
            pltpu.VMEM((PER_STEP, 3 * slab, 2 * HEAD), BF16),
            pltpu.VMEM((PER_STEP, 2 * RANK, slab), BF16),
            pltpu.VMEM((PER_STEP, 2 * RANK, slab), BF16),
            pltpu.VMEM((PER_STEP, slab, 2 * HEAD), BF16),
            pltpu.VMEM((PER_STEP, slab, HEAD), F32),
        ],
        input_output_aliases=aliases,
        compiler_params=pltpu.CompilerParams(
            dimension_semantics=("arbitrary",), vmem_limit_bytes=48 << 20
        ),
        cost_estimate=pl.CostEstimate(
            flops=heads * ATTEND_FLOPS, transcendentals=heads * 3 * slab * slab,
            bytes_accessed=heads * 10 * slab * HEAD * 2,
        ),
        name=f"attend_{h0}",
    )(*operands)


def prologue_kernel(step, x, shift_scale, down, fk, fv, x_mod, first_halo, low0_t, down_s):
    del step
    width = x.shape[2]
    heads = fk.shape[2] // HEAD

    @pl.when(pl.program_id(0) == 0)
    def _():
        down_s[...] = jnp.concatenate(
            [down[2], down[0], down[1], jnp.zeros((RANK, width), BF16)], axis=0
        )

    x_full = x[0].astype(F32)
    centred = x_full - jnp.sum(x_full, axis=1, keepdims=True) * (1.0 / width)
    variance = jnp.sum(centred * centred, axis=1, keepdims=True) * (1.0 / width)
    normed = centred * lax.rsqrt(variance + 1e-06)
    modulated = (normed * (1.0 + shift_scale[0, 1:2, :]) + shift_scale[0, 0:1, :]).astype(BF16)
    x_mod[...] = modulated
    reduced = dot_t(modulated, down_s[...])
    for n in range(heads):
        first_halo[n] = fk[0, :, n * HEAD:(n + 1) * HEAD]
        first_halo[heads + n] = fv[0, :, n * HEAD:(n + 1) * HEAD]
    first_halo[2 * heads] = reduced.astype(BF16)
    low0_t[...] = reduced.T[RANK:2 * RANK].astype(BF16)


def prologue(hidden, truncation_step, modulation, down, frozen_keys, frozen_values, heads):
    _, slab, width = hidden.shape
    hidden, modulation, down, frozen_keys, frozen_values = [
        pltpu.with_memory_space_constraint(x, pltpu.HBM)
        for x in (hidden, modulation, down, frozen_keys, frozen_values)
    ]
    frozen_spec = pl.BlockSpec((1, TILE, heads * HEAD), lambda i, step: (0, i, 0))
    return pl.pallas_call(
        prologue_kernel,
        grid_spec=pltpu.PrefetchScalarGridSpec(
            num_scalar_prefetch=1,
            grid=(slab // TILE,),
            in_specs=[
                pl.BlockSpec((1, TILE, width), lambda i, step: (0, i, 0)),
                pl.BlockSpec((1, 2, width), lambda i, step: (step[0], 0, 0)),
                whole(down),
                frozen_spec,
                frozen_spec,
            ],
            out_specs=[
                pl.BlockSpec((TILE, width), lambda i, step: (i, 0)),
                pl.BlockSpec((2 * heads + 1, TILE, HEAD), lambda i, step: (0, i, 0)),
                pl.BlockSpec((RANK, TILE), lambda i, step: (0, i)),
            ],
            scratch_shapes=[pltpu.VMEM((4 * RANK, width), BF16)],
        ),
        out_shape=[
            jax.ShapeDtypeStruct((slab, width), BF16),
            jax.ShapeDtypeStruct((2 * heads + 1, slab, HEAD), BF16),
            jax.ShapeDtypeStruct((RANK, slab), BF16),
        ],
        compiler_params=pltpu.CompilerParams(
            dimension_semantics=("arbitrary",), vmem_limit_bytes=48 << 20
        ),
        name="prologue",
    )(truncation_step, hidden, modulation, down, frozen_keys, frozen_values)


def project_kernel(factor, rq, rkv, from_prev, from_next, x_mod, *refs):
    parts, out = refs[:-1], refs[-1]
    rank_kv = rkv[...] + from_prev[...].astype(F32) + from_next[...].astype(F32)
    hi, lo = split_rows(jnp.concatenate([rq[...], rank_kv], axis=0))
    both = dot(jnp.concatenate([hi, lo], axis=0), x_mod[...])
    down = ((both[:3 * RANK] + both[3 * RANK:]) * factor).astype(BF16)
    columns = x_mod.shape[1] // HEAD
    tiles = 3 * RANK // 16
    first = pl.program_id(0) * (columns * tiles)
    for c in range(columns):
        for r in range(tiles):
            out[first + c * tiles + r] = down[16 * r:16 * r + 16, c * HEAD:(c + 1) * HEAD]

    @pl.when(pl.program_id(0) == pl.num_programs(0) - 1)
    def _():
        at = pl.num_programs(0) * (columns * tiles)
        for part in parts:
            for c in range(part.shape[2] // HEAD):
                for r in range(tiles):
                    rows = slice(16 * (r % 2), 16 * (r % 2) + 16)
                    piece = part[r // 2, rows, c * HEAD:(c + 1) * HEAD] * factor
                    out[at + r] = piece.astype(BF16)
                at = at + tiles
        for g in range(PADDING):
            out[at + g] = jnp.zeros((16, HEAD), BF16)


def project(factor, rq, rkv, from_prev, from_next, x_mod, parts):
    slab, width = x_mod.shape
    across = sum(p.shape[2] for p in parts)
    tiles = (width + across) // HEAD * (3 * RANK // 16) + PADDING
    block = width // 4
    shape = jax.ShapeDtypeStruct((tiles, 16, HEAD), BF16)
    return pl.pallas_call(
        functools.partial(project_kernel, factor),
        grid=(width // block,),
        in_specs=[
            whole(rq),
            pl.BlockSpec((2 * RANK, slab), lambda i: (0, 1)),
            whole(from_prev),
            whole(from_next),
            pl.BlockSpec((slab, block), lambda i: (0, i)),
        ] + [whole(p) for p in parts],
        out_specs=whole(shape),
        out_shape=shape,
        compiler_params=pltpu.CompilerParams(
            dimension_semantics=("arbitrary",), vmem_limit_bytes=48 << 20
        ),
        name="project",
    )(rq, rkv, from_prev, from_next, x_mod, *parts)


def unpack_kernel(packed, down, up):
    tiles = 3 * RANK // 16
    g = 0
    for out in (down, up):
        for c in range(out.shape[2] // HEAD):
            for r in range(tiles):
                rows = slice(16 * (r % 2), 16 * (r % 2) + 16)
                out[r // 2, rows, c * HEAD:(c + 1) * HEAD] = packed[g].astype(F32)
                g += 1


def unpack(packed, width, across):
    shapes = [jax.ShapeDtypeStruct((3, RANK, n), F32) for n in (width, across)]
    return pl.pallas_call(unpack_kernel, out_shape=shapes, name="unpack")(packed)


def neighbours(before, after, batch, tiles):
    peers, count = lax.axis_size(batch), lax.axis_size(tiles)
    up = [
        (b * count + i, b * count + i + 1 if i + 1 < count else (b + peers // 2) % peers * count)
        for b in range(peers) for i in range(count)
    ]
    down = [(j, i) for i, j in up]
    return lax.ppermute(before, (batch, tiles), up), lax.ppermute(after, (batch, tiles), down)


def reduce_everywhere(x, batch, tiles):
    count = lax.axis_size(tiles)
    parts = x.reshape(count, x.shape[0] // count * 16, HEAD)
    got = lax.all_to_all(parts, tiles, 0, 0, tiled=True)
    mine = jnp.sum(got.astype(F32), axis=0).astype(BF16)
    peers = lax.axis_size(batch)
    one, two, three = [
        lax.ppermute(mine, batch, [(i, i ^ d) for i in range(peers)]).astype(F32) for d in (1, 2, 3)
    ]
    total = ((mine.astype(F32) + one) + (two + three)).astype(BF16)
    spread = jnp.broadcast_to(total[None], (count,) + total.shape)
    return lax.all_to_all(spread, tiles, 0, 0, tiled=True).reshape(x.shape)


def per_device(
    hidden,
    frozen_queries,
    frozen_keys,
    frozen_values,
    reward_output_gradient,
    truncation_step,
    modulation,
    adapter_down_weight,
    adapter_up_weight,
    window,
):
    slab = hidden.shape[1]
    width = hidden.shape[2]
    across = frozen_queries.shape[2]
    bounds = []
    h0 = 0
    for heads in CHUNKS:
        bounds.append((h0, heads))
        h0 += heads

    def frozen_part(keys, values, h0, heads):
        columns = slice(h0 * HEAD, (h0 + heads) * HEAD)
        return jnp.concatenate([keys[:, :, columns], values[:, :, columns]], axis=0)

    x_mod, first_halo, low0_t = prologue(
        hidden, truncation_step, modulation, adapter_down_weight.transpose(0, 2, 1),
        frozen_keys, frozen_values, CHUNKS[0],
    )
    halos = [neighbours(first_halo, first_halo, "batch", "tiles")]
    first_halo, keys, values = lax.optimization_barrier((first_halo, frozen_keys, frozen_values))
    parts = [frozen_part(keys, values, *b) for b in bounds[1:]]
    halos += [neighbours(part, part, "batch", "tiles") for part in parts]
    low = first_halo[2 * CHUNKS[0]]

    up = adapter_up_weight
    pad = lambda x, before: jnp.pad(x, ((before, 3 * RANK - before), (0, 0)))
    up_wide = jnp.stack([pad(up[0], RANK), pad(up[1], 2 * RANK), pad(up[2], 0)])
    bias = tile_bias(window, lax.axis_index("tiles"), lax.axis_size("tiles"))
    shared = (bias, low, low0_t)
    own = (frozen_queries, frozen_keys, frozen_values, reward_output_gradient)
    carried = None
    grad_up_parts = []
    for i, ((h0, heads), halo) in enumerate(zip(bounds, halos)):
        attended, grad_up, rq, rkv, *sent = attend_chunk(
            h0, heads, i == len(bounds) - 1, shared, halos[0], own, (up_wide, up), halo, carried
        )
        carried = (attended, rq, rkv)
        grad_up_parts.append(grad_up)

    norm_factor = 1.0 / math.sqrt(
        hidden.shape[0] * lax.axis_size("batch") * slab * lax.axis_size("tiles")
    )
    to_prev, to_next = sent
    from_prev, from_next = neighbours(to_next, to_prev, "batch", "tiles")
    packed = project(norm_factor, rq, rkv, from_prev, from_next, x_mod, grad_up_parts)
    packed = reduce_everywhere(packed, "batch", "tiles")
    grad_down, grad_up = unpack(packed, width, across)
    return (attended, grad_down.transpose(0, 2, 1), grad_up)


def solution(mesh):
    placed = (
        P("batch", "tiles", None),
        P("batch", "tiles", None),
        P("batch", "tiles", None),
        P("batch", "tiles", None),
        P("batch", "tiles", None),
        P("batch"),
        P(),
        P(),
        P(),
        P("tiles", None),
    )
    return jax.shard_map(
        per_device,
        mesh=mesh,
        in_specs=placed,
        out_specs=(P("batch", "tiles", None), P(), P()),
        check_vma=False,
    )
```

```python
import functools
import math

import jax
import jax.numpy as jnp
from jax import lax
from jax.experimental import pallas as pl
from jax.experimental.pallas import tpu as pltpu
from jax.sharding import PartitionSpec as P

HEAD = 128
TILE = 128
GF = 2
GR = 2
RANK = 32
LOG2E = 1.4426950408889634
ATTEND_FLOPS = 4_600_000_000
CHUNKS = (6, 4, 2)
QBLOCK = 512
ROWS = 256
PADDING = 8
PER_STEP = 2
F32 = jnp.float32
BF16 = jnp.bfloat16


def tile_bias(window_rows, slab_index, slab_count):
    per_slab = GF * GR
    query_tile = jnp.arange(per_slab, dtype=jnp.int32)
    key_tile = jnp.arange(3 * per_slab, dtype=jnp.int32)
    key_side = key_tile // per_slab
    key_local = key_tile % per_slab
    frame_step = key_local[None, :] // GR - query_tile[:, None] // GR
    row_step = key_local[None, :] % GR - query_tile[:, None] % GR
    offset_code = (key_side[None, :] * 3 + frame_step + 1) * 3 + row_step + 1
    nearby = (jnp.abs(frame_step) <= 1) & (jnp.abs(row_step) <= 1)
    neighbour = slab_index + key_side - 1
    inside = (neighbour >= 0) & (neighbour < slab_count)
    offsets = jnp.arange(27, dtype=jnp.int32)
    listed = jnp.sum(
        jnp.where(offset_code[:, :, None] == offsets[None, None, :], window_rows[:, None, :], 0),
        axis=2,
    )
    tile_mask = nearby & inside[None, :] & (listed > 0)
    return jnp.repeat(jnp.where(tile_mask, 0.0, -1e30).astype(F32), TILE, axis=1)


def dot(a, b):
    return lax.dot_general(a, b, (((1,), (0,)), ((), ())), preferred_element_type=F32)


def dot_t(a, b):
    return lax.dot_general(a, b, (((1,), (1,)), ((), ())), preferred_element_type=F32)


def split_rows(x):
    hi = x.astype(BF16)
    lo = (x - hi.astype(F32)).astype(BF16)
    return hi, lo


def attend_kernel(first, last, slab, *refs):
    (bias, low_own, low0_t, low_prev, low_next, fq, fk, fv, out_grad, up_wide, up) = refs[:11]
    halos = refs[11:15]
    refs = refs[15:]
    if not first:
        rq_in, rkv_in, _ = refs[:3]
        refs = refs[3:]
    attended, grad_up, rq, rkv = refs[:4]
    refs = refs[4:]
    if last:
        to_prev, to_next = refs[:2]
        refs = refs[2:]
    q_s, kl_s, vl_s, xb_s, xd_s, dq_s, cat_s = refs
    scale = 1.0 / math.sqrt(HEAD)

    @pl.when(pl.program_id(0) == 0)
    def _():
        for n in range(PER_STEP):
            vl_s[n, slab:2 * slab, HEAD:] = low_own[...]
            kl_s[n, slab:2 * slab, HEAD:] = low_own[...]
            for i, low in ((0, low_prev), (2, low_next)):
                rows = slice(i * slab, (i + 1) * slab)
                vl_s[n, rows, HEAD:] = low[0]
                kl_s[n, rows, HEAD:] = low[0]
        if first:
            rq[...] = jnp.zeros_like(rq)
            rkv[...] = jnp.zeros_like(rkv)
        else:
            rq[...] = rq_in[...]
            rkv[...] = rkv_in[...]

    def pair(left, right):
        hi, lo = split_rows(left)
        both = dot(jnp.concatenate([hi, lo], axis=0), right)
        return both[:RANK] + both[RANK:]

    def prepare(n):
        cols = slice(n * HEAD, (n + 1) * HEAD)
        kv_up = jnp.concatenate([up_wide[1, :, cols], up_wide[2, :, cols]], axis=1)
        q_s[n] = (fq[0, :, cols].astype(F32) + dot(low_own[...], up_wide[0, :, cols])).astype(BF16)
        at = n if first else (0, slice(None), cols)
        arrived = [halo[at] for halo in halos]
        sides = (arrived[:2], (fk[0, :, cols], fv[0, :, cols]), arrived[2:])
        for i, (k_in, v_in) in enumerate(sides):
            rows = slice(i * slab, (i + 1) * slab)
            low = vl_s[n, rows, HEAD:]
            added = dot(low, kv_up)
            kl_s[n, rows, :HEAD] = (k_in.astype(F32) + added[:, :HEAD]).astype(BF16)
            vl_s[n, rows, :HEAD] = (v_in.astype(F32) + added[:, HEAD:]).astype(BF16)
        hi, lo = split_rows(dot_t(up[1, :, cols], q_s[n]))
        xb_s[n] = jnp.concatenate([hi, lo], axis=0)
        hi, lo = split_rows(dot_t(up[2, :, cols], out_grad[0, :, cols]))
        xd_s[n] = jnp.concatenate([hi, lo], axis=0)

    def products(n, rows):
        cols = slice(n * HEAD, (n + 1) * HEAD)
        scores = dot_t(q_s[n, rows, :], kl_s[n, :, :HEAD])
        prob_grad = dot_t(out_grad[0, rows, cols], vl_s[n, :, :HEAD])
        return scores, prob_grad

    def soften(rows, scores, prob_grad):
        tiles = range(rows.start // TILE, rows.stop // TILE)
        tile_rows = jnp.concatenate(
            [jnp.broadcast_to(bias[t:t + 1, :], (TILE, 3 * slab)) for t in tiles], axis=0
        )
        scores = scores * (scale * LOG2E) + tile_rows
        row_max = jnp.max(scores, axis=1, keepdims=True)
        weights = jnp.exp2(scores - row_max)
        totals = jnp.sum(weights, axis=1, keepdims=True)
        probs = weights * (1.0 / totals)
        centre = jnp.sum(probs * prob_grad, axis=1, keepdims=True)
        score_grad = (probs * (prob_grad - centre) * scale).astype(BF16)
        return probs.astype(BF16), score_grad

    def spread(n, rows, probs_low, score_grad):
        out = dot(probs_low, vl_s[n])
        attended[0, rows, n * HEAD:(n + 1) * HEAD] = out[:, :HEAD].astype(BF16)
        rows_seen = out[:, HEAD:]
        out = dot(score_grad, kl_s[n])
        hi, lo = split_rows(out[:, :HEAD])
        dq_s[n, rows, :HEAD] = hi
        dq_s[n, rows, HEAD:] = lo
        lane = lax.broadcasted_iota(jnp.int32, (QBLOCK, HEAD), 1)
        cat_s[n, rows, :] = jnp.where(lane < RANK, rows_seen, out[:, HEAD:])
        return dot(xd_s[n, :, rows], probs_low), dot(xb_s[n, :, rows], score_grad)

    def finish(n, d_total, b_total):
        cols = slice(n * HEAD, (n + 1) * HEAD)
        cat_t = cat_s[n].T
        both = dot(low0_t[...], dq_s[n])
        grad_up[0, :, cols] = both[:, :HEAD] + both[:, HEAD:]
        grad_up[1, :, cols] = pair(cat_t[2 * RANK:3 * RANK], q_s[n])
        grad_up[2, :, cols] = pair(cat_t[:RANK], out_grad[0, :, cols])
        up0 = up[0, :, cols]
        return (dot_t(jnp.concatenate([up0, up0], axis=1), dq_s[n]),
                b_total[:RANK] + b_total[RANK:], d_total[:RANK] + d_total[RANK:])

    steps = [(n, slice(r, r + QBLOCK)) for n in range(PER_STEP) for r in range(0, slab, QBLOCK)]
    totals = [[None, None] for _ in range(PER_STEP)]
    for n in range(PER_STEP):
        prepare(n)
    made = {}
    soft = {}
    for i in range(len(steps) + 2):
        if i < len(steps):
            made[i] = products(*steps[i])
        if 0 <= i - 1 < len(steps):
            soft[i - 1] = soften(steps[i - 1][1], *made.pop(i - 1))
        if 0 <= i - 2 < len(steps):
            n, rows = steps[i - 2]
            parts = spread(n, rows, *soft.pop(i - 2))
            totals[n] = [p if t is None else t + p for t, p in zip(totals[n], parts)]
    shares = [finish(n, *totals[n]) for n in range(PER_STEP)]
    rq[...] += sum(s[0] for s in shares)
    rkv[:RANK] += sum(s[1] for s in shares)
    rkv[RANK:] += sum(s[2] for s in shares)

    if last:
        @pl.when(pl.program_id(0) == pl.num_programs(0) - 1)
        def _():
            to_prev[...] = rkv[:, :slab].astype(BF16)
            to_next[...] = rkv[:, 2 * slab:].astype(BF16)


def whole(x):
    return pl.BlockSpec(x.shape, lambda *_: (0,) * len(x.shape))


def attend_chunk(h0, heads, last, shared, lows, own, ups, halo, carried):
    slab = own[0].shape[1]
    across = own[0].shape[2]
    first = carried is None
    steps = heads // PER_STEP
    wide = PER_STEP * HEAD

    own_spec = pl.BlockSpec((1, slab, wide), lambda h: (0, 0, h0 // PER_STEP + h))
    low_spec = pl.BlockSpec((1, slab, HEAD), lambda h: (lows[0].shape[0] - 1, 0, 0))
    if first:
        halo_specs = [
            pl.BlockSpec((PER_STEP, slab, HEAD), lambda h, skip=skip: (skip + h, 0, 0))
            for skip in (0, steps)
        ]
    else:
        halo_specs = [
            pl.BlockSpec((1, slab, wide), lambda h, kind=kind: (kind, 0, h)) for kind in (0, 1)
        ]
    in_specs = [whole(x) for x in shared] + [low_spec] * 2 + [own_spec] * 4 + [
        pl.BlockSpec((3, x.shape[1], wide), lambda h: (0, 0, h0 // PER_STEP + h)) for x in ups
    ] + halo_specs * 2
    operands = [*shared, *lows, *own, *ups, halo[0], halo[0], halo[1], halo[1]]
    aliases = {}
    if not first:
        attended, rq, rkv = carried
        aliases = {len(operands) + 2: 0}
        operands += [rq, rkv, attended]
        in_specs += [whole(rq), whole(rkv), pl.BlockSpec(memory_space=pl.ANY)]
    rq_shape = jax.ShapeDtypeStruct((RANK, slab), F32)
    rkv_shape = jax.ShapeDtypeStruct((2 * RANK, 3 * slab), F32)
    sent_shape = jax.ShapeDtypeStruct((2 * RANK, slab), BF16)
    return pl.pallas_call(
        functools.partial(attend_kernel, first, last, slab),
        grid=(steps,),
        in_specs=in_specs,
        out_specs=[
            own_spec,
            pl.BlockSpec((3, RANK, wide), lambda h: (0, 0, h)),
            whole(rq_shape),
            whole(rkv_shape),
        ] + [whole(sent_shape)] * (2 * last),
        out_shape=[
            jax.ShapeDtypeStruct((1, slab, across), BF16),
            jax.ShapeDtypeStruct((3, RANK, heads * HEAD), F32),
            rq_shape,
            rkv_shape,
        ] + [sent_shape] * (2 * last),
        scratch_shapes=[
            pltpu.VMEM((PER_STEP, slab, HEAD), BF16),
            pltpu.VMEM((PER_STEP, 3 * slab, 2 * HEAD), BF16),
            pltpu.VMEM((PER_STEP, 3 * slab, 2 * HEAD), BF16),
            pltpu.VMEM((PER_STEP, 2 * RANK, slab), BF16),
            pltpu.VMEM((PER_STEP, 2 * RANK, slab), BF16),
            pltpu.VMEM((PER_STEP, slab, 2 * HEAD), BF16),
            pltpu.VMEM((PER_STEP, slab, HEAD), F32),
        ],
        input_output_aliases=aliases,
        compiler_params=pltpu.CompilerParams(
            dimension_semantics=("arbitrary",), vmem_limit_bytes=48 << 20
        ),
        cost_estimate=pl.CostEstimate(
            flops=heads * ATTEND_FLOPS, transcendentals=heads * 3 * slab * slab,
            bytes_accessed=heads * 10 * slab * HEAD * 2,
        ),
        name=f"attend_{h0}",
    )(*operands)


def prologue_kernel(step, x, shift_scale, down, fk, fv, x_mod, first_halo, low0_t, down_s):
    del step
    width = x.shape[2]
    heads = fk.shape[2] // HEAD

    @pl.when(pl.program_id(0) == 0)
    def _():
        down_s[...] = jnp.concatenate(
            [down[2], down[0], down[1], jnp.zeros((RANK, width), BF16)], axis=0
        )

    x_full = x[0].astype(F32)
    centred = x_full - jnp.sum(x_full, axis=1, keepdims=True) * (1.0 / width)
    variance = jnp.sum(centred * centred, axis=1, keepdims=True) * (1.0 / width)
    normed = centred * lax.rsqrt(variance + 1e-06)
    modulated = (normed * (1.0 + shift_scale[0, 1:2, :]) + shift_scale[0, 0:1, :]).astype(BF16)
    x_mod[...] = modulated
    reduced = dot_t(modulated, down_s[...])
    for n in range(heads):
        first_halo[n] = fk[0, :, n * HEAD:(n + 1) * HEAD]
        first_halo[heads + n] = fv[0, :, n * HEAD:(n + 1) * HEAD]
    first_halo[2 * heads] = reduced.astype(BF16)
    low0_t[...] = reduced.T[RANK:2 * RANK].astype(BF16)


def prologue(hidden, truncation_step, modulation, down, frozen_keys, frozen_values, heads):
    _, slab, width = hidden.shape
    hidden, modulation, down, frozen_keys, frozen_values = [
        pltpu.with_memory_space_constraint(x, pltpu.HBM)
        for x in (hidden, modulation, down, frozen_keys, frozen_values)
    ]
    frozen_spec = pl.BlockSpec((1, ROWS, heads * HEAD), lambda i, step: (0, i, 0))
    return pl.pallas_call(
        prologue_kernel,
        grid_spec=pltpu.PrefetchScalarGridSpec(
            num_scalar_prefetch=1,
            grid=(slab // ROWS,),
            in_specs=[
                pl.BlockSpec((1, ROWS, width), lambda i, step: (0, i, 0)),
                pl.BlockSpec((1, 2, width), lambda i, step: (step[0], 0, 0)),
                whole(down),
                frozen_spec,
                frozen_spec,
            ],
            out_specs=[
                pl.BlockSpec((ROWS, width), lambda i, step: (i, 0)),
                pl.BlockSpec((2 * heads + 1, ROWS, HEAD), lambda i, step: (0, i, 0)),
                pl.BlockSpec((RANK, ROWS), lambda i, step: (0, i)),
            ],
            scratch_shapes=[pltpu.VMEM((4 * RANK, width), BF16)],
        ),
        out_shape=[
            jax.ShapeDtypeStruct((slab, width), BF16),
            jax.ShapeDtypeStruct((2 * heads + 1, slab, HEAD), BF16),
            jax.ShapeDtypeStruct((RANK, slab), BF16),
        ],
        compiler_params=pltpu.CompilerParams(
            dimension_semantics=("arbitrary",), vmem_limit_bytes=48 << 20
        ),
        name="prologue",
    )(truncation_step, hidden, modulation, down, frozen_keys, frozen_values)


def project_kernel(factor, rq, rkv, from_prev, from_next, x_mod, *refs):
    parts, out = refs[:-1], refs[-1]
    rank_kv = rkv[...] + from_prev[...].astype(F32) + from_next[...].astype(F32)
    hi, lo = split_rows(jnp.concatenate([rq[...], rank_kv], axis=0))
    both = dot(jnp.concatenate([hi, lo], axis=0), x_mod[...])
    down = ((both[:3 * RANK] + both[3 * RANK:]) * factor).astype(BF16)
    columns = x_mod.shape[1] // HEAD
    tiles = 3 * RANK // 16
    first = pl.program_id(0) * (columns * tiles)
    for c in range(columns):
        for r in range(tiles):
            out[first + c * tiles + r] = down[16 * r:16 * r + 16, c * HEAD:(c + 1) * HEAD]

    @pl.when(pl.program_id(0) == pl.num_programs(0) - 1)
    def _():
        at = pl.num_programs(0) * (columns * tiles)
        for part in parts:
            for c in range(part.shape[2] // HEAD):
                for r in range(tiles):
                    rows = slice(16 * (r % 2), 16 * (r % 2) + 16)
                    piece = part[r // 2, rows, c * HEAD:(c + 1) * HEAD] * factor
                    out[at + r] = piece.astype(BF16)
                at = at + tiles
        for g in range(PADDING):
            out[at + g] = jnp.zeros((16, HEAD), BF16)


def project(factor, rq, rkv, from_prev, from_next, x_mod, parts):
    slab, width = x_mod.shape
    across = sum(p.shape[2] for p in parts)
    tiles = (width + across) // HEAD * (3 * RANK // 16) + PADDING
    block = width // 4
    shape = jax.ShapeDtypeStruct((tiles, 16, HEAD), BF16)
    return pl.pallas_call(
        functools.partial(project_kernel, factor),
        grid=(width // block,),
        in_specs=[
            whole(rq),
            pl.BlockSpec((2 * RANK, slab), lambda i: (0, 1)),
            whole(from_prev),
            whole(from_next),
            pl.BlockSpec((slab, block), lambda i: (0, i)),
        ] + [whole(p) for p in parts],
        out_specs=whole(shape),
        out_shape=shape,
        compiler_params=pltpu.CompilerParams(
            dimension_semantics=("arbitrary",), vmem_limit_bytes=48 << 20
        ),
        name="project",
    )(rq, rkv, from_prev, from_next, x_mod, *parts)


def unpack_kernel(packed, down, up):
    tiles = 3 * RANK // 16
    g = 0
    for out in (down, up):
        for c in range(out.shape[2] // HEAD):
            for r in range(tiles):
                rows = slice(16 * (r % 2), 16 * (r % 2) + 16)
                out[r // 2, rows, c * HEAD:(c + 1) * HEAD] = packed[g].astype(F32)
                g += 1


def unpack(packed, width, across):
    shapes = [jax.ShapeDtypeStruct((3, RANK, n), F32) for n in (width, across)]
    return pl.pallas_call(unpack_kernel, out_shape=shapes, name="unpack")(packed)


def neighbours(before, after, batch, tiles):
    peers, count = lax.axis_size(batch), lax.axis_size(tiles)
    up = [
        (b * count + i, b * count + i + 1 if i + 1 < count else (b + peers // 2) % peers * count)
        for b in range(peers) for i in range(count)
    ]
    down = [(j, i) for i, j in up]
    return lax.ppermute(before, (batch, tiles), up), lax.ppermute(after, (batch, tiles), down)


def reduce_everywhere(x, batch, tiles):
    count = lax.axis_size(tiles)
    parts = x.reshape(count, x.shape[0] // count * 16, HEAD)
    got = lax.all_to_all(parts, tiles, 0, 0, tiled=True)
    mine = jnp.sum(got.astype(F32), axis=0).astype(BF16)
    peers = lax.axis_size(batch)
    one, two, three = [
        lax.ppermute(mine, batch, [(i, i ^ d) for i in range(peers)]).astype(F32) for d in (1, 2, 3)
    ]
    total = ((mine.astype(F32) + one) + (two + three)).astype(BF16)
    spread = jnp.broadcast_to(total[None], (count,) + total.shape)
    return lax.all_to_all(spread, tiles, 0, 0, tiled=True).reshape(x.shape)


def per_device(
    hidden,
    frozen_queries,
    frozen_keys,
    frozen_values,
    reward_output_gradient,
    truncation_step,
    modulation,
    adapter_down_weight,
    adapter_up_weight,
    window,
):
    slab = hidden.shape[1]
    width = hidden.shape[2]
    across = frozen_queries.shape[2]
    bounds = []
    h0 = 0
    for heads in CHUNKS:
        bounds.append((h0, heads))
        h0 += heads

    def frozen_part(keys, values, h0, heads):
        columns = slice(h0 * HEAD, (h0 + heads) * HEAD)
        return jnp.concatenate([keys[:, :, columns], values[:, :, columns]], axis=0)

    x_mod, first_halo, low0_t = prologue(
        hidden, truncation_step, modulation, adapter_down_weight.transpose(0, 2, 1),
        frozen_keys, frozen_values, CHUNKS[0],
    )
    halos = [neighbours(first_halo, first_halo, "batch", "tiles")]
    first_halo, keys, values = lax.optimization_barrier((first_halo, frozen_keys, frozen_values))
    parts = [frozen_part(keys, values, *b) for b in bounds[1:]]
    halos += [neighbours(part, part, "batch", "tiles") for part in parts]
    low = first_halo[2 * CHUNKS[0]]

    up = adapter_up_weight
    pad = lambda x, before: jnp.pad(x, ((before, 3 * RANK - before), (0, 0)))
    up_wide = jnp.stack([pad(up[0], RANK), pad(up[1], 2 * RANK), pad(up[2], 0)])
    bias = tile_bias(window, lax.axis_index("tiles"), lax.axis_size("tiles"))
    shared = (bias, low, low0_t)
    own = (frozen_queries, frozen_keys, frozen_values, reward_output_gradient)
    carried = None
    grad_up_parts = []
    for i, ((h0, heads), halo) in enumerate(zip(bounds, halos)):
        attended, grad_up, rq, rkv, *sent = attend_chunk(
            h0, heads, i == len(bounds) - 1, shared, halos[0], own, (up_wide, up), halo, carried
        )
        carried = (attended, rq, rkv)
        grad_up_parts.append(grad_up)

    norm_factor = 1.0 / math.sqrt(
        hidden.shape[0] * lax.axis_size("batch") * slab * lax.axis_size("tiles")
    )
    to_prev, to_next = sent
    from_prev, from_next = neighbours(to_next, to_prev, "batch", "tiles")
    packed = project(norm_factor, rq, rkv, from_prev, from_next, x_mod, grad_up_parts)
    packed = reduce_everywhere(packed, "batch", "tiles")
    grad_down, grad_up = unpack(packed, width, across)
    return (attended, grad_down.transpose(0, 2, 1), grad_up)


def solution(mesh):
    placed = (
        P("batch", "tiles", None),
        P("batch", "tiles", None),
        P("batch", "tiles", None),
        P("batch", "tiles", None),
        P("batch", "tiles", None),
        P("batch"),
        P(),
        P(),
        P(),
        P("tiles", None),
    )
    return jax.shard_map(
        per_device,
        mesh=mesh,
        in_specs=placed,
        out_specs=(P("batch", "tiles", None), P(), P()),
        check_vma=False,
    )
```
